32 devices in a mesh: tm: 8 (over z, x), clip: 4 (over y, core).
Axes of the slice: x: 2, y: 2, z: 4, core: 2. Of those that a mesh axis runs over, the one named last changes fastest.
Arguments:
- video: float32 [4, 8, 16, 32, 320], P('clip', 'tm'), may hold values from -6 to 6
- spatial_w: bfloat16 [9, 320, 320], P(None, 'clip'), may hold values from -0.109375 to 0.109375
- spatial_b: float32 [320], replicated, may hold values from -3 to 3
- temporal_w: float32 [3, 320, 320], P(None, 'clip'), may hold values from -0.1875 to 0.1875
- cotangent: float32 [4, 8, 16, 32, 320], P('clip', 'tm'), may hold values from -6 to 6
Outputs:
- output: float32 [4, 8, 16, 32, 320], P('clip', 'tm')
- grad_video: float32 [4, 8, 16, 32, 320], P('clip', 'tm')
- grad_temporal: float32 [3, 320, 320], P(None, 'clip')
The draws below stay inside these ranges and needn't reach their ends.
All inputs are finite; a program needn't handle non-finite values.
Results may differ from the reference program's by a relative error of at most 0.0049.
Values may be sent and summed in bfloat16 or wider, within the bound.
A program may use at most 64 MiB of HBM per device.

```python
import math
import jax
import jax.numpy as jnp
from jax import lax

C = 320
HEIGHT = 16
WIDTH = 32
FRAMES = 8
CLIPS = 4
ROWS_ALL = 16384


def steps_of(rng, extent, split, low, high):
    gain, own = 1.0, jax.random.fold_in(rng, 6)
    for axis_at, blocks in split:
        draws = jnp.exp(jax.random.uniform(jax.random.fold_in(own, axis_at), (blocks,), jnp.float32, low / len(split), high / len(split)))
        gain = gain * jnp.repeat(draws, extent[axis_at] // blocks).reshape([-1 if axis == axis_at else 1 for axis in range(len(extent))])
    return gain


def bell_draw(key, extent, deviation, bound, shards=(), kind=jnp.bfloat16):
    values = deviation * jax.random.normal(key, extent, jnp.float32)
    if shards:
        values = values * steps_of(key, extent, shards, -0.22, 0.18)
    return jnp.clip(values, -bound, bound).astype(kind)


def setup_inputs(seed: int = 0) -> dict:
    splits = jax.random.split(jax.random.key(seed), 6)
    video = bell_draw(splits[0], (CLIPS, FRAMES, HEIGHT, WIDTH, C), 1.0, 6.0, ((0, 4), (1, 8)), jnp.float32)
    spatial_w = bell_draw(splits[1], (9, C, C), (9 * C) ** -0.5, 0.109375, ((1, 4),))
    spatial_b = bell_draw(splits[2], (C,), 0.5, 3.0, (), jnp.float32)
    temporal_w = bell_draw(splits[3], (3, C, C), (3 * C) ** -0.5, 0.1875, ((1, 4),), jnp.float32)
    cotangent = bell_draw(splits[4], (CLIPS, FRAMES, HEIGHT, WIDTH, C), 1.0, 6.0, ((0, 4), (1, 8)), jnp.float32)
    return {"video": video, "spatial_w": spatial_w, "spatial_b": spatial_b, "temporal_w": temporal_w, "cotangent": cotangent}


def outer_dot(left, right):
    return lax.dot_general(left, right, (((0,), (0,)), ((), ())), preferred_element_type=jnp.float32)

def transpose_dot(left, right):
    return lax.dot_general(left, right, (((1,), (1,)), ((), ())), preferred_element_type=jnp.float32)

def one_clip(video, cotangent, spatial_w, spatial_b, temporal_b):
    frames, height, width, chans = video.shape
    row_count = frames * height * width
    video_b = video.astype(jnp.bfloat16)
    padded = jnp.pad(video_b, ((0, 0), (1, 1), (1, 1), (0, 0)))
    spatial = jnp.zeros((row_count, chans), jnp.float32)
    for shift_y in range(3):
        for shift_x in range(3):
            columns = padded[:, shift_y:shift_y + height, shift_x:shift_x + width, :].reshape(row_count, chans)
            spatial = spatial + jnp.dot(columns, spatial_w[3 * shift_y + shift_x], preferred_element_type=jnp.float32)
    spatial = spatial + spatial_b
    sigmoid_s = jax.nn.sigmoid(spatial)
    hidden = (spatial * sigmoid_s).astype(jnp.bfloat16).reshape(frames, height, width, chans)
    hidden_pad = jnp.pad(hidden, ((1, 1), (0, 0), (0, 0), (0, 0)))
    temporal = jnp.zeros((row_count, chans), jnp.float32)
    for kernel_tap in range(3):
        shifted = hidden_pad[kernel_tap:kernel_tap + frames].reshape(row_count, chans)
        temporal = temporal + jnp.dot(shifted, temporal_b[kernel_tap], preferred_element_type=jnp.float32)
    output = video + temporal.reshape(video.shape)
    cot_b = cotangent.astype(jnp.bfloat16)
    cot_flat = cot_b.reshape(row_count, chans)
    cot_pad = jnp.pad(cot_b, ((1, 1), (0, 0), (0, 0), (0, 0)))
    grad_hidden = jnp.zeros((row_count, chans), jnp.float32)
    grads = []
    for kernel_tap in range(3):
        shifted_cot = cot_pad[2 - kernel_tap:2 - kernel_tap + frames].reshape(row_count, chans)
        grad_hidden = grad_hidden + transpose_dot(shifted_cot, temporal_b[kernel_tap])
        shifted_hid = hidden_pad[kernel_tap:kernel_tap + frames].reshape(row_count, chans)
        grads.append(outer_dot(shifted_hid, cot_flat))
    grad_spatial = (grad_hidden * sigmoid_s * (1.0 + spatial * (1.0 - sigmoid_s))).astype(jnp.bfloat16)
    grad_pad = jnp.zeros((frames, height + 2, width + 2, chans), jnp.float32)
    for shift_y in range(3):
        for shift_x in range(3):
            contrib = transpose_dot(grad_spatial, spatial_w[3 * shift_y + shift_x]).reshape(frames, height, width, chans)
            grad_pad = grad_pad.at[:, shift_y:shift_y + height, shift_x:shift_x + width, :].add(contrib)
    grad_video = cotangent + grad_pad[:, 1:-1, 1:-1, :]
    return (output, grad_video, jnp.stack(grads))

def reference(video, spatial_w, spatial_b, temporal_w, cotangent):
    temporal_b = temporal_w.astype(jnp.bfloat16)

    def per_clip(pair):
        return one_clip(pair[0], pair[1], spatial_w, spatial_b, temporal_b)
    output, grad_video, grads = lax.map(per_clip, (video, cotangent))
    grad_temporal = lax.optimization_barrier(jnp.sum(grads, axis=0)) * (1.0 / math.sqrt(ROWS_ALL))
    return (output, grad_video, grad_temporal)
```

```python
import functools
import math

import jax
import jax.numpy as jnp
from jax import lax
from jax.experimental import pallas as pl
from jax.experimental.pallas import tpu as pltpu
from jax.sharding import PartitionSpec as P

F32 = jnp.float32
BF16 = jnp.bfloat16
MESH = pl.DeviceIdType.MESH


def nn_dot(left, right):
    return lax.dot_general(left, right, (((1,), (0,)), ((), ())), preferred_element_type=F32)


def outer_dot(left, right):
    return lax.dot_general(left, right, (((0,), (0,)), ((), ())), preferred_element_type=F32)


def transpose_dot(left, right):
    return lax.dot_general(left, right, (((1,), (1,)), ((), ())), preferred_element_type=F32)


def block_kernel(
    dims,
    video_h, sw_h, bias_h, tw_h, cot_h,
    out_v, gv_v, gt_v,
    video, cot, sw, tw, wp, wg, xcat, cb, chalo, hb, hpack, hhalo, slope, gpad,
    bias_ref, gtl, rx, ysend, ry, psum, pb, rs, ag,
    load_sem, w_send, w_recv, halo_send, halo_recv, g_send, g_recv, a_send, a_recv,
):
    n_tm, n_clip, height, width, chans, scale = dims
    rows = height * width
    depth = sw_h.shape[1]
    half = rows // 2
    quarter = rows // 4
    chunks = 4
    chunk = half // chunks
    tm = lax.axis_index("tm")
    c = lax.axis_index("clip")

    def flip(value, bit):
        return value + bit - 2 * bit * (lax.rem(value // bit, 2))

    core, ypart = flip(c, 1), flip(c, 2)
    xpart, zpart = flip(tm, 1), flip(tm, 2)
    parity = lax.rem(tm, 2)
    h = lax.rem(tm // 2, 2)

    barrier = pltpu.get_barrier_semaphore()
    for step in range(1, n_tm):
        pl.semaphore_signal(
            barrier, inc=1, device_id=(lax.rem(tm + step, n_tm), c), device_id_type=MESH
        )
    pl.semaphore_signal(barrier, inc=1, device_id=(tm, core), device_id_type=MESH)
    pl.semaphore_signal(barrier, inc=1, device_id=(tm, ypart), device_id_type=MESH)

    loads = [
        pltpu.make_async_copy(sw_h, sw, load_sem.at[0]),
        pltpu.make_async_copy(tw_h, tw, load_sem.at[1]),
        pltpu.make_async_copy(cot_h, cot, load_sem.at[2]),
        pltpu.make_async_copy(video_h, video, load_sem.at[3]),
        pltpu.make_async_copy(bias_h, bias_ref, load_sem.at[4]),
    ]
    for load in loads:
        load.start()

    def pack(value):
        return jnp.concatenate([value[:quarter], value[quarter:]], axis=1)

    def unpack(ref, slot):
        parts = []
        for q in range(2):
            both = ref[slot, q * quarter : (q + 1) * quarter]
            parts += [both[:, :chans], both[:, chans:]]
        return jnp.concatenate(parts, axis=0)

    loads[0].wait()
    loads[1].wait()
    shard = [sw[tap] for tap in range(9)] + [tw[tap].astype(BF16) for tap in range(3)]
    for pair in range(6):
        wp[c, pair] = jnp.concatenate([shard[2 * pair], shard[2 * pair + 1]], axis=1)
    pl.semaphore_wait(barrier, n_tm + 1)

    def send(src, dst, ssem, rsem, device):
        copy = pltpu.make_async_remote_copy(
            src_ref=src, dst_ref=dst, send_sem=ssem, recv_sem=rsem,
            device_id=device, device_id_type=MESH,
        )
        copy.start()
        return copy

    def wsend(slot, owner, pair, device):
        part = wp.at[owner, pair]
        return send(part, part, w_send.at[slot], w_recv.at[slot], device)

    y_pairs = [parity, 2 + h, 4, 5]
    shared_pairs = [1 - parity, 3 - h]
    sharers = [(xpart, c), (zpart, c)]
    y_copies = [wsend(j, c, y_pairs[j], (tm, ypart)) for j in range(4)]
    own_copy = send(wp.at[c], wp.at[c], w_send.at[6], w_recv.at[6], (tm, core))

    loads[2].wait()
    own_cot = cot[...].astype(BF16)
    for q in range(2):
        cb[q * quarter : (q + 1) * quarter] = pack(own_cot[q * half : (q + 1) * half])

    def near_send(base, own, halo, q):
        part = pl.ds(q * chunk, chunk)
        return send(
            own.at[part, :], halo.at[parity, part, :],
            halo_send.at[base + q], halo_recv.at[base + q], (xpart, c),
        )

    def far_copy(base, halo, q):
        target = lax.rem(tm + n_tm + 2 - 4 * parity, n_tm)
        part = pl.ds(q * chunk, chunk)
        return pltpu.make_async_remote_copy(
            src_ref=halo.at[1 - parity, part, :],
            dst_ref=halo.at[parity, part, :],
            send_sem=halo_send.at[base + chunks + q],
            recv_sem=halo_recv.at[base + chunks + q],
            device_id=(target, c),
            device_id_type=MESH,
        )

    sends_far = jnp.logical_or(
        jnp.logical_and(parity == 0, tm + 2 < n_tm), jnp.logical_and(parity == 1, tm >= 2)
    )
    gets_far = jnp.logical_or(
        jnp.logical_and(parity == 0, tm >= 2), jnp.logical_and(parity == 1, tm + 2 < n_tm)
    )

    def far_start(base, halo, q):
        @pl.when(sends_far)
        def _():
            far_copy(base, halo, q).start()

    def far_recv(base, halo):
        @pl.when(gets_far)
        def _():
            for q in range(chunks):
                far_copy(base, halo, q).wait_recv()

    def far_done(base, halo):
        @pl.when(sends_far)
        def _():
            for q in range(chunks):
                far_copy(base, halo, q).wait_send()

    cot_near = [near_send(0, cb, chalo, q) for q in range(2)]

    for edge, slot in ((0, 0), (n_tm - 1, 1)):
        @pl.when(tm == edge)
        def _():
            chalo[slot] = jnp.zeros((half, 2 * chans), BF16)
            hhalo[slot] = jnp.zeros((half, 2 * chans), BF16)

    column = lax.rem(lax.broadcasted_iota(jnp.int32, (rows, chans), 0), width)

    def shifted(value, step):
        if step == 0:
            return value
        rolled = pltpu.roll(value, step % rows, 0)
        return jnp.where(column == (0 if step == 1 else width - 1), 0.0, rolled)

    xcat[0:width] = jnp.zeros((width, 3 * chans), BF16)
    xcat[width + rows :] = jnp.zeros((width, 3 * chans), BF16)
    for b in range(3):
        gpad[b, 0:width] = jnp.zeros((width, chans), BF16)
        gpad[b, width + rows :] = jnp.zeros((width, chans), BF16)
    loads[3].wait()
    loads[4].wait()
    frame = video[...]
    xcat[width : width + rows] = jnp.concatenate(
        [shifted(frame, 1).astype(BF16), frame.astype(BF16), shifted(frame, -1).astype(BF16)], axis=1
    )

    relays = []
    z_copies = []
    for j in range(2):
        y_copies[j].wait_recv()
        z_copies.append(wsend(4 + j, ypart, y_pairs[j], sharers[j]))
        if j == 0:
            cot_near += [near_send(0, cb, chalo, q) for q in range(2, chunks)]
        relays.append(wsend(7 + j, ypart, y_pairs[j], (tm, core)))
        cot_near[j].wait_recv()
        far_start(0, chalo, j)
    y_copies[2].wait_recv()
    relays.append(wsend(9, ypart, y_pairs[2], (tm, core)))
    for j in range(2):
        z_copies[j].wait_recv()
        relays.append(wsend(11 + j, ypart, shared_pairs[j], (tm, core)))
        cot_near[2 + j].wait_recv()
        far_start(0, chalo, 2 + j)
    own_copy.wait_recv()
    for copy in relays:
        copy.wait_recv()

    def unpack_weights(pair):
        for owner in range(n_clip):
            both = wp[owner, pair]
            band = slice(owner * depth, (owner + 1) * depth)
            wg[2 * pair, band] = both[:, :chans]
            wg[2 * pair + 1, band] = both[:, chans:]

    for pair in range(5):
        unpack_weights(pair)

    hid_near = []
    for q in range(2):
        acc = bias_ref[...].reshape(1, chans) + jnp.zeros((half, chans), F32)
        for a in range(3):
            acc = acc + nn_dot(
                xcat[a * width + q * half : a * width + (q + 1) * half],
                wg[3 * a : 3 * a + 3].reshape(3 * chans, chans),
            )
        sig = jax.nn.sigmoid(acc)
        hidden = (acc * sig).astype(BF16)
        hb[q * half : (q + 1) * half] = hidden
        hpack[q * quarter : (q + 1) * quarter] = pack(hidden)
        hid_near += [near_send(2 * chunks, hpack, hhalo, 2 * q + e) for e in range(2)]
        slope[q * half : (q + 1) * half] = sig * (1.0 + acc * (1.0 - sig))

    y_copies[3].wait_recv()
    relays.append(wsend(10, ypart, y_pairs[3], (tm, core)))

    lanes = psum.shape[2]
    wide = n_tm // 2 * lanes
    far_recv(0, chalo)
    hidden_all = hb[...]
    own_cot = cot[...].astype(BF16)
    before, after = unpack(chalo, 0), unpack(chalo, 1)
    products = jnp.concatenate(
        [outer_dot(hidden_all, right) for right in (after, own_cot, before)]
        + [jnp.zeros((chans, n_tm * lanes - 3 * chans), F32)],
        axis=1,
    )
    for owner in range(n_clip):
        gtl[owner % 2, owner // 2] = products[owner * depth : (owner + 1) * depth]
    yc = c // 2
    mine = lax.rem(c, 2)
    core_copies = [
        send(gtl.at[1 - mine, side], rx.at[side], g_send.at[e], g_recv.at[e], (tm, core))
        for e, side in enumerate((1 - yc, yc))
    ]

    def pass_hidden(q):
        hid_near[q].wait_recv()
        far_start(2 * chunks, hhalo, q)

    relays[-1].wait_recv()
    unpack_weights(5)
    grad_h = transpose_dot(after, wg[9]) + transpose_dot(own_cot, wg[10])
    grad_h = grad_h + transpose_dot(before, wg[11])
    pass_hidden(0)

    core_copies[0].wait_recv()
    y_sum = (gtl[mine, 1 - yc] + rx[1 - yc]).astype(BF16)
    grad_y = []
    for e in range(2):
        ysend[e] = y_sum[:, e * wide : (e + 1) * wide]
        grad_y.append(send(ysend.at[e], ry.at[e], g_send.at[2 + e], g_recv.at[2 + e], (tm, ypart)))

    grad_s = grad_h * slope[...]
    for b in range(3):
        gpad[b, width : width + rows] = shifted(grad_s, b - 1).astype(BF16)
    pass_hidden(1)
    pass_hidden(2)

    def grad_conv(q):
        acc = cot[q * half : (q + 1) * half]
        for a in range(3):
            start = (2 - a) * width + q * half
            for b in range(3):
                acc = acc + transpose_dot(gpad[b, start : start + half], wg[3 * a + b])
        gv_v[q * half : (q + 1) * half] = acc

    grad_conv(0)
    pass_hidden(3)

    core_copies[1].wait_recv()
    own_sum = gtl[mine, yc] + rx[yc]
    def scatter_copy(to):
        return pltpu.make_async_remote_copy(
            src_ref=pb.at[to], dst_ref=rs.at[tm], send_sem=a_send.at[to], recv_sem=a_recv.at[tm],
            device_id=(to, c), device_id_type=MESH,
        )

    def arrival(sender):
        return pltpu.make_async_remote_copy(
            src_ref=pb.at[sender], dst_ref=rs.at[sender], send_sem=a_send.at[sender],
            recv_sem=a_recv.at[sender], device_id=(sender, c), device_id_type=MESH,
        )

    for e in range(2):
        grad_y[e].wait_recv()
        both = own_sum[:, e * wide : (e + 1) * wide] + ry[e].astype(F32)
        for place in range(n_tm // 2):
            to = e * (n_tm // 2) + place
            part = both[:, place * lanes : (place + 1) * lanes]
            psum[to] = part
            pb[to] = part.astype(BF16)

            @pl.when(tm != to)
            def _():
                scatter_copy(to).start()

    grad_conv(1)
    out_v[...] = video[...] + nn_dot(hb[...], wg[10])

    rs[tm] = jnp.zeros(rs.shape[1:], BF16)
    for sender in range(n_tm):
        @pl.when(tm != sender)
        def _():
            arrival(sender).wait_recv()
    total = psum[tm]
    for sender in range(n_tm):
        total = total + rs[sender].astype(F32)
    ag[tm] = total.astype(BF16)
    order = sorted(range(1, n_tm), key=lambda step: -min(step, n_tm - step))
    gathers = []
    for step in order:
        to = lax.rem(tm + step, n_tm)
        slot = n_tm - 1 + step
        gathers.append(send(ag.at[tm], ag.at[tm], a_send.at[slot], a_recv.at[slot], (to, c)))

    far_recv(2 * chunks, hhalo)
    out_v[...] = out_v[...] + nn_dot(unpack(hhalo, 0), wg[9]) + nn_dot(unpack(hhalo, 1), wg[11])

    for copy in gathers:
        copy.wait_recv()
    whole = jnp.concatenate([ag[to] for to in range(n_tm)], axis=1).astype(F32) * scale
    for k in range(3):
        gt_v[k] = whole[:, k * chans : (k + 1) * chans]

    for copy in (
        y_copies + z_copies + [own_copy] + relays + cot_near + hid_near
        + core_copies + grad_y + gathers
    ):
        copy.wait_send()
    far_done(0, chalo)
    far_done(2 * chunks, hhalo)
    for to in range(n_tm):
        @pl.when(tm != to)
        def _():
            arrival(to).wait_send()


def hand_over(*refs):
    n = len(refs) // 2
    ins, outs, sem = refs[:n], refs[n : 2 * n], refs[2 * n]
    writes = []
    for e in range(n):
        extent = ins[e].shape[0]
        count = 4 if extent % 64 == 0 else 1
        for q in range(count):
            part = pl.ds(q * (extent // count), extent // count)
            writes.append(pltpu.make_async_copy(ins[e].at[part], outs[e].at[part], sem.at[4 * e + q]))
    for write in writes:
        write.start()
    for write in writes:
        write.wait()


def fused(n_tm, n_clip, video, spatial_w, spatial_b, temporal_w, cotangent):
    clips, frames, height, width, chans = video.shape
    rows = height * width
    depth = spatial_w.shape[1]
    lanes = -(-3 * chans // (128 * n_tm)) * 128
    scale = 1.0 / math.sqrt(rows * n_tm * n_clip)
    any_spec = pl.BlockSpec(memory_space=pltpu.HBM)
    vm_spec = pl.BlockSpec(memory_space=pltpu.VMEM)
    vm = pltpu.VMEM
    dma = pltpu.SemaphoreType.DMA
    results = pl.pallas_call(
        functools.partial(block_kernel, (n_tm, n_clip, height, width, chans, scale)),
        out_shape=(
            vm((rows, chans), F32),
            vm((rows, chans), F32),
            vm((3, depth, chans), F32),
        ),
        in_specs=[any_spec, any_spec, any_spec, any_spec, any_spec],
        out_specs=(vm_spec, vm_spec, vm_spec),
        scratch_shapes=[
            vm((rows, chans), F32),
            vm((rows, chans), F32),
            vm((9, depth, chans), BF16),
            vm((3, depth, chans), F32),
            vm((n_clip, 6, depth, 2 * chans), BF16),
            vm((12, chans, chans), BF16),
            vm((rows + 2 * width, 3 * chans), BF16),
            vm((rows // 2, 2 * chans), BF16),
            vm((2, rows // 2, 2 * chans), BF16),
            vm((rows, chans), BF16),
            vm((rows // 2, 2 * chans), BF16),
            vm((2, rows // 2, 2 * chans), BF16),
            vm((rows, chans), F32),
            vm((3, rows + 2 * width, chans), BF16),
            vm((chans,), F32),
            vm((2, 2, depth, n_tm * lanes), F32),
            vm((2, depth, n_tm * lanes), F32),
            vm((2, depth, n_tm // 2 * lanes), BF16),
            vm((2, depth, n_tm // 2 * lanes), BF16),
            vm((n_tm, depth, lanes), F32),
            vm((n_tm, depth, lanes), BF16),
            vm((n_tm, depth, lanes), BF16),
            vm((n_tm, depth, lanes), BF16),
            dma((5,)),
            dma((13,)),
            dma((13,)),
            dma((16,)),
            dma((16,)),
            dma((4,)),
            dma((4,)),
            dma((2 * n_tm,)),
            dma((2 * n_tm,)),
        ],
        compiler_params=pltpu.CompilerParams(
            collective_id=0, has_side_effects=True, vmem_limit_bytes=65_000_000
        ),
        name="block",
    )(
        video.reshape(rows, chans), spatial_w, spatial_b, temporal_w,
        cotangent.reshape(rows, chans),
    )
    shapes = tuple(jax.ShapeDtypeStruct(array.shape, F32) for array in results)

    out, gv, gt = pl.pallas_call(
        hand_over,
        out_shape=shapes,
        in_specs=[vm_spec] * 3,
        out_specs=(any_spec,) * 3,
        scratch_shapes=[dma((12,))],
        compiler_params=pltpu.CompilerParams(vmem_limit_bytes=2**20),
        name="hand_over",
    )(*results)
    return out.reshape(video.shape), gv.reshape(video.shape), gt


def padded_2(cells, sides, width):
    for axis, dim in sides:
        count = lax.axis_size(axis)
        ends = count - 1
        head = lax.slice_in_dim(cells, 0, width, axis=dim)
        tail = lax.slice_in_dim(cells, cells.shape[dim] - width, cells.shape[dim], axis=dim)
        cells = jnp.concatenate(
            [
                lax.ppermute(tail, axis, [(i, (i + 1) % count) for i in range(ends)]),
                cells,
                lax.ppermute(head, axis, [((i + 1) % count, i) for i in range(ends)]),
            ],
            axis=dim,
        )
    return cells


def native(video, spatial_w, spatial_b, temporal_w, cotangent):
    clips, frames, height, width, chans = video.shape
    row_count = clips * frames * height * width
    pads = ((0, 0), (0, 0), (1, 1), (1, 1), (0, 0))
    padded = jnp.pad(video.astype(BF16), pads)
    temporal_b = temporal_w.astype(BF16)
    spatial_all = lax.all_gather(spatial_w, "clip", axis=1, tiled=True)
    temporal_all = lax.all_gather(temporal_b, "clip", axis=1, tiled=True)
    spatial = jnp.zeros((row_count, chans), F32)
    for y in range(3):
        for x in range(3):
            window = padded[:, :, y : y + height, x : x + width, :].reshape(row_count, chans)
            spatial = spatial + nn_dot(window, spatial_all[3 * y + x])
    spatial = spatial + spatial_b
    sigmoid_s = jax.nn.sigmoid(spatial)
    hidden = (spatial * sigmoid_s).astype(BF16).reshape(video.shape)
    hidden_pad = padded_2(hidden, (("tm", 1),), 1)
    cot_b = cotangent.astype(BF16)
    cot_flat = cot_b.reshape(row_count, chans)
    cot_pad = padded_2(cot_b, (("tm", 1),), 1)
    temporal = jnp.zeros((row_count, chans), F32)
    grad_hidden = jnp.zeros((row_count, chans), F32)
    grads = []
    for k in range(3):
        shifted_hid = hidden_pad[:, k : k + frames].reshape(row_count, chans)
        temporal = temporal + nn_dot(shifted_hid, temporal_all[k])
        shifted_cot = cot_pad[:, 2 - k : 2 - k + frames].reshape(row_count, chans)
        grad_hidden = grad_hidden + transpose_dot(shifted_cot, temporal_all[k])
        grads.append(outer_dot(shifted_hid, cot_flat))
    total_rows = row_count * lax.axis_size("tm") * lax.axis_size("clip")
    summed = lax.psum(jnp.stack(grads), "tm")
    owned = lax.psum_scatter(summed, "clip", scatter_dimension=1, tiled=True)
    grad_spatial = (grad_hidden * sigmoid_s * (1.0 + spatial * (1.0 - sigmoid_s))).astype(BF16)
    grad_frames = jnp.pad(grad_spatial.reshape(video.shape), pads)
    grad_acc = cotangent.reshape(row_count, chans)
    for y in range(3):
        for x in range(3):
            window = grad_frames[:, :, 2 - y : 2 - y + height, 2 - x : 2 - x + width, :]
            window = window.reshape(row_count, chans)
            grad_acc = grad_acc + transpose_dot(window, spatial_all[3 * y + x])
    return (
        video + temporal.reshape(video.shape),
        grad_acc.reshape(video.shape),
        owned * (1.0 / math.sqrt(total_rows)),
    )


def solution(mesh):
    n_tm, n_clip = mesh.shape["tm"], mesh.shape["clip"]

    def on_device(video, spatial_w, spatial_b, temporal_w, cotangent):
        args = (video, spatial_w, spatial_b, temporal_w, cotangent)
        one_frame = video.shape[0] == 1 and video.shape[1] == 1
        if one_frame and spatial_w.shape[1] % 16 == 0 and n_clip == 4 and n_tm % 4 == 0:
            return fused(n_tm, n_clip, *args)
        return native(*args)

    return jax.shard_map(
        on_device,
        mesh=mesh,
        in_specs=(
            P("clip", "tm", None, None, None),
            P(None, "clip", None),
            P(),
            P(None, "clip", None),
            P("clip", "tm", None, None, None),
        ),
        out_specs=(
            P("clip", "tm", None, None, None),
            P("clip", "tm", None, None, None),
            P(None, "clip", None),
        ),
        check_vma=False,
    )
```

```python
import functools
import math

import jax
import jax.numpy as jnp
from jax import lax
from jax.experimental import pallas as pl
from jax.experimental.pallas import tpu as pltpu
from jax.sharding import PartitionSpec as P

F32 = jnp.float32
BF16 = jnp.bfloat16
MESH = pl.DeviceIdType.MESH


def nn_dot(left, right):
    return lax.dot_general(left, right, (((1,), (0,)), ((), ())), preferred_element_type=F32)


def outer_dot(left, right):
    return lax.dot_general(left, right, (((0,), (0,)), ((), ())), preferred_element_type=F32)


def transpose_dot(left, right):
    return lax.dot_general(left, right, (((1,), (1,)), ((), ())), preferred_element_type=F32)


TAIL = 1


def own_cot_of(ref):
    return ref[...].astype(BF16)


def block_kernel(
    dims,
    video_h, sw_h, bias_h, tw_h, cot_h,
    out_v, gv_v, gt_v,
    video, cot, sw, tw, bias_ref, wp, wg, xcat, cb, chalo, cote, cotl, hb, hpack, hhalo, stash, spat, gpad,
    gtl, rx, ysend, ry, psum, pb, rs, ag,
    load_sem, w_send, w_recv, halo_send, halo_recv, g_send, g_recv, a_send, a_recv, gate,
):
    n_tm, n_clip, height, width, chans, scale = dims
    rows = height * width
    depth = sw_h.shape[1]
    half = rows // 2
    quarter = rows // 4
    side_chans = chans // 2
    chunks = 4
    chunk = half // chunks
    low = depth - 16 * TAIL
    head = -(-chans // 128) * 128
    lanes = psum.shape[2]
    n_early = 2 * chans // lanes
    n_late = n_tm - n_early
    skip = n_late * lanes - chans
    tm = lax.axis_index("tm")
    c = lax.axis_index("clip")

    def flip(value, bit):
        return value + bit - 2 * bit * (lax.rem(value // bit, 2))

    core, ypart = flip(c, 1), flip(c, 2)
    xpart, zpart = flip(tm, 1), flip(tm, 2)
    parity = lax.rem(tm, 2)
    h = lax.rem(tm // 2, 2)
    yc = c // 2
    mine = lax.rem(c, 2)
    has_up, has_down = tm + 2 < n_tm, tm >= 2

    def signal(sem, device):
        pl.semaphore_signal(sem, inc=1, device_id=device, device_id_type=MESH)

    def tm_signals(sem):
        signal(sem, (xpart, c))

        @pl.when(has_up)
        def _():
            signal(sem, (tm + 2, c))

        @pl.when(has_down)
        def _():
            signal(sem, (tm - 2, c))

    def tm_waits(sem, extra):
        n_z, z = n_tm // 2, tm // 2
        ups, downs = (2 * n_z - 2 - z) // n_z, (z + n_z - 1) // n_z
        pl.semaphore_wait(sem, 1 + extra + ups + downs)

    rounds = n_tm // 2 - 1

    def gate_step(r):
        if r < rounds:
            tm_waits(gate.at[r], 0)
        if r + 1 < rounds:
            tm_signals(gate.at[r + 1])

    barrier = pltpu.get_barrier_semaphore()
    signal(barrier, (tm, ypart))
    signal(barrier, (tm, core))
    tm_signals(barrier)

    loads = [
        pltpu.make_async_copy(sw_h, sw, load_sem.at[0]),
        pltpu.make_async_copy(tw_h, tw, load_sem.at[1]),
        pltpu.make_async_copy(cot_h, cot, load_sem.at[2]),
        pltpu.make_async_copy(video_h, video, load_sem.at[3]),
        pltpu.make_async_copy(bias_h, bias_ref, load_sem.at[4]),
    ]
    for load in loads:
        load.start()

    def pack(value):
        return jnp.concatenate([value[:quarter], value[quarter:]], axis=1)

    def unpack(ref, slot):
        parts = []
        for q in range(2):
            both = ref[slot, q * quarter : (q + 1) * quarter]
            parts += [both[:, :chans], both[:, chans:]]
        return jnp.concatenate(parts, axis=0)

    loads[0].wait()
    loads[1].wait()
    shard = [sw[tap] for tap in range(9)] + [tw[tap].astype(BF16) for tap in range(3)]
    for pair in range(6):
        wp[c, pair] = jnp.concatenate([shard[2 * pair], shard[2 * pair + 1]], axis=1)
    tm_waits(barrier, 2)

    def send(src, dst, ssem, rsem, device):
        copy = pltpu.make_async_remote_copy(
            src_ref=src, dst_ref=dst, send_sem=ssem, recv_sem=rsem,
            device_id=device, device_id_type=MESH,
        )
        copy.start()
        return copy

    w_copies = []

    def wsend(slot, part, device):
        copy = send(part, part, w_send.at[slot], w_recv.at[slot], device)
        w_copies.append(copy)
        return copy

    def low_part(owner, pair):
        return wp.at[owner, pair, pl.ds(0, low)]

    def rest_part(owner):
        return wp.at[owner, pl.ds(0, 4), pl.ds(low, depth - low)]

    def head_part(owner):
        return wp.at[owner, 4, :, pl.ds(0, head)]

    def tail_part(owner):
        return wp.at[owner, 4, :, pl.ds(head, 2 * chans - head)]

    at_y, at_core, at_x, at_z = (tm, ypart), (tm, core), (xpart, c), (zpart, c)
    y_a = wsend(0, low_part(c, parity), at_y)
    y_b = wsend(1, low_part(c, 2 + h), at_y)
    y_rest = wsend(2, rest_part(c), at_y)
    y_head = wsend(3, head_part(c), at_y)
    own = wsend(8, wp.at[c, pl.ds(0, 5)], at_core)
    tm_signals(gate.at[0])

    loads[2].wait()
    own_cot = cot[...].astype(BF16)
    for q in range(2):
        cb[q * quarter : (q + 1) * quarter] = pack(own_cot[q * half : (q + 1) * half])

    def near_send(base, own_ref, halo, q):
        part = pl.ds(q * chunk, chunk)
        return send(
            own_ref.at[part, :], halo.at[parity, part, :],
            halo_send.at[base + q], halo_recv.at[base + q], (xpart, c),
        )

    def far_copy(base, halo, q):
        target = lax.rem(tm + n_tm + 2 - 4 * parity, n_tm)
        part = pl.ds(q * chunk, chunk)
        return pltpu.make_async_remote_copy(
            src_ref=halo.at[1 - parity, part, :],
            dst_ref=halo.at[parity, part, :],
            send_sem=halo_send.at[base + chunks + q],
            recv_sem=halo_recv.at[base + chunks + q],
            device_id=(target, c),
            device_id_type=MESH,
        )

    sends_far = jnp.logical_or(
        jnp.logical_and(parity == 0, has_up), jnp.logical_and(parity == 1, has_down)
    )
    gets_far = jnp.logical_or(
        jnp.logical_and(parity == 0, has_down), jnp.logical_and(parity == 1, has_up)
    )

    def far_start(base, halo, q):
        @pl.when(sends_far)
        def _():
            far_copy(base, halo, q).start()

    def far_recv(base, halo):
        @pl.when(gets_far)
        def _():
            for q in range(chunks):
                far_copy(base, halo, q).wait_recv()

    def far_done(base, halo):
        @pl.when(sends_far)
        def _():
            for q in range(chunks):
                far_copy(base, halo, q).wait_send()

    cot_near = [near_send(0, cb, chalo, q) for q in range(2)]

    for edge, slot in ((0, 0), (n_tm - 1, 1)):
        @pl.when(tm == edge)
        def _():
            chalo[slot] = jnp.zeros((half, 2 * chans), BF16)
            hhalo[slot] = jnp.zeros((half, 2 * chans), BF16)

    column = lax.rem(lax.broadcasted_iota(jnp.int32, (rows, chans), 0), width)

    def shifted(value, step):
        if step == 0:
            return value
        rolled = pltpu.roll(value, step % rows, 0)
        return jnp.where(column == (0 if step == 1 else width - 1), 0.0, rolled)

    for s in range(2):
        xcat[s, 0:width] = jnp.zeros((width, 3 * side_chans), BF16)
        xcat[s, width + rows :] = jnp.zeros((width, 3 * side_chans), BF16)
    for b in range(3):
        gpad[b, 0:width] = jnp.zeros((width, chans), BF16)
        gpad[b, width + rows :] = jnp.zeros((width, chans), BF16)
    loads[3].wait()
    loads[4].wait()
    frame = video[...]
    views = [shifted(frame, 1 - b).astype(BF16) for b in range(3)]
    for s in range(2):
        xcat[s, width : width + rows] = jnp.concatenate(
            [view[:, s * side_chans : (s + 1) * side_chans] for view in views], axis=1
        )

    def unpack_pair(owner, pair, taps=(0, 1)):
        both = wp[owner, pair] if 1 in taps else wp[owner, pair, :, 0:head]
        band = pl.ds(pl.multiple_of(owner * depth, 16), depth)
        for e in taps:
            wg[2 * pair + e, band] = both[:, e * chans : (e + 1) * chans]

    def unpack_spatial(owner):
        for pair in range(4):
            unpack_pair(owner, pair)
        unpack_pair(owner, 4, (0,))

    def conv_part(s, q):
        total = None
        for a in range(3):
            band = pl.ds(pl.multiple_of(s * side_chans, 16), side_chans)
            weights = jnp.concatenate([wg[3 * a + b, band] for b in range(3)], axis=0)
            term = nn_dot(
                xcat[s, a * width + q * half : a * width + (q + 1) * half], weights
            )
            total = term if total is None else total + term
        return total

    unpack_spatial(c)

    @pl.when(parity == 0)
    def _():
        cote[:, chans : 2 * chans] = own_cot_of(cot)
        cotl[:, chans:] = jnp.zeros((rows, skip), BF16)

    @pl.when(parity == 1)
    def _():
        middle = own_cot_of(cot)
        cote[:, 0 : chans - skip] = middle[:, skip:]
        cote[:, 2 * chans - skip :] = jnp.zeros((rows, skip), BF16)
        cotl[:, chans:] = middle[:, :skip]

    own.wait_recv()
    unpack_spatial(core)
    for q in range(2):
        spat[q * half : (q + 1) * half] = bias_ref[...].reshape(1, chans) + conv_part(yc, q)

    y_a.wait_recv()
    x_a = wsend(6, low_part(ypart, parity), at_x)
    r_a = wsend(10, low_part(ypart, parity), at_core)
    cot_near += [near_send(0, cb, chalo, q) for q in range(2, chunks)]
    cot_near[0].wait_recv()
    far_start(0, chalo, 0)
    y_b.wait_recv()
    z_b = wsend(7, low_part(ypart, 2 + h), at_z)
    r_b = wsend(11, low_part(ypart, 2 + h), at_core)
    cot_near[1].wait_recv()
    far_start(0, chalo, 1)
    gate_step(0)
    y_rest.wait_recv()
    r_rest = wsend(12, rest_part(ypart), at_core)
    y_tail = wsend(4, tail_part(c), at_y)
    y_last = wsend(5, wp.at[c, 5], at_y)
    own_last = wsend(9, wp.at[c, 5], at_core)
    x_a.wait_recv()
    r_x = wsend(14, low_part(ypart, 1 - parity), at_core)
    gate_step(1)
    y_head.wait_recv()
    r_head = wsend(13, head_part(ypart), at_core)
    z_b.wait_recv()
    r_z = wsend(15, low_part(ypart, 3 - h), at_core)
    unpack_spatial(ypart)
    cot_near[2].wait_recv()
    far_start(0, chalo, 2)
    for copy in (r_a, r_b, r_rest, r_x, r_head, r_z):
        copy.wait_recv()
    unpack_spatial(flip(core, 2))

    def stash_copy(q):
        part = pl.ds(q * chunk, chunk)
        return pltpu.make_async_remote_copy(
            src_ref=hpack.at[part, :], dst_ref=stash.at[part, :],
            send_sem=halo_send.at[4 * chunks + q], recv_sem=halo_recv.at[4 * chunks + q],
            device_id=(lax.rem(tm + n_tm + 4 * parity - 2, n_tm), c), device_id_type=MESH,
        )

    def forward_copy(q):
        part = pl.ds(q * chunk, chunk)
        return pltpu.make_async_remote_copy(
            src_ref=stash.at[part, :], dst_ref=hhalo.at[1 - parity, part, :],
            send_sem=halo_send.at[3 * chunks + q], recv_sem=halo_recv.at[3 * chunks + q],
            device_id=at_x, device_id_type=MESH,
        )

    def stash_hidden(q):
        @pl.when(gets_far)
        def _():
            stash_copy(q).start()

    def forward_hidden(q):
        @pl.when(sends_far)
        def _():
            stash_copy(q).wait_recv()
            forward_copy(q).start()

    hid_near = []
    for q in range(2):
        acc = spat[q * half : (q + 1) * half] + conv_part(1 - yc, q)
        hidden = (acc * jax.nn.sigmoid(acc)).astype(BF16)
        hb[q * half : (q + 1) * half] = hidden
        hpack[q * quarter : (q + 1) * quarter] = pack(hidden)
        hid_near += [near_send(2 * chunks, hpack, hhalo, 2 * q + e) for e in range(2)]
        if q == 1:
            stash_hidden(2)
            stash_hidden(3)
        spat[q * half : (q + 1) * half] = acc
        if q == 0:
            cot_near[3].wait_recv()
            far_start(0, chalo, 3)

    early = (n_tm - n_early) * parity
    late = n_early * (1 - parity)

    def place(products, first, count):
        for i in range(count):
            for owner in range(n_clip):
                gtl[owner % 2, owner // 2, first + i] = products[
                    owner * depth : (owner + 1) * depth, i * lanes : (i + 1) * lanes
                ]

    def core_send(slot, side, first, count):
        part = pl.ds(first, count)
        return send(
            gtl.at[1 - mine, side, part], rx.at[side, part],
            g_send.at[slot], g_recv.at[slot], at_core,
        )

    def y_send(slot, first, count):
        for i in range(count):
            ysend[first + i] = (gtl[mine, 1 - yc, first + i] + rx[1 - yc, first + i]).astype(BF16)
        part = pl.ds(first, count)
        return send(ysend.at[part], ry.at[part], g_send.at[slot], g_recv.at[slot], at_y)

    share = n_tm // 4
    first_owner = n_tm // 2 - 2
    owns = jnp.logical_and(tm >= first_owner, tm < first_owner + 4)

    def scatter_copy(unit):
        place_in = lax.rem(unit, share)
        return pltpu.make_async_remote_copy(
            src_ref=pb.at[unit], dst_ref=rs.at[tm, place_in],
            send_sem=a_send.at[unit], recv_sem=a_recv.at[tm * share + place_in],
            device_id=(first_owner + unit // share, c), device_id_type=MESH,
        )

    def arrival(sender, place_in):
        return pltpu.make_async_remote_copy(
            src_ref=pb.at[place_in], dst_ref=rs.at[sender, place_in], send_sem=a_send.at[place_in],
            recv_sem=a_recv.at[sender * share + place_in],
            device_id=(sender, c), device_id_type=MESH,
        )

    def gather_copy(owner, to):
        part = ag.at[pl.ds(owner * share, share)]
        return pltpu.make_async_remote_copy(
            src_ref=part, dst_ref=part,
            send_sem=a_send.at[n_tm + to], recv_sem=a_recv.at[n_tm * share + owner],
            device_id=(to, c), device_id_type=MESH,
        )

    def scatter(first, count):
        for i in range(count):
            to = first + i
            part = gtl[mine, yc, to] + rx[yc, to] + ry[to].astype(F32)
            psum[to] = part
            pb[to] = part.astype(BF16)

            @pl.when(tm != first_owner + to // share)
            def _():
                scatter_copy(to).start()

    def pass_hidden(q):
        hid_near[q].wait_recv()
        far_start(2 * chunks, hhalo, q)

    @pl.when(parity == 0)
    def _():
        cote[:, 0:chans] = unpack(chalo, 1)

    @pl.when(parity == 1)
    def _():
        cote[:, chans - skip : 2 * chans - skip] = unpack(chalo, 0)

    place(outer_dot(hb[...], cote[...]), early, n_early)
    core_e = [core_send(e, side, early, n_early) for e, side in enumerate((1 - yc, yc))]
    core_e[0].wait_recv()
    y_e = y_send(4, early, n_early)

    far_recv(0, chalo)
    cotl[:, 0:chans] = unpack(chalo, parity)
    place(outer_dot(hb[...], cotl[...]), late, n_late)
    core_l = [core_send(2 + e, side, late, n_late) for e, side in enumerate((1 - yc, yc))]

    y_tail.wait_recv()
    r_tail = wsend(16, tail_part(ypart), at_core)
    y_last.wait_recv()
    r_last = wsend(17, wp.at[ypart, 5], at_core)
    pass_hidden(0)
    core_l[0].wait_recv()
    y_l = y_send(5, late, n_late)

    for copy in (own_last, r_tail, r_last):
        copy.wait_recv()
    for owner in range(n_clip):
        unpack_pair(owner, 4, (1,))
        unpack_pair(owner, 5)
    grad_h = transpose_dot(unpack(chalo, 1), wg[9])
    grad_h = grad_h + transpose_dot(cot[...].astype(BF16), wg[10])
    grad_h = grad_h + transpose_dot(unpack(chalo, 0), wg[11])
    acc = spat[...]
    sig = jax.nn.sigmoid(acc)
    grad_s = grad_h * (sig * (1.0 + acc * (1.0 - sig)))
    for b in range(3):
        gpad[b, width : width + rows] = shifted(grad_s, b - 1).astype(BF16)

    for r in range(2, rounds):
        gate_step(r)
    core_e[1].wait_recv()
    y_e.wait_recv()
    scatter(early, n_early)
    pass_hidden(1)

    def grad_conv(q):
        acc = cot[q * half : (q + 1) * half]
        for a in range(3):
            start = (2 - a) * width + q * half
            for b in range(3):
                acc = acc + transpose_dot(gpad[b, start : start + half], wg[3 * a + b])
        gv_v[q * half : (q + 1) * half] = acc

    core_l[1].wait_recv()
    y_l.wait_recv()
    scatter(late, n_late)
    forward_hidden(2)
    forward_hidden(3)
    grad_conv(0)
    grad_conv(1)
    out_v[...] = video[...] + nn_dot(hb[...], wg[10])

    @pl.when(owns)
    def _():
        mine_at = tm - first_owner
        rs[tm] = jnp.zeros(rs.shape[1:], BF16)
        for sender in range(n_tm):
            @pl.when(tm != sender)
            def _():
                for e in range(share):
                    arrival(sender, e).wait_recv()
        for e in range(share):
            total = psum[mine_at * share + e]
            for sender in range(n_tm):
                total = total + rs[sender, e].astype(F32)
            ag[mine_at * share + e] = total.astype(BF16)
        for to in (0, 1, n_tm - 2, n_tm - 1, *range(2, n_tm - 2)):
            @pl.when(tm != to)
            def _():
                gather_copy(mine_at, to).start()

    far_recv(2 * chunks, hhalo)
    hid_near[2].wait_recv()
    hid_near[3].wait_recv()
    out_v[...] = out_v[...] + nn_dot(unpack(hhalo, 0), wg[9]) + nn_dot(unpack(hhalo, 1), wg[11])

    for owner in range(4):
        @pl.when(tm != first_owner + owner)
        def _():
            gather_copy(owner, tm).wait_recv()
    whole = jnp.concatenate([ag[to] for to in range(n_tm)], axis=1).astype(F32) * scale
    for k in range(3):
        gt_v[k] = whole[:, k * chans : (k + 1) * chans]

    for copy in w_copies + cot_near + hid_near + core_e + core_l + [y_e, y_l]:
        copy.wait_send()
    far_done(0, chalo)

    @pl.when(sends_far)
    def _():
        for q in range(2):
            far_copy(2 * chunks, hhalo, q).wait_send()
        for q in range(2, chunks):
            forward_copy(q).wait_send()

    @pl.when(gets_far)
    def _():
        for q in range(2, chunks):
            stash_copy(q).wait_send()

    for unit in range(n_tm):
        @pl.when(tm != first_owner + unit // share)
        def _():
            scatter_copy(unit).wait_send()

    @pl.when(owns)
    def _():
        for to in range(n_tm):
            @pl.when(tm != to)
            def _():
                gather_copy(tm - first_owner, to).wait_send()


def hand_over(*refs):
    n = len(refs) // 2
    ins, outs, sem = refs[:n], refs[n : 2 * n], refs[2 * n]
    writes = []
    for e in range(n):
        extent = ins[e].shape[0]
        count = 4 if extent % 64 == 0 else 1
        for q in range(count):
            part = pl.ds(q * (extent // count), extent // count)
            writes.append(pltpu.make_async_copy(ins[e].at[part], outs[e].at[part], sem.at[4 * e + q]))
    for write in writes:
        write.start()
    for write in writes:
        write.wait()


def fused(n_tm, n_clip, video, spatial_w, spatial_b, temporal_w, cotangent):
    clips, frames, height, width, chans = video.shape
    rows = height * width
    depth = spatial_w.shape[1]
    lanes = -(-3 * chans // (128 * n_tm)) * 128
    scale = 1.0 / math.sqrt(rows * n_tm * n_clip)
    any_spec = pl.BlockSpec(memory_space=pltpu.HBM)
    vm_spec = pl.BlockSpec(memory_space=pltpu.VMEM)
    vm = pltpu.VMEM
    dma = pltpu.SemaphoreType.DMA
    results = pl.pallas_call(
        functools.partial(block_kernel, (n_tm, n_clip, height, width, chans, scale)),
        out_shape=(
            vm((rows, chans), F32),
            vm((rows, chans), F32),
            vm((3, depth, chans), F32),
        ),
        in_specs=[any_spec, any_spec, any_spec, any_spec, any_spec],
        out_specs=(vm_spec, vm_spec, vm_spec),
        scratch_shapes=[
            vm((rows, chans), F32),
            vm((rows, chans), F32),
            vm((9, depth, chans), BF16),
            vm((3, depth, chans), F32),
            vm((chans,), F32),
            vm((n_clip, 6, depth, 2 * chans), BF16),
            vm((12, chans, chans), BF16),
            vm((2, rows + 2 * width, 3 * chans // 2), BF16),
            vm((rows // 2, 2 * chans), BF16),
            vm((2, rows // 2, 2 * chans), BF16),
            vm((rows, 2 * chans), BF16),
            vm((rows, n_tm * lanes - 2 * chans), BF16),
            vm((rows, chans), BF16),
            vm((rows // 2, 2 * chans), BF16),
            vm((2, rows // 2, 2 * chans), BF16),
            vm((rows // 2, 2 * chans), BF16),
            vm((rows, chans), F32),
            vm((3, rows + 2 * width, chans), BF16),
            vm((2, 2, n_tm, depth, lanes), F32),
            vm((2, n_tm, depth, lanes), F32),
            vm((n_tm, depth, lanes), BF16),
            vm((n_tm, depth, lanes), BF16),
            vm((n_tm, depth, lanes), F32),
            vm((n_tm, depth, lanes), BF16),
            vm((n_tm, n_tm // 4, depth, lanes), BF16),
            vm((n_tm, depth, lanes), BF16),
            dma((5,)),
            dma((18,)),
            dma((18,)),
            dma((20,)),
            dma((20,)),
            dma((6,)),
            dma((6,)),
            dma((2 * n_tm,)),
            dma((n_tm * (n_tm // 4) + 4,)),
            pltpu.SemaphoreType.REGULAR((n_tm // 2 - 1,)),
        ],
        compiler_params=pltpu.CompilerParams(
            collective_id=0, has_side_effects=True, vmem_limit_bytes=65_000_000
        ),
        name="block",
    )(
        video.reshape(rows, chans), spatial_w, spatial_b, temporal_w,
        cotangent.reshape(rows, chans),
    )
    shapes = tuple(jax.ShapeDtypeStruct(array.shape, F32) for array in results)

    out, gv, gt = pl.pallas_call(
        hand_over,
        out_shape=shapes,
        in_specs=[vm_spec] * 3,
        out_specs=(any_spec,) * 3,
        scratch_shapes=[dma((12,))],
        compiler_params=pltpu.CompilerParams(vmem_limit_bytes=2**20),
        name="hand_over",
    )(*results)
    return out.reshape(video.shape), gv.reshape(video.shape), gt


def padded_2(cells, sides, width):
    for axis, dim in sides:
        count = lax.axis_size(axis)
        ends = count - 1
        head = lax.slice_in_dim(cells, 0, width, axis=dim)
        tail = lax.slice_in_dim(cells, cells.shape[dim] - width, cells.shape[dim], axis=dim)
        cells = jnp.concatenate(
            [
                lax.ppermute(tail, axis, [(i, (i + 1) % count) for i in range(ends)]),
                cells,
                lax.ppermute(head, axis, [((i + 1) % count, i) for i in range(ends)]),
            ],
            axis=dim,
        )
    return cells


def native(video, spatial_w, spatial_b, temporal_w, cotangent):
    clips, frames, height, width, chans = video.shape
    row_count = clips * frames * height * width
    pads = ((0, 0), (0, 0), (1, 1), (1, 1), (0, 0))
    padded = jnp.pad(video.astype(BF16), pads)
    temporal_b = temporal_w.astype(BF16)
    spatial_all = lax.all_gather(spatial_w, "clip", axis=1, tiled=True)
    temporal_all = lax.all_gather(temporal_b, "clip", axis=1, tiled=True)
    spatial = jnp.zeros((row_count, chans), F32)
    for y in range(3):
        for x in range(3):
            window = padded[:, :, y : y + height, x : x + width, :].reshape(row_count, chans)
            spatial = spatial + nn_dot(window, spatial_all[3 * y + x])
    spatial = spatial + spatial_b
    sigmoid_s = jax.nn.sigmoid(spatial)
    hidden = (spatial * sigmoid_s).astype(BF16).reshape(video.shape)
    hidden_pad = padded_2(hidden, (("tm", 1),), 1)
    cot_b = cotangent.astype(BF16)
    cot_flat = cot_b.reshape(row_count, chans)
    cot_pad = padded_2(cot_b, (("tm", 1),), 1)
    temporal = jnp.zeros((row_count, chans), F32)
    grad_hidden = jnp.zeros((row_count, chans), F32)
    grads = []
    for k in range(3):
        shifted_hid = hidden_pad[:, k : k + frames].reshape(row_count, chans)
        temporal = temporal + nn_dot(shifted_hid, temporal_all[k])
        shifted_cot = cot_pad[:, 2 - k : 2 - k + frames].reshape(row_count, chans)
        grad_hidden = grad_hidden + transpose_dot(shifted_cot, temporal_all[k])
        grads.append(outer_dot(shifted_hid, cot_flat))
    total_rows = row_count * lax.axis_size("tm") * lax.axis_size("clip")
    summed = lax.psum(jnp.stack(grads), "tm")
    owned = lax.psum_scatter(summed, "clip", scatter_dimension=1, tiled=True)
    grad_spatial = (grad_hidden * sigmoid_s * (1.0 + spatial * (1.0 - sigmoid_s))).astype(BF16)
    grad_frames = jnp.pad(grad_spatial.reshape(video.shape), pads)
    grad_acc = cotangent.reshape(row_count, chans)
    for y in range(3):
        for x in range(3):
            window = grad_frames[:, :, 2 - y : 2 - y + height, 2 - x : 2 - x + width, :]
            window = window.reshape(row_count, chans)
            grad_acc = grad_acc + transpose_dot(window, spatial_all[3 * y + x])
    return (
        video + temporal.reshape(video.shape),
        grad_acc.reshape(video.shape),
        owned * (1.0 / math.sqrt(total_rows)),
    )


def solution(mesh):
    n_tm, n_clip = mesh.shape["tm"], mesh.shape["clip"]

    def on_device(video, spatial_w, spatial_b, temporal_w, cotangent):
        args = (video, spatial_w, spatial_b, temporal_w, cotangent)
        one_frame = video.shape[0] == 1 and video.shape[1] == 1
        depth, chans = spatial_w.shape[1:]
        lanes = -(-3 * chans // (128 * n_tm)) * 128
        fits = depth % 16 == 0 and depth > 16 * TAIL and 2 * chans % lanes == 0
        if one_frame and fits and n_clip == 4 and n_tm % 4 == 0 and n_tm * lanes <= 4 * chans:
            return fused(n_tm, n_clip, *args)
        return native(*args)

    return jax.shard_map(
        on_device,
        mesh=mesh,
        in_specs=(
            P("clip", "tm", None, None, None),
            P(None, "clip", None),
            P(),
            P(None, "clip", None),
            P("clip", "tm", None, None, None),
        ),
        out_specs=(
            P("clip", "tm", None, None, None),
            P("clip", "tm", None, None, None),
            P(None, "clip", None),
        ),
        check_vma=False,
    )
```

```python
import functools
import math

import jax
import jax.numpy as jnp
from jax import lax
from jax.experimental import pallas as pl
from jax.experimental.pallas import tpu as pltpu
from jax.sharding import PartitionSpec as P

F32 = jnp.float32
BF16 = jnp.bfloat16
MESH = pl.DeviceIdType.MESH


def nn_dot(left, right):
    return lax.dot_general(left, right, (((1,), (0,)), ((), ())), preferred_element_type=F32)


def outer_dot(left, right):
    return lax.dot_general(left, right, (((0,), (0,)), ((), ())), preferred_element_type=F32)


def transpose_dot(left, right):
    return lax.dot_general(left, right, (((1,), (1,)), ((), ())), preferred_element_type=F32)


TAIL = 2


def own_cot_of(ref):
    return ref[...].astype(BF16)


def block_kernel(
    dims,
    video_h, sw_h, bias_h, tw_h, cot_h,
    out_v, gv_v, gt_v,
    video, cot, sw, tw, bias_ref, wp, wg, xcat, cb, chalo, cote, cotl, hb, cstash, hpack, hhalo, hstash, spat, gpad,
    gtl, rx, ysend, ry, psum, pb, rs, ag,
    load_sem, w_send, w_recv, halo_send, halo_recv, g_send, g_recv, a_send, a_recv, gate,
):
    n_tm, n_clip, height, width, chans, scale = dims
    rows = height * width
    depth = sw_h.shape[1]
    half = rows // 2
    quarter = rows // 4
    side_chans = chans // 2
    chunks = 4
    chunk = half // chunks
    low = depth - 16 * TAIL
    head = -(-chans // 128) * 128
    lanes = psum.shape[2]
    n_early = 2 * chans // lanes
    n_late = n_tm - n_early
    skip = n_late * lanes - chans
    tm = lax.axis_index("tm")
    c = lax.axis_index("clip")

    def flip(value, bit):
        return value + bit - 2 * bit * (lax.rem(value // bit, 2))

    core, ypart = flip(c, 1), flip(c, 2)
    xpart, zpart = flip(tm, 1), flip(tm, 2)
    parity = lax.rem(tm, 2)
    h = lax.rem(tm // 2, 2)
    yc = c // 2
    mine = lax.rem(c, 2)
    has_up, has_down = tm + 2 < n_tm, tm >= 2

    def signal(sem, device):
        pl.semaphore_signal(sem, inc=1, device_id=device, device_id_type=MESH)

    def tm_signals(sem):
        signal(sem, (xpart, c))

        @pl.when(has_up)
        def _():
            signal(sem, (tm + 2, c))

        @pl.when(has_down)
        def _():
            signal(sem, (tm - 2, c))

    def tm_waits(sem, extra):
        n_z, z = n_tm // 2, tm // 2
        ups, downs = (2 * n_z - 2 - z) // n_z, (z + n_z - 1) // n_z
        pl.semaphore_wait(sem, 1 + extra + ups + downs)

    rounds = n_tm // 2 - 1

    def gate_step(r):
        if r < rounds:
            tm_waits(gate.at[r], 0)
        if r + 1 < rounds:
            tm_signals(gate.at[r + 1])

    barrier = pltpu.get_barrier_semaphore()
    signal(barrier, (tm, ypart))
    signal(barrier, (tm, core))
    tm_signals(barrier)

    loads = [
        pltpu.make_async_copy(sw_h.at[pl.ds(0, 4)], sw.at[pl.ds(0, 4)], load_sem.at[0]),
        pltpu.make_async_copy(sw_h.at[pl.ds(4, 4)], sw.at[pl.ds(4, 4)], load_sem.at[5]),
        pltpu.make_async_copy(sw_h.at[pl.ds(8, 1)], sw.at[pl.ds(8, 1)], load_sem.at[6]),
        pltpu.make_async_copy(tw_h, tw, load_sem.at[1]),
        pltpu.make_async_copy(cot_h, cot, load_sem.at[2]),
        pltpu.make_async_copy(video_h, video, load_sem.at[3]),
        pltpu.make_async_copy(bias_h, bias_ref, load_sem.at[4]),
    ]
    for load in loads:
        load.start()

    def pack(value):
        return jnp.concatenate([value[:quarter], value[quarter:]], axis=1)

    def unpack(ref, slot):
        parts = []
        for q in range(2):
            both = ref[slot, q * quarter : (q + 1) * quarter]
            parts += [both[:, :chans], both[:, chans:]]
        return jnp.concatenate(parts, axis=0)

    for load in loads[:2]:
        load.wait()
    for pair in range(4):
        wp[c, pair] = jnp.concatenate([sw[2 * pair], sw[2 * pair + 1]], axis=1)
    tm_waits(barrier, 2)

    def send(src, dst, ssem, rsem, device):
        copy = pltpu.make_async_remote_copy(
            src_ref=src, dst_ref=dst, send_sem=ssem, recv_sem=rsem,
            device_id=device, device_id_type=MESH,
        )
        copy.start()
        return copy

    w_copies = []

    def wsend(slot, part, device):
        copy = send(part, part, w_send.at[slot], w_recv.at[slot], device)
        w_copies.append(copy)
        return copy

    def low_part(owner, pair):
        return wp.at[owner, pair, pl.ds(0, low)]

    def rest_part(owner):
        return wp.at[owner, pl.ds(0, 4), pl.ds(low, depth - low)]

    def head_part(owner):
        return wp.at[owner, 4, :, pl.ds(0, head)]

    def tail_part(owner):
        return wp.at[owner, 4, :, pl.ds(head, 2 * chans - head)]

    at_y, at_core, at_x, at_z = (tm, ypart), (tm, core), (xpart, c), (zpart, c)
    y_a = wsend(0, low_part(c, h), at_y)
    y_b = wsend(1, low_part(c, 2 + h), at_y)
    y_rest = wsend(2, rest_part(c), at_y)
    for load in loads[2:4]:
        load.wait()
    first = tw[0].astype(BF16)
    wp[c, 4] = jnp.concatenate([sw[8], first], axis=1)
    wp[c, 5] = jnp.concatenate([tw[1].astype(BF16), tw[2].astype(BF16)], axis=1)
    y_head = wsend(3, head_part(c), at_y)
    own = wsend(8, wp.at[c, pl.ds(0, 5)], at_core)
    tm_signals(gate.at[0])

    loads[4].wait()
    own_cot = cot[...].astype(BF16)
    for q in range(2):
        cb[q * quarter : (q + 1) * quarter] = pack(own_cot[q * half : (q + 1) * half])

    def near_send(base, own_ref, halo, q):
        part = pl.ds(q * chunk, chunk)
        return send(
            own_ref.at[part, :], halo.at[parity, part, :],
            halo_send.at[base + q], halo_recv.at[base + q], (xpart, c),
        )

    def far_copy(base, halo, q):
        target = lax.rem(tm + n_tm + 2 - 4 * parity, n_tm)
        part = pl.ds(q * chunk, chunk)
        return pltpu.make_async_remote_copy(
            src_ref=halo.at[1 - parity, part, :],
            dst_ref=halo.at[parity, part, :],
            send_sem=halo_send.at[base + chunks + q],
            recv_sem=halo_recv.at[base + chunks + q],
            device_id=(target, c),
            device_id_type=MESH,
        )

    sends_far = jnp.logical_or(
        jnp.logical_and(parity == 0, has_up), jnp.logical_and(parity == 1, has_down)
    )
    gets_far = jnp.logical_or(
        jnp.logical_and(parity == 0, has_down), jnp.logical_and(parity == 1, has_up)
    )

    def far_start(base, halo, q):
        @pl.when(sends_far)
        def _():
            far_copy(base, halo, q).start()

    def far_recv(base, halo):
        @pl.when(gets_far)
        def _():
            for q in range(chunks):
                far_copy(base, halo, q).wait_recv()

    def stash_copy(slot, own_ref, held, q):
        part = pl.ds(q * chunk, chunk)
        return pltpu.make_async_remote_copy(
            src_ref=own_ref.at[part, :], dst_ref=held.at[part, :],
            send_sem=halo_send.at[4 * chunks + slot], recv_sem=halo_recv.at[4 * chunks + slot],
            device_id=(lax.rem(tm + n_tm + 4 * parity - 2, n_tm), c), device_id_type=MESH,
        )

    def forward_copy(base, held, halo, q):
        part = pl.ds(q * chunk, chunk)
        return pltpu.make_async_remote_copy(
            src_ref=held.at[part, :], dst_ref=halo.at[1 - parity, part, :],
            send_sem=halo_send.at[base + chunks + q], recv_sem=halo_recv.at[base + chunks + q],
            device_id=at_x, device_id_type=MESH,
        )

    cot_stash = (0, cb, cstash), (1, cb, cstash)
    hid_stash = (2, hpack, hstash), (3, hpack, hstash)

    def stash_start(which, q):
        @pl.when(gets_far)
        def _():
            stash_copy(*which, q).start()

    def forward(base, which, halo, q):
        @pl.when(sends_far)
        def _():
            stash_copy(*which, q).wait_recv()
            forward_copy(base, which[2], halo, q).start()

    cot_near = [near_send(0, cb, chalo, q) for q in range(chunks)]
    for e in range(2):
        stash_start(cot_stash[e], 2 + e)

    for edge, slot in ((0, 0), (n_tm - 1, 1)):
        @pl.when(tm == edge)
        def _():
            chalo[slot] = jnp.zeros((half, 2 * chans), BF16)
            hhalo[slot] = jnp.zeros((half, 2 * chans), BF16)

    column = lax.rem(lax.broadcasted_iota(jnp.int32, (rows, chans), 0), width)

    def shifted(value, step):
        if step == 0:
            return value
        rolled = pltpu.roll(value, step % rows, 0)
        return jnp.where(column == (0 if step == 1 else width - 1), 0.0, rolled)

    for s in range(2):
        xcat[s, 0:width] = jnp.zeros((width, 3 * side_chans), BF16)
        xcat[s, width + rows :] = jnp.zeros((width, 3 * side_chans), BF16)
    for b in range(3):
        gpad[b, 0:width] = jnp.zeros((width, chans), BF16)
        gpad[b, width + rows :] = jnp.zeros((width, chans), BF16)
    loads[5].wait()
    loads[6].wait()
    frame = video[...]
    views = [shifted(frame, 1 - b).astype(BF16) for b in range(3)]
    for s in range(2):
        xcat[s, width : width + rows] = jnp.concatenate(
            [view[:, s * side_chans : (s + 1) * side_chans] for view in views], axis=1
        )

    def unpack_pair(owner, pair, taps=(0, 1)):
        both = wp[owner, pair] if 1 in taps else wp[owner, pair, :, 0:head]
        band = pl.ds(pl.multiple_of(owner * depth, 16), depth)
        for e in taps:
            wg[2 * pair + e, band] = both[:, e * chans : (e + 1) * chans]

    def unpack_spatial(owner, first=0, count=5):
        for pair in range(first, first + count):
            unpack_pair(owner, pair, (0, 1) if pair < 4 else (0,))

    def conv_part(s, q, taps=(0, 1, 2)):
        total = None
        for a in taps:
            band = pl.ds(pl.multiple_of(s * side_chans, 16), side_chans)
            weights = jnp.concatenate([wg[3 * a + b, band] for b in range(3)], axis=0)
            term = nn_dot(
                xcat[s, a * width + q * half : a * width + (q + 1) * half], weights
            )
            total = term if total is None else total + term
        return total

    unpack_spatial(c)

    @pl.when(parity == 0)
    def _():
        cote[:, chans : 2 * chans] = own_cot_of(cot)
        cotl[:, chans:] = jnp.zeros((rows, skip), BF16)

    @pl.when(parity == 1)
    def _():
        middle = own_cot_of(cot)
        cote[:, 0 : chans - skip] = middle[:, skip:]
        cote[:, 2 * chans - skip :] = jnp.zeros((rows, skip), BF16)
        cotl[:, chans:] = middle[:, :skip]

    own.wait_recv()
    unpack_spatial(core)
    for q in range(2):
        spat[q * half : (q + 1) * half] = bias_ref[...].reshape(1, chans) + conv_part(yc, q)

    y_a.wait_recv()
    z_a = wsend(6, low_part(ypart, h), at_z)
    r_a = wsend(10, low_part(ypart, h), at_core)
    y_b.wait_recv()
    z_b = wsend(7, low_part(ypart, 2 + h), at_z)
    r_b = wsend(11, low_part(ypart, 2 + h), at_core)
    gate_step(0)
    y_rest.wait_recv()
    r_rest = wsend(12, rest_part(ypart), at_core)
    z_a.wait_recv()
    r_za = wsend(14, low_part(ypart, 1 - h), at_core)
    gate_step(1)
    y_head.wait_recv()
    r_head = wsend(13, head_part(ypart), at_core)
    y_tail = wsend(4, tail_part(c), at_y)
    y_last = wsend(5, wp.at[c, 5], at_y)
    for q in range(2):
        cot_near[q].wait_recv()
        far_start(0, chalo, q)
    z_b.wait_recv()
    r_zb = wsend(15, low_part(ypart, 3 - h), at_core)
    for e in range(2):
        forward(0, cot_stash[e], chalo, 2 + e)
    diagonal = flip(core, 2)
    unpack_spatial(ypart)
    for copy in (r_a, r_rest, r_za):
        copy.wait_recv()
    unpack_spatial(diagonal, 0, 2)
    for q in range(2):
        part = pl.ds(q * half, half)
        spat[part] = spat[part] + conv_part(1 - yc, q, (0,))
    for copy in (r_b, r_head, r_zb):
        copy.wait_recv()
    own_last = wsend(9, wp.at[c, 5], at_core)
    unpack_spatial(diagonal, 2, 3)

    hid_near = []
    for q in range(2):
        acc = spat[q * half : (q + 1) * half] + conv_part(1 - yc, q, (1, 2))
        hidden = (acc * jax.nn.sigmoid(acc)).astype(BF16)
        hb[q * half : (q + 1) * half] = hidden
        hpack[q * quarter : (q + 1) * quarter] = pack(hidden)
        hid_near += [near_send(2 * chunks, hpack, hhalo, 2 * q + e) for e in range(2)]
        if q == 1:
            for e in range(2):
                stash_start(hid_stash[e], 2 + e)
        spat[q * half : (q + 1) * half] = acc
    cot_near[2].wait_recv()
    cot_near[3].wait_recv()

    early = (n_tm - n_early) * parity
    late = n_early * (1 - parity)

    def place(products, first, count):
        for i in range(count):
            for owner in range(n_clip):
                gtl[owner % 2, owner // 2, first + i] = products[
                    owner * depth : (owner + 1) * depth, i * lanes : (i + 1) * lanes
                ]

    def core_send(slot, side, first, count):
        part = pl.ds(first, count)
        return send(
            gtl.at[1 - mine, side, part], rx.at[side, part],
            g_send.at[slot], g_recv.at[slot], at_core,
        )

    def y_send(slot, first, count):
        for i in range(count):
            ysend[first + i] = (gtl[mine, 1 - yc, first + i] + rx[1 - yc, first + i]).astype(BF16)
        part = pl.ds(first, count)
        return send(ysend.at[part], ry.at[part], g_send.at[slot], g_recv.at[slot], at_y)

    share = n_tm // 4
    first_owner = n_tm // 2 - 2
    owns = jnp.logical_and(tm >= first_owner, tm < first_owner + 4)

    def scatter_copy(unit):
        place_in = lax.rem(unit, share)
        return pltpu.make_async_remote_copy(
            src_ref=pb.at[unit], dst_ref=rs.at[tm, place_in],
            send_sem=a_send.at[unit], recv_sem=a_recv.at[tm * share + place_in],
            device_id=(first_owner + unit // share, c), device_id_type=MESH,
        )

    def arrival(sender, place_in):
        return pltpu.make_async_remote_copy(
            src_ref=pb.at[place_in], dst_ref=rs.at[sender, place_in], send_sem=a_send.at[place_in],
            recv_sem=a_recv.at[sender * share + place_in],
            device_id=(sender, c), device_id_type=MESH,
        )

    def gather_copy(owner, to):
        part = ag.at[pl.ds(owner * share, share)]
        return pltpu.make_async_remote_copy(
            src_ref=part, dst_ref=part,
            send_sem=a_send.at[n_tm + to], recv_sem=a_recv.at[n_tm * share + owner],
            device_id=(to, c), device_id_type=MESH,
        )

    def scatter(first, count):
        for i in range(count):
            to = first + i
            part = gtl[mine, yc, to] + rx[yc, to] + ry[to].astype(F32)
            psum[to] = part
            pb[to] = part.astype(BF16)

            @pl.when(tm != first_owner + to // share)
            def _():
                scatter_copy(to).start()

    def pass_hidden(q):
        hid_near[q].wait_recv()
        far_start(2 * chunks, hhalo, q)

    @pl.when(parity == 0)
    def _():
        cote[:, 0:chans] = unpack(chalo, 1)

    @pl.when(parity == 1)
    def _():
        cote[:, chans - skip : 2 * chans - skip] = unpack(chalo, 0)

    place(outer_dot(hb[...], cote[...]), early, n_early)
    core_e = [core_send(e, side, early, n_early) for e, side in enumerate((1 - yc, yc))]
    core_e[0].wait_recv()
    y_e = y_send(4, early, n_early)

    far_recv(0, chalo)
    cotl[:, 0:chans] = unpack(chalo, parity)
    place(outer_dot(hb[...], cotl[...]), late, n_late)
    core_l = [core_send(2 + e, side, late, n_late) for e, side in enumerate((1 - yc, yc))]

    y_tail.wait_recv()
    r_tail = wsend(16, tail_part(ypart), at_core)
    y_last.wait_recv()
    r_last = wsend(17, wp.at[ypart, 5], at_core)
    pass_hidden(0)
    core_l[0].wait_recv()
    y_l = y_send(5, late, n_late)

    for copy in (own_last, r_tail, r_last):
        copy.wait_recv()
    for owner in range(n_clip):
        unpack_pair(owner, 4, (1,))
        unpack_pair(owner, 5)
    grad_h = transpose_dot(unpack(chalo, 1), wg[9])
    grad_h = grad_h + transpose_dot(cot[...].astype(BF16), wg[10])
    grad_h = grad_h + transpose_dot(unpack(chalo, 0), wg[11])
    acc = spat[...]
    sig = jax.nn.sigmoid(acc)
    grad_s = grad_h * (sig * (1.0 + acc * (1.0 - sig)))
    for b in range(3):
        gpad[b, width : width + rows] = shifted(grad_s, b - 1).astype(BF16)

    for r in range(2, rounds):
        gate_step(r)
    core_e[1].wait_recv()
    y_e.wait_recv()
    scatter(early, n_early)

    def grad_conv(q):
        acc = cot[q * half : (q + 1) * half]
        for a in range(3):
            start = (2 - a) * width + q * half
            for b in range(3):
                acc = acc + transpose_dot(gpad[b, start : start + half], wg[3 * a + b])
        gv_v[q * half : (q + 1) * half] = acc

    core_l[1].wait_recv()
    y_l.wait_recv()
    scatter(late, n_late)
    grad_conv(0)
    pass_hidden(1)
    grad_conv(1)
    for e in range(2):
        forward(2 * chunks, hid_stash[e], hhalo, 2 + e)
    out_v[...] = video[...] + nn_dot(hb[...], wg[10])

    @pl.when(owns)
    def _():
        mine_at = tm - first_owner
        rs[tm] = jnp.zeros(rs.shape[1:], BF16)
        for sender in range(n_tm):
            @pl.when(tm != sender)
            def _():
                for e in range(share):
                    arrival(sender, e).wait_recv()
        for e in range(share):
            total = psum[mine_at * share + e]
            for sender in range(n_tm):
                total = total + rs[sender, e].astype(F32)
            ag[mine_at * share + e] = total.astype(BF16)
        for to in (0, 1, n_tm - 2, n_tm - 1, *range(2, n_tm - 2)):
            @pl.when(tm != to)
            def _():
                gather_copy(mine_at, to).start()

    far_recv(2 * chunks, hhalo)
    hid_near[2].wait_recv()
    hid_near[3].wait_recv()
    out_v[...] = out_v[...] + nn_dot(unpack(hhalo, 0), wg[9]) + nn_dot(unpack(hhalo, 1), wg[11])

    for owner in range(4):
        @pl.when(tm != first_owner + owner)
        def _():
            gather_copy(owner, tm).wait_recv()
    whole = jnp.concatenate([ag[to] for to in range(n_tm)], axis=1).astype(F32) * scale
    for k in range(3):
        gt_v[k] = whole[:, k * chans : (k + 1) * chans]

    for copy in w_copies + cot_near + hid_near + core_e + core_l + [y_e, y_l]:
        copy.wait_send()

    @pl.when(sends_far)
    def _():
        for q in range(2):
            far_copy(0, chalo, q).wait_send()
        for q in range(2, chunks):
            forward_copy(0, cstash, chalo, q).wait_send()
        for q in range(2):
            far_copy(2 * chunks, hhalo, q).wait_send()
        for q in range(2, chunks):
            forward_copy(2 * chunks, hstash, hhalo, q).wait_send()

    @pl.when(gets_far)
    def _():
        for e in range(2):
            stash_copy(*cot_stash[e], 2 + e).wait_send()
        for e in range(2):
            stash_copy(*hid_stash[e], 2 + e).wait_send()

    for unit in range(n_tm):
        @pl.when(tm != first_owner + unit // share)
        def _():
            scatter_copy(unit).wait_send()

    @pl.when(owns)
    def _():
        for to in range(n_tm):
            @pl.when(tm != to)
            def _():
                gather_copy(tm - first_owner, to).wait_send()


def hand_over(*refs):
    n = len(refs) // 2
    ins, outs, sem = refs[:n], refs[n : 2 * n], refs[2 * n]
    writes = []
    for e in range(n):
        extent = ins[e].shape[0]
        count = 4 if extent % 64 == 0 else 1
        for q in range(count):
            part = pl.ds(q * (extent // count), extent // count)
            writes.append(pltpu.make_async_copy(ins[e].at[part], outs[e].at[part], sem.at[4 * e + q]))
    for write in writes:
        write.start()
    for write in writes:
        write.wait()


def fused(n_tm, n_clip, video, spatial_w, spatial_b, temporal_w, cotangent):
    clips, frames, height, width, chans = video.shape
    rows = height * width
    depth = spatial_w.shape[1]
    lanes = -(-3 * chans // (128 * n_tm)) * 128
    scale = 1.0 / math.sqrt(rows * n_tm * n_clip)
    any_spec = pl.BlockSpec(memory_space=pltpu.HBM)
    vm_spec = pl.BlockSpec(memory_space=pltpu.VMEM)
    vm = pltpu.VMEM
    dma = pltpu.SemaphoreType.DMA
    results = pl.pallas_call(
        functools.partial(block_kernel, (n_tm, n_clip, height, width, chans, scale)),
        out_shape=(
            vm((rows, chans), F32),
            vm((rows, chans), F32),
            vm((3, depth, chans), F32),
        ),
        in_specs=[any_spec, any_spec, any_spec, any_spec, any_spec],
        out_specs=(vm_spec, vm_spec, vm_spec),
        scratch_shapes=[
            vm((rows, chans), F32),
            vm((rows, chans), F32),
            vm((9, depth, chans), BF16),
            vm((3, depth, chans), F32),
            vm((chans,), F32),
            vm((n_clip, 6, depth, 2 * chans), BF16),
            vm((12, chans, chans), BF16),
            vm((2, rows + 2 * width, 3 * chans // 2), BF16),
            vm((rows // 2, 2 * chans), BF16),
            vm((2, rows // 2, 2 * chans), BF16),
            vm((rows, 2 * chans), BF16),
            vm((rows, n_tm * lanes - 2 * chans), BF16),
            vm((rows, chans), BF16),
            vm((rows // 2, 2 * chans), BF16),
            vm((rows // 2, 2 * chans), BF16),
            vm((2, rows // 2, 2 * chans), BF16),
            vm((rows // 2, 2 * chans), BF16),
            vm((rows, chans), F32),
            vm((3, rows + 2 * width, chans), BF16),
            vm((2, 2, n_tm, depth, lanes), F32),
            vm((2, n_tm, depth, lanes), F32),
            vm((n_tm, depth, lanes), BF16),
            vm((n_tm, depth, lanes), BF16),
            vm((n_tm, depth, lanes), F32),
            vm((n_tm, depth, lanes), BF16),
            vm((n_tm, n_tm // 4, depth, lanes), BF16),
            vm((n_tm, depth, lanes), BF16),
            dma((7,)),
            dma((18,)),
            dma((18,)),
            dma((20,)),
            dma((20,)),
            dma((6,)),
            dma((6,)),
            dma((2 * n_tm,)),
            dma((n_tm * (n_tm // 4) + 4,)),
            pltpu.SemaphoreType.REGULAR((n_tm // 2 - 1,)),
        ],
        compiler_params=pltpu.CompilerParams(
            collective_id=0, has_side_effects=True, vmem_limit_bytes=65_000_000
        ),
        name="block",
    )(
        video.reshape(rows, chans), spatial_w, spatial_b, temporal_w,
        cotangent.reshape(rows, chans),
    )
    shapes = tuple(jax.ShapeDtypeStruct(array.shape, F32) for array in results)

    out, gv, gt = pl.pallas_call(
        hand_over,
        out_shape=shapes,
        in_specs=[vm_spec] * 3,
        out_specs=(any_spec,) * 3,
        scratch_shapes=[dma((12,))],
        compiler_params=pltpu.CompilerParams(vmem_limit_bytes=2**20),
        name="hand_over",
    )(*results)
    return out.reshape(video.shape), gv.reshape(video.shape), gt


def padded_2(cells, sides, width):
    for axis, dim in sides:
        count = lax.axis_size(axis)
        ends = count - 1
        head = lax.slice_in_dim(cells, 0, width, axis=dim)
        tail = lax.slice_in_dim(cells, cells.shape[dim] - width, cells.shape[dim], axis=dim)
        cells = jnp.concatenate(
            [
                lax.ppermute(tail, axis, [(i, (i + 1) % count) for i in range(ends)]),
                cells,
                lax.ppermute(head, axis, [((i + 1) % count, i) for i in range(ends)]),
            ],
            axis=dim,
        )
    return cells


def native(video, spatial_w, spatial_b, temporal_w, cotangent):
    clips, frames, height, width, chans = video.shape
    row_count = clips * frames * height * width
    pads = ((0, 0), (0, 0), (1, 1), (1, 1), (0, 0))
    padded = jnp.pad(video.astype(BF16), pads)
    temporal_b = temporal_w.astype(BF16)
    spatial_all = lax.all_gather(spatial_w, "clip", axis=1, tiled=True)
    temporal_all = lax.all_gather(temporal_b, "clip", axis=1, tiled=True)
    spatial = jnp.zeros((row_count, chans), F32)
    for y in range(3):
        for x in range(3):
            window = padded[:, :, y : y + height, x : x + width, :].reshape(row_count, chans)
            spatial = spatial + nn_dot(window, spatial_all[3 * y + x])
    spatial = spatial + spatial_b
    sigmoid_s = jax.nn.sigmoid(spatial)
    hidden = (spatial * sigmoid_s).astype(BF16).reshape(video.shape)
    hidden_pad = padded_2(hidden, (("tm", 1),), 1)
    cot_b = cotangent.astype(BF16)
    cot_flat = cot_b.reshape(row_count, chans)
    cot_pad = padded_2(cot_b, (("tm", 1),), 1)
    temporal = jnp.zeros((row_count, chans), F32)
    grad_hidden = jnp.zeros((row_count, chans), F32)
    grads = []
    for k in range(3):
        shifted_hid = hidden_pad[:, k : k + frames].reshape(row_count, chans)
        temporal = temporal + nn_dot(shifted_hid, temporal_all[k])
        shifted_cot = cot_pad[:, 2 - k : 2 - k + frames].reshape(row_count, chans)
        grad_hidden = grad_hidden + transpose_dot(shifted_cot, temporal_all[k])
        grads.append(outer_dot(shifted_hid, cot_flat))
    total_rows = row_count * lax.axis_size("tm") * lax.axis_size("clip")
    summed = lax.psum(jnp.stack(grads), "tm")
    owned = lax.psum_scatter(summed, "clip", scatter_dimension=1, tiled=True)
    grad_spatial = (grad_hidden * sigmoid_s * (1.0 + spatial * (1.0 - sigmoid_s))).astype(BF16)
    grad_frames = jnp.pad(grad_spatial.reshape(video.shape), pads)
    grad_acc = cotangent.reshape(row_count, chans)
    for y in range(3):
        for x in range(3):
            window = grad_frames[:, :, 2 - y : 2 - y + height, 2 - x : 2 - x + width, :]
            window = window.reshape(row_count, chans)
            grad_acc = grad_acc + transpose_dot(window, spatial_all[3 * y + x])
    return (
        video + temporal.reshape(video.shape),
        grad_acc.reshape(video.shape),
        owned * (1.0 / math.sqrt(total_rows)),
    )


def solution(mesh):
    n_tm, n_clip = mesh.shape["tm"], mesh.shape["clip"]

    def on_device(video, spatial_w, spatial_b, temporal_w, cotangent):
        args = (video, spatial_w, spatial_b, temporal_w, cotangent)
        one_frame = video.shape[0] == 1 and video.shape[1] == 1
        depth, chans = spatial_w.shape[1:]
        lanes = -(-3 * chans // (128 * n_tm)) * 128
        fits = depth % 16 == 0 and depth > 16 * TAIL and 2 * chans % lanes == 0
        if one_frame and fits and n_clip == 4 and n_tm % 4 == 0 and n_tm * lanes <= 4 * chans:
            return fused(n_tm, n_clip, *args)
        return native(*args)

    return jax.shard_map(
        on_device,
        mesh=mesh,
        in_specs=(
            P("clip", "tm", None, None, None),
            P(None, "clip", None),
            P(),
            P(None, "clip", None),
            P("clip", "tm", None, None, None),
        ),
        out_specs=(
            P("clip", "tm", None, None, None),
            P("clip", "tm", None, None, None),
            P(None, "clip", None),
        ),
        check_vma=False,
    )
```

```python
import functools
import math

import jax
import jax.numpy as jnp
from jax import lax
from jax.experimental import pallas as pl
from jax.experimental.pallas import tpu as pltpu
from jax.sharding import PartitionSpec as P

F32 = jnp.float32
BF16 = jnp.bfloat16
MESH = pl.DeviceIdType.MESH


def nn_dot(left, right):
    return lax.dot_general(left, right, (((1,), (0,)), ((), ())), preferred_element_type=F32)


def outer_dot(left, right):
    return lax.dot_general(left, right, (((0,), (0,)), ((), ())), preferred_element_type=F32)


def transpose_dot(left, right):
    return lax.dot_general(left, right, (((1,), (1,)), ((), ())), preferred_element_type=F32)


TAIL = 2


def own_cot_of(ref):
    return ref[...].astype(BF16)


def block_kernel(
    dims,
    video_h, sw_h, bias_h, tw_h, cot_h,
    out_v, gv_v, gt_v,
    video, cot, sw, tw, bias_ref, wp, wg, xcat, cb, chalo, cote, cotl, hb, cstash, hpack, hhalo, hstash, spat, gpad,
    gtl, rx, ysend, ry, psum, pb, rs, ag,
    load_sem, w_send, w_recv, halo_send, halo_recv, g_send, g_recv, a_send, a_recv, gate,
):
    n_tm, n_clip, height, width, chans, scale = dims
    rows = height * width
    depth = sw_h.shape[1]
    half = rows // 2
    quarter = rows // 4
    side_chans = chans // 2
    chunks = 4
    chunk = half // chunks
    low = depth - 16 * TAIL
    head = -(-chans // 128) * 128
    lanes = psum.shape[2]
    n_early = 2 * chans // lanes
    n_late = n_tm - n_early
    skip = n_late * lanes - chans
    tm = lax.axis_index("tm")
    c = lax.axis_index("clip")

    def flip(value, bit):
        return value + bit - 2 * bit * (lax.rem(value // bit, 2))

    core, ypart = flip(c, 1), flip(c, 2)
    xpart, zpart = flip(tm, 1), flip(tm, 2)
    parity = lax.rem(tm, 2)
    h = lax.rem(tm // 2, 2)
    yc = c // 2
    mine = lax.rem(c, 2)
    has_up, has_down = tm + 2 < n_tm, tm >= 2

    def signal(sem, device):
        pl.semaphore_signal(sem, inc=1, device_id=device, device_id_type=MESH)

    def tm_signals(sem):
        signal(sem, (xpart, c))

        @pl.when(has_up)
        def _():
            signal(sem, (tm + 2, c))

        @pl.when(has_down)
        def _():
            signal(sem, (tm - 2, c))

    def tm_waits(sem, extra):
        n_z, z = n_tm // 2, tm // 2
        ups, downs = (2 * n_z - 2 - z) // n_z, (z + n_z - 1) // n_z
        pl.semaphore_wait(sem, 1 + extra + ups + downs)

    rounds = n_tm // 2 - 1

    def gate_step(r):
        if r < rounds:
            tm_waits(gate.at[r], 0)
        if r + 1 < rounds:
            tm_signals(gate.at[r + 1])

    barrier = pltpu.get_barrier_semaphore()
    signal(barrier, (tm, ypart))
    signal(barrier, (tm, core))
    tm_signals(barrier)

    loads = [
        pltpu.make_async_copy(sw_h.at[pl.ds(0, 4)], sw.at[pl.ds(0, 4)], load_sem.at[0]),
        pltpu.make_async_copy(sw_h.at[pl.ds(4, 4)], sw.at[pl.ds(4, 4)], load_sem.at[0]),
        pltpu.make_async_copy(sw_h.at[pl.ds(8, 1)], sw.at[pl.ds(8, 1)], load_sem.at[5]),
        pltpu.make_async_copy(tw_h, tw, load_sem.at[1]),
        pltpu.make_async_copy(cot_h, cot, load_sem.at[2]),
        pltpu.make_async_copy(video_h, video, load_sem.at[3]),
        pltpu.make_async_copy(bias_h, bias_ref, load_sem.at[4]),
    ]
    for load in loads:
        load.start()

    def pack(value):
        return jnp.concatenate([value[:quarter], value[quarter:]], axis=1)

    def unpack(ref, slot):
        parts = []
        for q in range(2):
            both = ref[slot, q * quarter : (q + 1) * quarter]
            parts += [both[:, :chans], both[:, chans:]]
        return jnp.concatenate(parts, axis=0)

    pltpu.make_async_copy(sw_h.at[pl.ds(0, 8)], sw.at[pl.ds(0, 8)], load_sem.at[0]).wait()
    for pair in range(4):
        wp[c, pair] = jnp.concatenate([sw[2 * pair], sw[2 * pair + 1]], axis=1)
    tm_waits(barrier, 2)

    def send(src, dst, ssem, rsem, device):
        copy = pltpu.make_async_remote_copy(
            src_ref=src, dst_ref=dst, send_sem=ssem, recv_sem=rsem,
            device_id=device, device_id_type=MESH,
        )
        copy.start()
        return copy

    def settle(ref, ssem, rsem):
        return pltpu.make_async_remote_copy(
            src_ref=ref, dst_ref=ref, send_sem=ssem, recv_sem=rsem,
            device_id=(tm, core), device_id_type=MESH,
        )

    def sent(ref, sem):
        settle(ref, sem, sem).wait_send()

    def received(ref, sem):
        settle(ref, sem, sem).wait_recv()

    def block_rows(count):
        return chalo.at[0, pl.ds(0, count)]

    def wsend(slot, part, device):
        return send(part, part, w_send.at[0], w_recv.at[slot], device)

    def low_part(owner, pair):
        return wp.at[owner, pair, pl.ds(0, low)]

    def rest_part(owner):
        return wp.at[owner, pl.ds(0, 4), pl.ds(low, depth - low)]

    def head_part(owner):
        return wp.at[owner, 4, :, pl.ds(0, head)]

    def tail_part(owner):
        return wp.at[owner, 4, :, pl.ds(head, 2 * chans - head)]

    at_y, at_core, at_x, at_z = (tm, ypart), (tm, core), (xpart, c), (zpart, c)
    y_a = wsend(0, low_part(c, h), at_y)
    y_b = wsend(1, low_part(c, 2 + h), at_y)
    y_rest = wsend(2, rest_part(c), at_y)
    for load in loads[2:4]:
        load.wait()
    first = tw[0].astype(BF16)
    wp[c, 4] = jnp.concatenate([sw[8], first], axis=1)
    wp[c, 5] = jnp.concatenate([tw[1].astype(BF16), tw[2].astype(BF16)], axis=1)
    y_head = wsend(3, head_part(c), at_y)
    own = wsend(8, wp.at[c, pl.ds(0, 5)], at_core)
    tm_signals(gate.at[0])

    loads[4].wait()
    own_cot = cot[...].astype(BF16)
    for q in range(2):
        cb[q * quarter : (q + 1) * quarter] = pack(own_cot[q * half : (q + 1) * half])

    def near_send(which, own_ref, halo, q):
        part = pl.ds(q * chunk, chunk)
        return send(
            own_ref.at[part, :], halo.at[parity, part, :],
            halo_send.at[which], halo_recv.at[3 * which + min(q, 2)], (xpart, c),
        )

    def far_copy(which, halo, q):
        target = lax.rem(tm + n_tm + 2 - 4 * parity, n_tm)
        part = pl.ds(q * chunk, chunk)
        return pltpu.make_async_remote_copy(
            src_ref=halo.at[1 - parity, part, :],
            dst_ref=halo.at[parity, part, :],
            send_sem=halo_send.at[2],
            recv_sem=halo_recv.at[6 + which],
            device_id=(target, c),
            device_id_type=MESH,
        )

    sends_far = jnp.logical_or(
        jnp.logical_and(parity == 0, has_up), jnp.logical_and(parity == 1, has_down)
    )
    gets_far = jnp.logical_or(
        jnp.logical_and(parity == 0, has_down), jnp.logical_and(parity == 1, has_up)
    )

    def far_start(which, halo, q):
        @pl.when(sends_far)
        def _():
            far_copy(which, halo, q).start()

    def far_recv(which):
        @pl.when(gets_far)
        def _():
            received(block_rows(half), halo_recv.at[6 + which])

    def stash_start(which, own_ref, held):
        @pl.when(gets_far)
        def _():
            for q in range(2, chunks):
                part = pl.ds(q * chunk, chunk)
                pltpu.make_async_remote_copy(
                    src_ref=own_ref.at[part, :], dst_ref=held.at[part, :],
                    send_sem=halo_send.at[3], recv_sem=halo_recv.at[8 + which],
                    device_id=(lax.rem(tm + n_tm + 4 * parity - 2, n_tm), c), device_id_type=MESH,
                ).start()

    def forward(which, held, halo):
        @pl.when(sends_far)
        def _():
            received(block_rows(2 * chunk), halo_recv.at[8 + which])
            for q in range(2, chunks):
                part = pl.ds(q * chunk, chunk)
                pltpu.make_async_remote_copy(
                    src_ref=held.at[part, :], dst_ref=halo.at[1 - parity, part, :],
                    send_sem=halo_send.at[2], recv_sem=halo_recv.at[6 + which],
                    device_id=at_x, device_id_type=MESH,
                ).start()

    cot_near = [near_send(0, cb, chalo, q) for q in range(chunks)]
    stash_start(0, cb, cstash)

    for edge, slot in ((0, 0), (n_tm - 1, 1)):
        @pl.when(tm == edge)
        def _():
            chalo[slot] = jnp.zeros((half, 2 * chans), BF16)
            hhalo[slot] = jnp.zeros((half, 2 * chans), BF16)

    column = lax.rem(lax.broadcasted_iota(jnp.int32, (rows, chans), 0), width)

    def shifted(value, step):
        if step == 0:
            return value
        rolled = pltpu.roll(value, step % rows, 0)
        return jnp.where(column == (0 if step == 1 else width - 1), 0.0, rolled)

    for s in range(2):
        xcat[s, 0:width] = jnp.zeros((width, 3 * side_chans), BF16)
        xcat[s, width + rows :] = jnp.zeros((width, 3 * side_chans), BF16)
    for b in range(3):
        gpad[b, 0:width] = jnp.zeros((width, chans), BF16)
        gpad[b, width + rows :] = jnp.zeros((width, chans), BF16)
    loads[5].wait()
    loads[6].wait()
    frame = video[...]
    views = [shifted(frame, 1 - b).astype(BF16) for b in range(3)]
    for s in range(2):
        xcat[s, width : width + rows] = jnp.concatenate(
            [view[:, s * side_chans : (s + 1) * side_chans] for view in views], axis=1
        )

    def unpack_pair(owner, pair, taps=(0, 1)):
        both = wp[owner, pair] if 1 in taps else wp[owner, pair, :, 0:head]
        band = pl.ds(pl.multiple_of(owner * depth, 16), depth)
        for e in taps:
            wg[2 * pair + e, band] = both[:, e * chans : (e + 1) * chans]

    def unpack_spatial(owner, first=0, count=5):
        for pair in range(first, first + count):
            unpack_pair(owner, pair, (0, 1) if pair < 4 else (0,))

    def conv_part(s, q, taps=(0, 1, 2)):
        total = None
        for a in taps:
            band = pl.ds(pl.multiple_of(s * side_chans, 16), side_chans)
            weights = jnp.concatenate([wg[3 * a + b, band] for b in range(3)], axis=0)
            term = nn_dot(
                xcat[s, a * width + q * half : a * width + (q + 1) * half], weights
            )
            total = term if total is None else total + term
        return total

    unpack_spatial(c)

    @pl.when(parity == 0)
    def _():
        cote[:, chans : 2 * chans] = own_cot_of(cot)
        cotl[:, chans:] = jnp.zeros((rows, skip), BF16)

    @pl.when(parity == 1)
    def _():
        middle = own_cot_of(cot)
        cote[:, 0 : chans - skip] = middle[:, skip:]
        cote[:, 2 * chans - skip :] = jnp.zeros((rows, skip), BF16)
        cotl[:, chans:] = middle[:, :skip]

    own.wait_recv()
    unpack_spatial(core)
    for q in range(2):
        spat[q * half : (q + 1) * half] = bias_ref[...].reshape(1, chans) + conv_part(yc, q)

    y_a.wait_recv()
    z_a = wsend(6, low_part(ypart, h), at_z)
    wsend(9, low_part(ypart, h), at_core)
    y_b.wait_recv()
    z_b = wsend(7, low_part(ypart, 2 + h), at_z)
    wsend(10, low_part(ypart, 2 + h), at_core)
    gate_step(0)
    y_rest.wait_recv()
    wsend(9, rest_part(ypart), at_core)
    z_a.wait_recv()
    wsend(9, low_part(ypart, 1 - h), at_core)
    gate_step(1)
    y_head.wait_recv()
    wsend(10, head_part(ypart), at_core)
    y_tail = wsend(4, tail_part(c), at_y)
    y_last = wsend(5, wp.at[c, 5], at_y)
    for q in range(2):
        cot_near[q].wait_recv()
        far_start(0, chalo, q)
    z_b.wait_recv()
    wsend(10, low_part(ypart, 3 - h), at_core)
    forward(0, cstash, chalo)
    diagonal = flip(core, 2)
    unpack_spatial(ypart)
    received(block_rows(4 * depth - 2 * low), w_recv.at[9])
    unpack_spatial(diagonal, 0, 2)
    for q in range(2):
        part = pl.ds(q * half, half)
        spat[part] = spat[part] + conv_part(1 - yc, q, (0,))
    head_rows = depth * head // (2 * chans)
    received(block_rows(2 * low + head_rows), w_recv.at[10])
    wsend(11, wp.at[c, 5], at_core)
    unpack_spatial(diagonal, 2, 3)

    hid_near = []
    for q in range(2):
        acc = spat[q * half : (q + 1) * half] + conv_part(1 - yc, q, (1, 2))
        hidden = (acc * jax.nn.sigmoid(acc)).astype(BF16)
        hb[q * half : (q + 1) * half] = hidden
        hpack[q * quarter : (q + 1) * quarter] = pack(hidden)
        hid_near += [near_send(1, hpack, hhalo, 2 * q + e) for e in range(2)]
        if q == 1:
            stash_start(1, hpack, hstash)
        spat[q * half : (q + 1) * half] = acc
    received(block_rows(2 * chunk), halo_recv.at[2])

    early = (n_tm - n_early) * parity
    late = n_early * (1 - parity)

    def place(products, first, count):
        for i in range(count):
            for owner in range(n_clip):
                gtl[owner % 2, owner // 2, first + i] = products[
                    owner * depth : (owner + 1) * depth, i * lanes : (i + 1) * lanes
                ]

    def core_send(slot, side, first, count):
        part = pl.ds(first, count)
        return send(
            gtl.at[1 - mine, side, part], rx.at[side, part],
            g_send.at[0], g_recv.at[slot], at_core,
        )

    def y_send(slot, first, count):
        for i in range(count):
            ysend[first + i] = (gtl[mine, 1 - yc, first + i] + rx[1 - yc, first + i]).astype(BF16)
        part = pl.ds(first, count)
        return send(ysend.at[part], ry.at[part], g_send.at[1], g_recv.at[slot], at_y)

    share = n_tm // 4
    first_owner = n_tm // 2 - 2
    owns = jnp.logical_and(tm >= first_owner, tm < first_owner + 4)

    def scatter_copy(unit):
        place_in = lax.rem(unit, share)
        return pltpu.make_async_remote_copy(
            src_ref=pb.at[unit], dst_ref=rs.at[tm, place_in],
            send_sem=a_send.at[0], recv_sem=a_recv.at[0],
            device_id=(first_owner + unit // share, c), device_id_type=MESH,
        )

    def gather_copy(owner, to):
        part = ag.at[pl.ds(owner * share, share)]
        return pltpu.make_async_remote_copy(
            src_ref=part, dst_ref=part,
            send_sem=a_send.at[1], recv_sem=a_recv.at[1],
            device_id=(to, c), device_id_type=MESH,
        )

    def scatter(first, count):
        for i in range(count):
            to = first + i
            part = gtl[mine, yc, to] + rx[yc, to] + ry[to].astype(F32)
            psum[to] = part
            pb[to] = part.astype(BF16)

            @pl.when(tm != first_owner + to // share)
            def _():
                scatter_copy(to).start()

    def pass_hidden(q):
        hid_near[q].wait_recv()
        far_start(1, hhalo, q)

    @pl.when(parity == 0)
    def _():
        cote[:, 0:chans] = unpack(chalo, 1)

    @pl.when(parity == 1)
    def _():
        cote[:, chans - skip : 2 * chans - skip] = unpack(chalo, 0)

    place(outer_dot(hb[...], cote[...]), early, n_early)
    core_e = [core_send(e, side, early, n_early) for e, side in enumerate((1 - yc, yc))]
    core_e[0].wait_recv()
    y_e = y_send(4, early, n_early)

    far_recv(0)
    cotl[:, 0:chans] = unpack(chalo, parity)
    place(outer_dot(hb[...], cotl[...]), late, n_late)
    core_l = [core_send(2 + e, side, late, n_late) for e, side in enumerate((1 - yc, yc))]

    y_tail.wait_recv()
    wsend(11, tail_part(ypart), at_core)
    y_last.wait_recv()
    wsend(11, wp.at[ypart, 5], at_core)
    pass_hidden(0)
    core_l[0].wait_recv()
    y_l = y_send(5, late, n_late)

    received(block_rows(3 * depth - head_rows), w_recv.at[11])
    for owner in range(n_clip):
        unpack_pair(owner, 4, (1,))
        unpack_pair(owner, 5)
    grad_h = transpose_dot(unpack(chalo, 1), wg[9])
    grad_h = grad_h + transpose_dot(cot[...].astype(BF16), wg[10])
    grad_h = grad_h + transpose_dot(unpack(chalo, 0), wg[11])
    acc = spat[...]
    sig = jax.nn.sigmoid(acc)
    grad_s = grad_h * (sig * (1.0 + acc * (1.0 - sig)))
    for b in range(3):
        gpad[b, width : width + rows] = shifted(grad_s, b - 1).astype(BF16)

    for r in range(2, rounds):
        gate_step(r)
    core_e[1].wait_recv()
    y_e.wait_recv()
    scatter(early, n_early)

    def grad_conv(q):
        acc = cot[q * half : (q + 1) * half]
        for a in range(3):
            start = (2 - a) * width + q * half
            for b in range(3):
                acc = acc + transpose_dot(gpad[b, start : start + half], wg[3 * a + b])
        gv_v[q * half : (q + 1) * half] = acc

    core_l[1].wait_recv()
    y_l.wait_recv()
    scatter(late, n_late)
    grad_conv(0)
    pass_hidden(1)
    grad_conv(1)
    forward(1, hstash, hhalo)
    out_v[...] = video[...] + nn_dot(hb[...], wg[10])

    @pl.when(owns)
    def _():
        mine_at = tm - first_owner
        rs[tm] = jnp.zeros(rs.shape[1:], BF16)
        received(rs.at[pl.ds(0, n_tm - 1)], a_recv.at[0])
        for e in range(share):
            total = psum[mine_at * share + e]
            for sender in range(n_tm):
                total = total + rs[sender, e].astype(F32)
            ag[mine_at * share + e] = total.astype(BF16)
        for to in (0, 1, n_tm - 2, n_tm - 1, *range(2, n_tm - 2)):
            @pl.when(tm != to)
            def _():
                gather_copy(mine_at, to).start()

    far_recv(1)
    received(block_rows(2 * chunk), halo_recv.at[5])
    out_v[...] = out_v[...] + nn_dot(unpack(hhalo, 0), wg[9]) + nn_dot(unpack(hhalo, 1), wg[11])

    @pl.when(owns)
    def _():
        received(ag.at[pl.ds(0, 3 * share)], a_recv.at[1])

    @pl.when(jnp.logical_not(owns))
    def _():
        received(ag, a_recv.at[1])

    whole = jnp.concatenate([ag[to] for to in range(n_tm)], axis=1).astype(F32) * scale
    for k in range(3):
        gt_v[k] = whole[:, k * chans : (k + 1) * chans]

    sent(wp.at[pl.ds(0, 3)], w_send.at[0])
    sent(block_rows(half), halo_send.at[0])
    sent(block_rows(half), halo_send.at[1])
    sent(gtl.at[0], g_send.at[0])
    sent(ysend, g_send.at[1])

    @pl.when(sends_far)
    def _():
        sent(chalo, halo_send.at[2])

    @pl.when(gets_far)
    def _():
        sent(block_rows(half), halo_send.at[3])

    @pl.when(owns)
    def _():
        sent(pb.at[pl.ds(0, n_tm - share)], a_send.at[0])
        sent(rs.at[pl.ds(0, n_tm - 1)], a_send.at[1])

    @pl.when(jnp.logical_not(owns))
    def _():
        sent(pb, a_send.at[0])


def hand_over(*refs):
    n = len(refs) // 2
    ins, outs, sem = refs[:n], refs[n : 2 * n], refs[2 * n]
    writes = []
    for e in range(n):
        writes.append(pltpu.make_async_copy(ins[e], outs[e], sem.at[e]))
    for write in writes:
        write.start()
    for write in writes:
        write.wait()


def fused(n_tm, n_clip, video, spatial_w, spatial_b, temporal_w, cotangent):
    clips, frames, height, width, chans = video.shape
    rows = height * width
    depth = spatial_w.shape[1]
    lanes = -(-3 * chans // (128 * n_tm)) * 128
    scale = 1.0 / math.sqrt(rows * n_tm * n_clip)
    any_spec = pl.BlockSpec(memory_space=pltpu.HBM)
    vm_spec = pl.BlockSpec(memory_space=pltpu.VMEM)
    vm = pltpu.VMEM
    dma = pltpu.SemaphoreType.DMA
    results = pl.pallas_call(
        functools.partial(block_kernel, (n_tm, n_clip, height, width, chans, scale)),
        out_shape=(
            vm((rows, chans), F32),
            vm((rows, chans), F32),
            vm((3, depth, chans), F32),
        ),
        in_specs=[any_spec, any_spec, any_spec, any_spec, any_spec],
        out_specs=(vm_spec, vm_spec, vm_spec),
        scratch_shapes=[
            vm((rows, chans), F32),
            vm((rows, chans), F32),
            vm((9, depth, chans), BF16),
            vm((3, depth, chans), F32),
            vm((chans,), F32),
            vm((n_clip, 6, depth, 2 * chans), BF16),
            vm((12, chans, chans), BF16),
            vm((2, rows + 2 * width, 3 * chans // 2), BF16),
            vm((rows // 2, 2 * chans), BF16),
            vm((2, rows // 2, 2 * chans), BF16),
            vm((rows, 2 * chans), BF16),
            vm((rows, n_tm * lanes - 2 * chans), BF16),
            vm((rows, chans), BF16),
            vm((rows // 2, 2 * chans), BF16),
            vm((rows // 2, 2 * chans), BF16),
            vm((2, rows // 2, 2 * chans), BF16),
            vm((rows // 2, 2 * chans), BF16),
            vm((rows, chans), F32),
            vm((3, rows + 2 * width, chans), BF16),
            vm((2, 2, n_tm, depth, lanes), F32),
            vm((2, n_tm, depth, lanes), F32),
            vm((n_tm, depth, lanes), BF16),
            vm((n_tm, depth, lanes), BF16),
            vm((n_tm, depth, lanes), F32),
            vm((n_tm, depth, lanes), BF16),
            vm((n_tm, n_tm // 4, depth, lanes), BF16),
            vm((n_tm, depth, lanes), BF16),
            dma((6,)),
            dma((1,)),
            dma((12,)),
            dma((4,)),
            dma((10,)),
            dma((2,)),
            dma((6,)),
            dma((2,)),
            dma((2,)),
            pltpu.SemaphoreType.REGULAR((n_tm // 2 - 1,)),
        ],
        compiler_params=pltpu.CompilerParams(
            collective_id=0, has_side_effects=True, vmem_limit_bytes=65_000_000
        ),
        name="block",
    )(
        video.reshape(rows, chans), spatial_w, spatial_b, temporal_w,
        cotangent.reshape(rows, chans),
    )
    shapes = tuple(jax.ShapeDtypeStruct(array.shape, F32) for array in results)

    out, gv, gt = pl.pallas_call(
        hand_over,
        out_shape=shapes,
        in_specs=[vm_spec] * 3,
        out_specs=(any_spec,) * 3,
        scratch_shapes=[dma((3,))],
        compiler_params=pltpu.CompilerParams(vmem_limit_bytes=2**20),
        name="hand_over",
    )(*results)
    return out.reshape(video.shape), gv.reshape(video.shape), gt


def padded_2(cells, sides, width):
    for axis, dim in sides:
        count = lax.axis_size(axis)
        ends = count - 1
        head = lax.slice_in_dim(cells, 0, width, axis=dim)
        tail = lax.slice_in_dim(cells, cells.shape[dim] - width, cells.shape[dim], axis=dim)
        cells = jnp.concatenate(
            [
                lax.ppermute(tail, axis, [(i, (i + 1) % count) for i in range(ends)]),
                cells,
                lax.ppermute(head, axis, [((i + 1) % count, i) for i in range(ends)]),
            ],
            axis=dim,
        )
    return cells


def native(video, spatial_w, spatial_b, temporal_w, cotangent):
    clips, frames, height, width, chans = video.shape
    row_count = clips * frames * height * width
    pads = ((0, 0), (0, 0), (1, 1), (1, 1), (0, 0))
    padded = jnp.pad(video.astype(BF16), pads)
    temporal_b = temporal_w.astype(BF16)
    spatial_all = lax.all_gather(spatial_w, "clip", axis=1, tiled=True)
    temporal_all = lax.all_gather(temporal_b, "clip", axis=1, tiled=True)
    spatial = jnp.zeros((row_count, chans), F32)
    for y in range(3):
        for x in range(3):
            window = padded[:, :, y : y + height, x : x + width, :].reshape(row_count, chans)
            spatial = spatial + nn_dot(window, spatial_all[3 * y + x])
    spatial = spatial + spatial_b
    sigmoid_s = jax.nn.sigmoid(spatial)
    hidden = (spatial * sigmoid_s).astype(BF16).reshape(video.shape)
    hidden_pad = padded_2(hidden, (("tm", 1),), 1)
    cot_b = cotangent.astype(BF16)
    cot_flat = cot_b.reshape(row_count, chans)
    cot_pad = padded_2(cot_b, (("tm", 1),), 1)
    temporal = jnp.zeros((row_count, chans), F32)
    grad_hidden = jnp.zeros((row_count, chans), F32)
    grads = []
    for k in range(3):
        shifted_hid = hidden_pad[:, k : k + frames].reshape(row_count, chans)
        temporal = temporal + nn_dot(shifted_hid, temporal_all[k])
        shifted_cot = cot_pad[:, 2 - k : 2 - k + frames].reshape(row_count, chans)
        grad_hidden = grad_hidden + transpose_dot(shifted_cot, temporal_all[k])
        grads.append(outer_dot(shifted_hid, cot_flat))
    total_rows = row_count * lax.axis_size("tm") * lax.axis_size("clip")
    summed = lax.psum(jnp.stack(grads), "tm")
    owned = lax.psum_scatter(summed, "clip", scatter_dimension=1, tiled=True)
    grad_spatial = (grad_hidden * sigmoid_s * (1.0 + spatial * (1.0 - sigmoid_s))).astype(BF16)
    grad_frames = jnp.pad(grad_spatial.reshape(video.shape), pads)
    grad_acc = cotangent.reshape(row_count, chans)
    for y in range(3):
        for x in range(3):
            window = grad_frames[:, :, 2 - y : 2 - y + height, 2 - x : 2 - x + width, :]
            window = window.reshape(row_count, chans)
            grad_acc = grad_acc + transpose_dot(window, spatial_all[3 * y + x])
    return (
        video + temporal.reshape(video.shape),
        grad_acc.reshape(video.shape),
        owned * (1.0 / math.sqrt(total_rows)),
    )


def solution(mesh):
    n_tm, n_clip = mesh.shape["tm"], mesh.shape["clip"]

    def on_device(video, spatial_w, spatial_b, temporal_w, cotangent):
        args = (video, spatial_w, spatial_b, temporal_w, cotangent)
        one_frame = video.shape[0] == 1 and video.shape[1] == 1
        depth, chans = spatial_w.shape[1:]
        lanes = -(-3 * chans // (128 * n_tm)) * 128
        whole_rows = depth * (-(-chans // 128) * 128) % (2 * chans) == 0
        fits = depth % 16 == 0 and depth > 16 * TAIL and 2 * chans % lanes == 0
        if one_frame and fits and n_clip == 4 and n_tm % 4 == 0 and n_tm * lanes <= 4 * chans and whole_rows:
            return fused(n_tm, n_clip, *args)
        return native(*args)

    return jax.shard_map(
        on_device,
        mesh=mesh,
        in_specs=(
            P("clip", "tm", None, None, None),
            P(None, "clip", None),
            P(),
            P(None, "clip", None),
            P("clip", "tm", None, None, None),
        ),
        out_specs=(
            P("clip", "tm", None, None, None),
            P("clip", "tm", None, None, None),
            P(None, "clip", None),
        ),
        check_vma=False,
    )
```

```python
import functools
import math

import jax
import jax.numpy as jnp
from jax import lax
from jax.experimental import pallas as pl
from jax.experimental.pallas import tpu as pltpu
from jax.sharding import PartitionSpec as P

F32 = jnp.float32
BF16 = jnp.bfloat16
MESH = pl.DeviceIdType.MESH


def nn_dot(left, right):
    return lax.dot_general(left, right, (((1,), (0,)), ((), ())), preferred_element_type=F32)


def outer_dot(left, right):
    return lax.dot_general(left, right, (((0,), (0,)), ((), ())), preferred_element_type=F32)


def transpose_dot(left, right):
    return lax.dot_general(left, right, (((1,), (1,)), ((), ())), preferred_element_type=F32)


TAIL = 2


def own_cot_of(ref):
    return ref[...].astype(BF16)


def block_kernel(
    dims,
    video_h, sw_h, bias_h, tw_h, cot_h,
    out_v, gv_v, gt_v,
    video, cot, sw, tw, bias_ref, wp, wg, xcat, cb, chalo, cote, cotl, hb, cstash, hpack, hhalo, hstash, spat, gpad,
    gtl, rx, ysend, ry, psum, pb, rs, ag,
    load_sem, w_send, w_recv, halo_send, halo_recv, g_send, g_recv, a_send, a_recv, gate,
):
    n_tm, n_clip, height, width, chans, scale = dims
    rows = height * width
    depth = sw_h.shape[1]
    half = rows // 2
    quarter = rows // 4
    side_chans = chans // 2
    chunks = 4
    chunk = half // chunks
    low = depth - 16 * TAIL
    head = -(-chans // 128) * 128
    lanes = psum.shape[2]
    n_early = 2 * chans // lanes
    n_late = n_tm - n_early
    skip = n_late * lanes - chans
    tm = lax.axis_index("tm")
    c = lax.axis_index("clip")

    def flip(value, bit):
        return value + bit - 2 * bit * (lax.rem(value // bit, 2))

    core, ypart = flip(c, 1), flip(c, 2)
    xpart, zpart = flip(tm, 1), flip(tm, 2)
    parity = lax.rem(tm, 2)
    h = lax.rem(tm // 2, 2)
    yc = c // 2
    mine = lax.rem(c, 2)
    has_up, has_down = tm + 2 < n_tm, tm >= 2

    def signal(sem, device):
        pl.semaphore_signal(sem, inc=1, device_id=device, device_id_type=MESH)

    def tm_signals(sem):
        signal(sem, (xpart, c))

        @pl.when(has_up)
        def _():
            signal(sem, (tm + 2, c))

        @pl.when(has_down)
        def _():
            signal(sem, (tm - 2, c))

    def tm_waits(sem, extra):
        n_z, z = n_tm // 2, tm // 2
        ups, downs = (2 * n_z - 2 - z) // n_z, (z + n_z - 1) // n_z
        pl.semaphore_wait(sem, 1 + extra + ups + downs)

    rounds = n_tm // 2 - 1

    def gate_step(r):
        if r < rounds:
            tm_waits(gate.at[r], 0)
        if r + 1 < rounds:
            tm_signals(gate.at[r + 1])

    barrier = pltpu.get_barrier_semaphore()
    signal(barrier, (tm, ypart))
    signal(barrier, (tm, core))
    tm_signals(barrier)

    loads = [
        pltpu.make_async_copy(sw_h.at[pl.ds(0, 4)], sw.at[pl.ds(0, 4)], load_sem.at[0]),
        pltpu.make_async_copy(sw_h.at[pl.ds(4, 4)], sw.at[pl.ds(4, 4)], load_sem.at[0]),
        pltpu.make_async_copy(sw_h.at[pl.ds(8, 1)], sw.at[pl.ds(8, 1)], load_sem.at[5]),
        pltpu.make_async_copy(tw_h, tw, load_sem.at[1]),
        pltpu.make_async_copy(cot_h, cot, load_sem.at[2]),
        pltpu.make_async_copy(video_h, video, load_sem.at[3]),
        pltpu.make_async_copy(bias_h, bias_ref, load_sem.at[4]),
    ]
    for load in loads:
        load.start()

    def pack(value):
        return jnp.concatenate([value[:quarter], value[quarter:]], axis=1)

    def unpack(ref, slot):
        parts = []
        for q in range(2):
            both = ref[slot, q * quarter : (q + 1) * quarter]
            parts += [both[:, :chans], both[:, chans:]]
        return jnp.concatenate(parts, axis=0)

    pltpu.make_async_copy(sw_h.at[pl.ds(0, 8)], sw.at[pl.ds(0, 8)], load_sem.at[0]).wait()
    for pair in range(4):
        wp[c, pair] = jnp.concatenate([sw[2 * pair], sw[2 * pair + 1]], axis=1)
    tm_waits(barrier, 2)

    def send(src, dst, ssem, rsem, device):
        copy = pltpu.make_async_remote_copy(
            src_ref=src, dst_ref=dst, send_sem=ssem, recv_sem=rsem,
            device_id=device, device_id_type=MESH,
        )
        copy.start()
        return copy

    def settle(ref, ssem, rsem):
        return pltpu.make_async_remote_copy(
            src_ref=ref, dst_ref=ref, send_sem=ssem, recv_sem=rsem,
            device_id=(tm, core), device_id_type=MESH,
        )

    def sent(ref, sem):
        settle(ref, sem, sem).wait_send()

    def received(ref, sem):
        settle(ref, sem, sem).wait_recv()

    def block_rows(count):
        return chalo.at[0, pl.ds(0, count)]

    def wsend(slot, part, device):
        return send(part, part, w_send.at[0], w_recv.at[slot], device)

    def low_part(owner, pair):
        return wp.at[owner, pair, pl.ds(0, low)]

    def rest_part(owner):
        return wp.at[owner, pl.ds(0, 4), pl.ds(low, depth - low)]

    def head_part(owner):
        return wp.at[owner, 4, :, pl.ds(0, head)]

    def tail_part(owner):
        return wp.at[owner, 4, :, pl.ds(head, 2 * chans - head)]

    at_y, at_core, at_x, at_z = (tm, ypart), (tm, core), (xpart, c), (zpart, c)
    y_a = wsend(0, low_part(c, h), at_y)
    y_b = wsend(1, low_part(c, 2 + h), at_y)
    y_rest = wsend(2, rest_part(c), at_y)
    for load in loads[2:4]:
        load.wait()
    first = tw[0].astype(BF16)
    wp[c, 4] = jnp.concatenate([sw[8], first], axis=1)
    wp[c, 5] = jnp.concatenate([tw[1].astype(BF16), tw[2].astype(BF16)], axis=1)
    y_head = wsend(3, head_part(c), at_y)
    own = wsend(8, wp.at[c, pl.ds(0, 5)], at_core)
    tm_signals(gate.at[0])

    loads[4].wait()
    own_cot = cot[...].astype(BF16)
    for q in range(2):
        cb[q * quarter : (q + 1) * quarter] = pack(own_cot[q * half : (q + 1) * half])

    def near_send(which, own_ref, halo, q):
        part = pl.ds(q * chunk, chunk)
        return send(
            own_ref.at[part, :], halo.at[parity, part, :],
            halo_send.at[which], halo_recv.at[3 * which + min(q, 2)], (xpart, c),
        )

    def far_copy(which, halo, q):
        target = lax.rem(tm + n_tm + 2 - 4 * parity, n_tm)
        part = pl.ds(q * chunk, chunk)
        return pltpu.make_async_remote_copy(
            src_ref=halo.at[1 - parity, part, :],
            dst_ref=halo.at[parity, part, :],
            send_sem=halo_send.at[2],
            recv_sem=halo_recv.at[6 + which],
            device_id=(target, c),
            device_id_type=MESH,
        )

    sends_far = jnp.logical_or(
        jnp.logical_and(parity == 0, has_up), jnp.logical_and(parity == 1, has_down)
    )
    gets_far = jnp.logical_or(
        jnp.logical_and(parity == 0, has_down), jnp.logical_and(parity == 1, has_up)
    )

    def far_start(which, halo, q):
        @pl.when(sends_far)
        def _():
            far_copy(which, halo, q).start()

    def far_recv(which):
        @pl.when(gets_far)
        def _():
            received(block_rows(half), halo_recv.at[6 + which])

    def stash_start(which, own_ref, held):
        @pl.when(gets_far)
        def _():
            for q in range(2, chunks):
                part = pl.ds(q * chunk, chunk)
                pltpu.make_async_remote_copy(
                    src_ref=own_ref.at[part, :], dst_ref=held.at[part, :],
                    send_sem=halo_send.at[3], recv_sem=halo_recv.at[8 + which],
                    device_id=(lax.rem(tm + n_tm + 4 * parity - 2, n_tm), c), device_id_type=MESH,
                ).start()

    def forward(which, held, halo):
        @pl.when(sends_far)
        def _():
            received(block_rows(2 * chunk), halo_recv.at[8 + which])
            for q in range(2, chunks):
                part = pl.ds(q * chunk, chunk)
                pltpu.make_async_remote_copy(
                    src_ref=held.at[part, :], dst_ref=halo.at[1 - parity, part, :],
                    send_sem=halo_send.at[2], recv_sem=halo_recv.at[6 + which],
                    device_id=at_x, device_id_type=MESH,
                ).start()

    cot_near = [near_send(0, cb, chalo, q) for q in range(chunks)]
    stash_start(0, cb, cstash)

    for edge, slot in ((0, 0), (n_tm - 1, 1)):
        @pl.when(tm == edge)
        def _():
            chalo[slot] = jnp.zeros((half, 2 * chans), BF16)
            hhalo[slot] = jnp.zeros((half, 2 * chans), BF16)

    column = lax.rem(lax.broadcasted_iota(jnp.int32, (rows, chans), 0), width)

    def shifted(value, step):
        if step == 0:
            return value
        rolled = pltpu.roll(value, step % rows, 0)
        return jnp.where(column == (0 if step == 1 else width - 1), 0.0, rolled)

    for s in range(2):
        xcat[s, 0:width] = jnp.zeros((width, 3 * side_chans), BF16)
        xcat[s, width + rows :] = jnp.zeros((width, 3 * side_chans), BF16)
    for b in range(3):
        gpad[b, 0:width] = jnp.zeros((width, chans), BF16)
        gpad[b, width + rows :] = jnp.zeros((width, chans), BF16)
    loads[5].wait()
    loads[6].wait()
    frame = video[...]
    views = [shifted(frame, 1 - b).astype(BF16) for b in range(3)]
    for s in range(2):
        xcat[s, width : width + rows] = jnp.concatenate(
            [view[:, s * side_chans : (s + 1) * side_chans] for view in views], axis=1
        )

    def unpack_pair(owner, pair, taps=(0, 1)):
        both = wp[owner, pair] if 1 in taps else wp[owner, pair, :, 0:head]
        band = pl.ds(pl.multiple_of(owner * depth, 16), depth)
        for e in taps:
            wg[2 * pair + e, band] = both[:, e * chans : (e + 1) * chans]

    def unpack_spatial(owner, first=0, count=5):
        for pair in range(first, first + count):
            unpack_pair(owner, pair, (0, 1) if pair < 4 else (0,))

    def conv_part(s, q, taps=(0, 1, 2)):
        total = None
        for a in taps:
            band = pl.ds(pl.multiple_of(s * side_chans, 16), side_chans)
            weights = jnp.concatenate([wg[3 * a + b, band] for b in range(3)], axis=0)
            term = nn_dot(
                xcat[s, a * width + q * half : a * width + (q + 1) * half], weights
            )
            total = term if total is None else total + term
        return total

    unpack_spatial(c)

    @pl.when(parity == 0)
    def _():
        cote[:, chans : 2 * chans] = own_cot_of(cot)
        cotl[:, chans:] = jnp.zeros((rows, skip), BF16)

    @pl.when(parity == 1)
    def _():
        middle = own_cot_of(cot)
        cote[:, 0 : chans - skip] = middle[:, skip:]
        cote[:, 2 * chans - skip :] = jnp.zeros((rows, skip), BF16)
        cotl[:, chans:] = middle[:, :skip]

    own.wait_recv()
    unpack_spatial(core)
    for q in range(2):
        spat[q * half : (q + 1) * half] = bias_ref[...].reshape(1, chans) + conv_part(yc, q)

    y_a.wait_recv()
    z_a = wsend(6, low_part(ypart, h), at_z)
    wsend(9, low_part(ypart, h), at_core)
    y_b.wait_recv()
    z_b = wsend(7, low_part(ypart, 2 + h), at_z)
    wsend(10, low_part(ypart, 2 + h), at_core)
    gate_step(0)
    y_rest.wait_recv()
    wsend(9, rest_part(ypart), at_core)
    forward(0, cstash, chalo)
    z_a.wait_recv()
    wsend(9, low_part(ypart, 1 - h), at_core)
    gate_step(1)
    y_head.wait_recv()
    wsend(10, head_part(ypart), at_core)
    y_tail = wsend(4, tail_part(c), at_y)
    y_last = wsend(5, wp.at[c, 5], at_y)
    for q in range(2):
        cot_near[q].wait_recv()
        far_start(0, chalo, q)
    z_b.wait_recv()
    wsend(10, low_part(ypart, 3 - h), at_core)
    diagonal = flip(core, 2)
    unpack_spatial(ypart)
    received(block_rows(4 * depth - 2 * low), w_recv.at[9])
    unpack_spatial(diagonal, 0, 2)
    for q in range(2):
        part = pl.ds(q * half, half)
        spat[part] = spat[part] + conv_part(1 - yc, q, (0,))
    head_rows = depth * head // (2 * chans)
    received(block_rows(2 * low + head_rows), w_recv.at[10])
    wsend(11, wp.at[c, 5], at_core)
    unpack_spatial(diagonal, 2, 3)

    hid_near = []
    for q in range(2):
        acc = spat[q * half : (q + 1) * half] + conv_part(1 - yc, q, (1, 2))
        hidden = (acc * jax.nn.sigmoid(acc)).astype(BF16)
        hb[q * half : (q + 1) * half] = hidden
        hpack[q * quarter : (q + 1) * quarter] = pack(hidden)
        hid_near += [near_send(1, hpack, hhalo, 2 * q + e) for e in range(2)]
        if q == 1:
            stash_start(1, hpack, hstash)
        spat[q * half : (q + 1) * half] = acc
    received(block_rows(2 * chunk), halo_recv.at[2])

    early = (n_tm - n_early) * parity
    late = n_early * (1 - parity)

    def place(products, first, count):
        for i in range(count):
            for owner in range(n_clip):
                gtl[owner % 2, owner // 2, first + i] = products[
                    owner * depth : (owner + 1) * depth, i * lanes : (i + 1) * lanes
                ]

    def core_send(slot, side, first, count):
        part = pl.ds(first, count)
        return send(
            gtl.at[1 - mine, side, part], rx.at[side, part],
            g_send.at[0], g_recv.at[slot], at_core,
        )

    def y_send(slot, first, count):
        for i in range(count):
            ysend[first + i] = (gtl[mine, 1 - yc, first + i] + rx[1 - yc, first + i]).astype(BF16)
        part = pl.ds(first, count)
        return send(ysend.at[part], ry.at[part], g_send.at[1], g_recv.at[slot], at_y)

    share = n_tm // 4
    first_owner = n_tm // 2 - 2
    owns = jnp.logical_and(tm >= first_owner, tm < first_owner + 4)

    def scatter_copy(unit):
        place_in = lax.rem(unit, share)
        return pltpu.make_async_remote_copy(
            src_ref=pb.at[unit], dst_ref=rs.at[tm, place_in],
            send_sem=a_send.at[0], recv_sem=a_recv.at[0],
            device_id=(first_owner + unit // share, c), device_id_type=MESH,
        )

    def gather_copy(owner, to):
        part = ag.at[pl.ds(owner * share, share)]
        return pltpu.make_async_remote_copy(
            src_ref=part, dst_ref=part,
            send_sem=a_send.at[1], recv_sem=a_recv.at[1],
            device_id=(to, c), device_id_type=MESH,
        )

    def scatter(first, count):
        for i in range(count):
            to = first + i
            part = gtl[mine, yc, to] + rx[yc, to] + ry[to].astype(F32)
            psum[to] = part
            pb[to] = part.astype(BF16)

            @pl.when(tm != first_owner + to // share)
            def _():
                scatter_copy(to).start()

    def pass_hidden(q):
        hid_near[q].wait_recv()
        far_start(1, hhalo, q)

    @pl.when(parity == 0)
    def _():
        cote[:, 0:chans] = unpack(chalo, 1)

    @pl.when(parity == 1)
    def _():
        cote[:, chans - skip : 2 * chans - skip] = unpack(chalo, 0)

    place(outer_dot(hb[...], cote[...]), early, n_early)
    core_e = [core_send(e, side, early, n_early) for e, side in enumerate((1 - yc, yc))]
    core_e[0].wait_recv()
    y_e = y_send(4, early, n_early)

    far_recv(0)
    cotl[:, 0:chans] = unpack(chalo, parity)
    place(outer_dot(hb[...], cotl[...]), late, n_late)
    core_l = [core_send(2 + e, side, late, n_late) for e, side in enumerate((1 - yc, yc))]

    y_tail.wait_recv()
    wsend(11, tail_part(ypart), at_core)
    y_last.wait_recv()
    wsend(11, wp.at[ypart, 5], at_core)
    core_l[0].wait_recv()
    y_l = y_send(5, late, n_late)
    pass_hidden(0)

    received(block_rows(3 * depth - head_rows), w_recv.at[11])
    for owner in range(n_clip):
        unpack_pair(owner, 4, (1,))
        unpack_pair(owner, 5)
    grad_h = transpose_dot(unpack(chalo, 1), wg[9])
    grad_h = grad_h + transpose_dot(cot[...].astype(BF16), wg[10])
    grad_h = grad_h + transpose_dot(unpack(chalo, 0), wg[11])
    acc = spat[...]
    sig = jax.nn.sigmoid(acc)
    grad_s = grad_h * (sig * (1.0 + acc * (1.0 - sig)))
    for b in range(3):
        gpad[b, width : width + rows] = shifted(grad_s, b - 1).astype(BF16)

    for r in range(2, rounds):
        gate_step(r)
    core_e[1].wait_recv()
    y_e.wait_recv()
    scatter(early, n_early)

    def grad_conv(q):
        acc = cot[q * half : (q + 1) * half]
        for a in range(3):
            start = (2 - a) * width + q * half
            for b in range(3):
                acc = acc + transpose_dot(gpad[b, start : start + half], wg[3 * a + b])
        gv_v[q * half : (q + 1) * half] = acc

    core_l[1].wait_recv()
    y_l.wait_recv()
    scatter(late, n_late)
    grad_conv(0)
    pass_hidden(1)
    grad_conv(1)
    forward(1, hstash, hhalo)
    out_v[...] = video[...] + nn_dot(hb[...], wg[10])

    @pl.when(owns)
    def _():
        mine_at = tm - first_owner
        rs[tm] = jnp.zeros(rs.shape[1:], BF16)
        received(rs.at[pl.ds(0, n_tm - 1)], a_recv.at[0])
        for e in range(share):
            total = psum[mine_at * share + e]
            for sender in range(n_tm):
                total = total + rs[sender, e].astype(F32)
            ag[mine_at * share + e] = total.astype(BF16)
        for to in (0, 1, n_tm - 2, n_tm - 1, *range(2, n_tm - 2)):
            @pl.when(tm != to)
            def _():
                gather_copy(mine_at, to).start()

    received(block_rows(2 * chunk), halo_recv.at[5])
    out_v[...] = out_v[...] + nn_dot(unpack(hhalo, 1 - parity), wg[11 - 2 * parity])
    far_recv(1)
    out_v[...] = out_v[...] + nn_dot(unpack(hhalo, parity), wg[9 + 2 * parity])

    @pl.when(owns)
    def _():
        received(ag.at[pl.ds(0, 3 * share)], a_recv.at[1])

    @pl.when(jnp.logical_not(owns))
    def _():
        received(ag, a_recv.at[1])

    whole = jnp.concatenate([ag[to] for to in range(n_tm)], axis=1).astype(F32) * scale
    for k in range(3):
        gt_v[k] = whole[:, k * chans : (k + 1) * chans]

    sent(wp.at[pl.ds(0, 3)], w_send.at[0])
    sent(block_rows(half), halo_send.at[0])
    sent(block_rows(half), halo_send.at[1])
    sent(gtl.at[0], g_send.at[0])
    sent(ysend, g_send.at[1])

    @pl.when(sends_far)
    def _():
        sent(chalo, halo_send.at[2])

    @pl.when(gets_far)
    def _():
        sent(block_rows(half), halo_send.at[3])

    @pl.when(owns)
    def _():
        sent(pb.at[pl.ds(0, n_tm - share)], a_send.at[0])
        sent(rs.at[pl.ds(0, n_tm - 1)], a_send.at[1])

    @pl.when(jnp.logical_not(owns))
    def _():
        sent(pb, a_send.at[0])


def hand_over(*refs):
    n = len(refs) // 2
    ins, outs, sem = refs[:n], refs[n : 2 * n], refs[2 * n]
    writes = []
    for e in range(n):
        writes.append(pltpu.make_async_copy(ins[e], outs[e], sem.at[e]))
    for write in writes:
        write.start()
    for write in writes:
        write.wait()


def fused(n_tm, n_clip, video, spatial_w, spatial_b, temporal_w, cotangent):
    clips, frames, height, width, chans = video.shape
    rows = height * width
    depth = spatial_w.shape[1]
    lanes = -(-3 * chans // (128 * n_tm)) * 128
    scale = 1.0 / math.sqrt(rows * n_tm * n_clip)
    any_spec = pl.BlockSpec(memory_space=pltpu.HBM)
    vm_spec = pl.BlockSpec(memory_space=pltpu.VMEM)
    vm = pltpu.VMEM
    dma = pltpu.SemaphoreType.DMA
    results = pl.pallas_call(
        functools.partial(block_kernel, (n_tm, n_clip, height, width, chans, scale)),
        out_shape=(
            vm((rows, chans), F32),
            vm((rows, chans), F32),
            vm((3, depth, chans), F32),
        ),
        in_specs=[any_spec, any_spec, any_spec, any_spec, any_spec],
        out_specs=(vm_spec, vm_spec, vm_spec),
        scratch_shapes=[
            vm((rows, chans), F32),
            vm((rows, chans), F32),
            vm((9, depth, chans), BF16),
            vm((3, depth, chans), F32),
            vm((chans,), F32),
            vm((n_clip, 6, depth, 2 * chans), BF16),
            vm((12, chans, chans), BF16),
            vm((2, rows + 2 * width, 3 * chans // 2), BF16),
            vm((rows // 2, 2 * chans), BF16),
            vm((2, rows // 2, 2 * chans), BF16),
            vm((rows, 2 * chans), BF16),
            vm((rows, n_tm * lanes - 2 * chans), BF16),
            vm((rows, chans), BF16),
            vm((rows // 2, 2 * chans), BF16),
            vm((rows // 2, 2 * chans), BF16),
            vm((2, rows // 2, 2 * chans), BF16),
            vm((rows // 2, 2 * chans), BF16),
            vm((rows, chans), F32),
            vm((3, rows + 2 * width, chans), BF16),
            vm((2, 2, n_tm, depth, lanes), F32),
            vm((2, n_tm, depth, lanes), F32),
            vm((n_tm, depth, lanes), BF16),
            vm((n_tm, depth, lanes), BF16),
            vm((n_tm, depth, lanes), F32),
            vm((n_tm, depth, lanes), BF16),
            vm((n_tm, n_tm // 4, depth, lanes), BF16),
            vm((n_tm, depth, lanes), BF16),
            dma((6,)),
            dma((1,)),
            dma((12,)),
            dma((4,)),
            dma((10,)),
            dma((2,)),
            dma((6,)),
            dma((2,)),
            dma((2,)),
            pltpu.SemaphoreType.REGULAR((n_tm // 2 - 1,)),
        ],
        compiler_params=pltpu.CompilerParams(
            collective_id=0, has_side_effects=True, vmem_limit_bytes=65_000_000
        ),
        name="block",
    )(
        video.reshape(rows, chans), spatial_w, spatial_b, temporal_w,
        cotangent.reshape(rows, chans),
    )
    shapes = tuple(jax.ShapeDtypeStruct(array.shape, F32) for array in results)

    out, gv, gt = pl.pallas_call(
        hand_over,
        out_shape=shapes,
        in_specs=[vm_spec] * 3,
        out_specs=(any_spec,) * 3,
        scratch_shapes=[dma((3,))],
        compiler_params=pltpu.CompilerParams(vmem_limit_bytes=2**20),
        name="hand_over",
    )(*results)
    return out.reshape(video.shape), gv.reshape(video.shape), gt


def padded_2(cells, sides, width):
    for axis, dim in sides:
        count = lax.axis_size(axis)
        ends = count - 1
        head = lax.slice_in_dim(cells, 0, width, axis=dim)
        tail = lax.slice_in_dim(cells, cells.shape[dim] - width, cells.shape[dim], axis=dim)
        cells = jnp.concatenate(
            [
                lax.ppermute(tail, axis, [(i, (i + 1) % count) for i in range(ends)]),
                cells,
                lax.ppermute(head, axis, [((i + 1) % count, i) for i in range(ends)]),
            ],
            axis=dim,
        )
    return cells


def native(video, spatial_w, spatial_b, temporal_w, cotangent):
    clips, frames, height, width, chans = video.shape
    row_count = clips * frames * height * width
    pads = ((0, 0), (0, 0), (1, 1), (1, 1), (0, 0))
    padded = jnp.pad(video.astype(BF16), pads)
    temporal_b = temporal_w.astype(BF16)
    spatial_all = lax.all_gather(spatial_w, "clip", axis=1, tiled=True)
    temporal_all = lax.all_gather(temporal_b, "clip", axis=1, tiled=True)
    spatial = jnp.zeros((row_count, chans), F32)
    for y in range(3):
        for x in range(3):
            window = padded[:, :, y : y + height, x : x + width, :].reshape(row_count, chans)
            spatial = spatial + nn_dot(window, spatial_all[3 * y + x])
    spatial = spatial + spatial_b
    sigmoid_s = jax.nn.sigmoid(spatial)
    hidden = (spatial * sigmoid_s).astype(BF16).reshape(video.shape)
    hidden_pad = padded_2(hidden, (("tm", 1),), 1)
    cot_b = cotangent.astype(BF16)
    cot_flat = cot_b.reshape(row_count, chans)
    cot_pad = padded_2(cot_b, (("tm", 1),), 1)
    temporal = jnp.zeros((row_count, chans), F32)
    grad_hidden = jnp.zeros((row_count, chans), F32)
    grads = []
    for k in range(3):
        shifted_hid = hidden_pad[:, k : k + frames].reshape(row_count, chans)
        temporal = temporal + nn_dot(shifted_hid, temporal_all[k])
        shifted_cot = cot_pad[:, 2 - k : 2 - k + frames].reshape(row_count, chans)
        grad_hidden = grad_hidden + transpose_dot(shifted_cot, temporal_all[k])
        grads.append(outer_dot(shifted_hid, cot_flat))
    total_rows = row_count * lax.axis_size("tm") * lax.axis_size("clip")
    summed = lax.psum(jnp.stack(grads), "tm")
    owned = lax.psum_scatter(summed, "clip", scatter_dimension=1, tiled=True)
    grad_spatial = (grad_hidden * sigmoid_s * (1.0 + spatial * (1.0 - sigmoid_s))).astype(BF16)
    grad_frames = jnp.pad(grad_spatial.reshape(video.shape), pads)
    grad_acc = cotangent.reshape(row_count, chans)
    for y in range(3):
        for x in range(3):
            window = grad_frames[:, :, 2 - y : 2 - y + height, 2 - x : 2 - x + width, :]
            window = window.reshape(row_count, chans)
            grad_acc = grad_acc + transpose_dot(window, spatial_all[3 * y + x])
    return (
        video + temporal.reshape(video.shape),
        grad_acc.reshape(video.shape),
        owned * (1.0 / math.sqrt(total_rows)),
    )


def solution(mesh):
    n_tm, n_clip = mesh.shape["tm"], mesh.shape["clip"]

    def on_device(video, spatial_w, spatial_b, temporal_w, cotangent):
        args = (video, spatial_w, spatial_b, temporal_w, cotangent)
        one_frame = video.shape[0] == 1 and video.shape[1] == 1
        depth, chans = spatial_w.shape[1:]
        lanes = -(-3 * chans // (128 * n_tm)) * 128
        whole_rows = depth * (-(-chans // 128) * 128) % (2 * chans) == 0
        fits = depth % 16 == 0 and depth > 16 * TAIL and 2 * chans % lanes == 0
        if one_frame and fits and n_clip == 4 and n_tm % 4 == 0 and n_tm * lanes <= 4 * chans and whole_rows:
            return fused(n_tm, n_clip, *args)
        return native(*args)

    return jax.shard_map(
        on_device,
        mesh=mesh,
        in_specs=(
            P("clip", "tm", None, None, None),
            P(None, "clip", None),
            P(),
            P(None, "clip", None),
            P("clip", "tm", None, None, None),
        ),
        out_specs=(
            P("clip", "tm", None, None, None),
            P("clip", "tm", None, None, None),
            P(None, "clip", None),
        ),
        check_vma=False,
    )
```

```python
import functools
import math

import jax
import jax.numpy as jnp
from jax import lax
from jax.experimental import pallas as pl
from jax.experimental.pallas import tpu as pltpu
from jax.sharding import PartitionSpec as P

F32 = jnp.float32
BF16 = jnp.bfloat16
MESH = pl.DeviceIdType.MESH


def nn_dot(left, right):
    return lax.dot_general(left, right, (((1,), (0,)), ((), ())), preferred_element_type=F32)


def outer_dot(left, right):
    return lax.dot_general(left, right, (((0,), (0,)), ((), ())), preferred_element_type=F32)


def transpose_dot(left, right):
    return lax.dot_general(left, right, (((1,), (1,)), ((), ())), preferred_element_type=F32)


TAIL = 2


def own_cot_of(ref):
    return ref[...].astype(BF16)


def block_kernel(
    dims,
    video_h, sw_h, bias_h, tw_h, cot_h,
    out_v, gv_v, gt_v,
    video, cot, sw, tw, bias_ref, wp, wg, xcat, cb, chalo, cote, cotl, hb, cstash, hpack, hhalo, hstash, spat, gpad,
    gtl, rx, ysend, ry, psum, pb, rs, ag,
    load_sem, w_send, w_recv, halo_send, halo_recv, g_send, g_recv, a_send, a_recv, gate,
):
    n_tm, n_clip, height, width, chans, scale = dims
    rows = height * width
    depth = sw_h.shape[1]
    half = rows // 2
    quarter = rows // 4
    side_chans = chans // 2
    chunks = 4
    chunk = half // chunks
    low = depth - 16 * TAIL
    head = -(-chans // 128) * 128
    lanes = psum.shape[2]
    n_early = 2 * chans // lanes
    n_late = n_tm - n_early
    skip = n_late * lanes - chans
    tm = lax.axis_index("tm")
    c = lax.axis_index("clip")

    def flip(value, bit):
        return value + bit - 2 * bit * (lax.rem(value // bit, 2))

    core, ypart = flip(c, 1), flip(c, 2)
    xpart, zpart = flip(tm, 1), flip(tm, 2)
    parity = lax.rem(tm, 2)
    h = lax.rem(tm // 2, 2)
    yc = c // 2
    mine = lax.rem(c, 2)
    has_up, has_down = tm + 2 < n_tm, tm >= 2

    def signal(sem, device):
        pl.semaphore_signal(sem, inc=1, device_id=device, device_id_type=MESH)

    def tm_signals(sem):
        signal(sem, (xpart, c))

        @pl.when(has_up)
        def _():
            signal(sem, (tm + 2, c))

        @pl.when(has_down)
        def _():
            signal(sem, (tm - 2, c))

    def tm_waits(sem, extra):
        n_z, z = n_tm // 2, tm // 2
        ups, downs = (2 * n_z - 2 - z) // n_z, (z + n_z - 1) // n_z
        pl.semaphore_wait(sem, 1 + extra + ups + downs)

    rounds = n_tm // 2 - 1

    def gate_step(r):
        if r < rounds:
            tm_waits(gate.at[r], 0)
        if r + 1 < rounds:
            tm_signals(gate.at[r + 1])

    barrier = pltpu.get_barrier_semaphore()
    signal(barrier, (tm, ypart))
    signal(barrier, (tm, core))
    tm_signals(barrier)

    loads = [
        pltpu.make_async_copy(sw_h.at[pl.ds(0, 4)], sw.at[pl.ds(0, 4)], load_sem.at[0]),
        pltpu.make_async_copy(sw_h.at[pl.ds(4, 4)], sw.at[pl.ds(4, 4)], load_sem.at[0]),
        pltpu.make_async_copy(sw_h.at[pl.ds(8, 1)], sw.at[pl.ds(8, 1)], load_sem.at[5]),
        pltpu.make_async_copy(tw_h, tw, load_sem.at[1]),
        pltpu.make_async_copy(cot_h, cot, load_sem.at[2]),
        pltpu.make_async_copy(video_h, video, load_sem.at[3]),
        pltpu.make_async_copy(bias_h, bias_ref, load_sem.at[4]),
    ]
    for load in loads:
        load.start()

    def pack(value):
        return jnp.concatenate([value[:quarter], value[quarter:]], axis=1)

    def unpack(ref, slot):
        parts = []
        for q in range(2):
            both = ref[slot, q * quarter : (q + 1) * quarter]
            parts += [both[:, :chans], both[:, chans:]]
        return jnp.concatenate(parts, axis=0)

    pltpu.make_async_copy(sw_h.at[pl.ds(0, 8)], sw.at[pl.ds(0, 8)], load_sem.at[0]).wait()
    for pair in range(4):
        wp[c, pair] = jnp.concatenate([sw[2 * pair], sw[2 * pair + 1]], axis=1)
    tm_waits(barrier, 2)

    def send(src, dst, ssem, rsem, device):
        copy = pltpu.make_async_remote_copy(
            src_ref=src, dst_ref=dst, send_sem=ssem, recv_sem=rsem,
            device_id=device, device_id_type=MESH,
        )
        copy.start()
        return copy

    def settle(ref, ssem, rsem):
        return pltpu.make_async_remote_copy(
            src_ref=ref, dst_ref=ref, send_sem=ssem, recv_sem=rsem,
            device_id=(tm, core), device_id_type=MESH,
        )

    def sent(ref, sem):
        settle(ref, sem, sem).wait_send()

    def received(ref, sem):
        settle(ref, sem, sem).wait_recv()

    def block_rows(count):
        return chalo.at[0, pl.ds(0, count)]

    def wsend(slot, part, device):
        return send(part, part, w_send.at[0], w_recv.at[slot], device)

    def low_part(owner, pair):
        return wp.at[owner, pair, pl.ds(0, low)]

    def rest_part(owner):
        return wp.at[owner, pl.ds(0, 4), pl.ds(low, depth - low)]

    def head_part(owner):
        return wp.at[owner, 4, :, pl.ds(0, head)]

    def tail_part(owner):
        return wp.at[owner, 4, :, pl.ds(head, 2 * chans - head)]

    at_y, at_core, at_x, at_z = (tm, ypart), (tm, core), (xpart, c), (zpart, c)
    y_a = wsend(0, low_part(c, h), at_y)
    y_b = wsend(1, low_part(c, 2 + h), at_y)
    y_rest = wsend(2, rest_part(c), at_y)
    for load in loads[2:4]:
        load.wait()
    first = tw[0].astype(BF16)
    wp[c, 4] = jnp.concatenate([sw[8], first], axis=1)
    wp[c, 5] = jnp.concatenate([tw[1].astype(BF16), tw[2].astype(BF16)], axis=1)
    y_head = wsend(3, head_part(c), at_y)
    own = wsend(8, wp.at[c, pl.ds(0, 5)], at_core)
    tm_signals(gate.at[0])

    loads[4].wait()
    own_cot = cot[...].astype(BF16)
    for q in range(2):
        cb[q * quarter : (q + 1) * quarter] = pack(own_cot[q * half : (q + 1) * half])

    def near_send(which, own_ref, halo, q):
        part = pl.ds(q * chunk, chunk)
        return send(
            own_ref.at[part, :], halo.at[parity, part, :],
            halo_send.at[which], halo_recv.at[3 * which + min(q, 2)], (xpart, c),
        )

    def far_copy(which, halo, q):
        target = lax.rem(tm + n_tm + 2 - 4 * parity, n_tm)
        part = pl.ds(q * chunk, chunk)
        return pltpu.make_async_remote_copy(
            src_ref=halo.at[1 - parity, part, :],
            dst_ref=halo.at[parity, part, :],
            send_sem=halo_send.at[2],
            recv_sem=halo_recv.at[6 + which],
            device_id=(target, c),
            device_id_type=MESH,
        )

    sends_far = jnp.logical_or(
        jnp.logical_and(parity == 0, has_up), jnp.logical_and(parity == 1, has_down)
    )
    gets_far = jnp.logical_or(
        jnp.logical_and(parity == 0, has_down), jnp.logical_and(parity == 1, has_up)
    )

    def far_start(which, halo, q):
        @pl.when(sends_far)
        def _():
            far_copy(which, halo, q).start()

    def far_recv(which):
        @pl.when(gets_far)
        def _():
            received(block_rows(half), halo_recv.at[6 + which])

    def stash_start(which, own_ref, held):
        @pl.when(gets_far)
        def _():
            for q in range(2, chunks):
                part = pl.ds(q * chunk, chunk)
                pltpu.make_async_remote_copy(
                    src_ref=own_ref.at[part, :], dst_ref=held.at[part, :],
                    send_sem=halo_send.at[3], recv_sem=halo_recv.at[8 + which],
                    device_id=(lax.rem(tm + n_tm + 4 * parity - 2, n_tm), c), device_id_type=MESH,
                ).start()

    def forward(which, held, halo):
        @pl.when(sends_far)
        def _():
            received(block_rows(2 * chunk), halo_recv.at[8 + which])
            for q in range(2, chunks):
                part = pl.ds(q * chunk, chunk)
                pltpu.make_async_remote_copy(
                    src_ref=held.at[part, :], dst_ref=halo.at[1 - parity, part, :],
                    send_sem=halo_send.at[2], recv_sem=halo_recv.at[6 + which],
                    device_id=at_x, device_id_type=MESH,
                ).start()

    cot_near = [near_send(0, cb, chalo, q) for q in range(chunks)]
    stash_start(0, cb, cstash)

    for edge, slot in ((0, 0), (n_tm - 1, 1)):
        @pl.when(tm == edge)
        def _():
            chalo[slot] = jnp.zeros((half, 2 * chans), BF16)
            hhalo[slot] = jnp.zeros((half, 2 * chans), BF16)

    column = lax.rem(lax.broadcasted_iota(jnp.int32, (rows, chans), 0), width)

    def shifted(value, step):
        if step == 0:
            return value
        rolled = pltpu.roll(value, step % rows, 0)
        return jnp.where(column == (0 if step == 1 else width - 1), 0.0, rolled)

    for s in range(2):
        xcat[s, 0:width] = jnp.zeros((width, 3 * side_chans), BF16)
        xcat[s, width + rows :] = jnp.zeros((width, 3 * side_chans), BF16)
    for b in range(3):
        gpad[b, 0:width] = jnp.zeros((width, chans), BF16)
        gpad[b, width + rows :] = jnp.zeros((width, chans), BF16)
    loads[5].wait()
    loads[6].wait()
    frame = video[...]
    views = [shifted(frame, 1 - b).astype(BF16) for b in range(3)]
    for s in range(2):
        xcat[s, width : width + rows] = jnp.concatenate(
            [view[:, s * side_chans : (s + 1) * side_chans] for view in views], axis=1
        )

    def unpack_pair(owner, pair, taps=(0, 1)):
        both = wp[owner, pair] if 1 in taps else wp[owner, pair, :, 0:head]
        band = pl.ds(pl.multiple_of(owner * depth, 16), depth)
        for e in taps:
            wg[2 * pair + e, band] = both[:, e * chans : (e + 1) * chans]

    def unpack_spatial(owner, first=0, count=5):
        for pair in range(first, first + count):
            unpack_pair(owner, pair, (0, 1) if pair < 4 else (0,))

    def conv_part(s, q, taps=(0, 1, 2)):
        total = None
        for a in taps:
            band = pl.ds(pl.multiple_of(s * side_chans, 16), side_chans)
            weights = jnp.concatenate([wg[3 * a + b, band] for b in range(3)], axis=0)
            term = nn_dot(
                xcat[s, a * width + q * half : a * width + (q + 1) * half], weights
            )
            total = term if total is None else total + term
        return total

    unpack_spatial(c)

    @pl.when(parity == 0)
    def _():
        cote[:, chans : 2 * chans] = own_cot_of(cot)
        cotl[:, chans:] = jnp.zeros((rows, skip), BF16)

    @pl.when(parity == 1)
    def _():
        middle = own_cot_of(cot)
        cote[:, 0 : chans - skip] = middle[:, skip:]
        cote[:, 2 * chans - skip :] = jnp.zeros((rows, skip), BF16)
        cotl[:, chans:] = middle[:, :skip]

    own.wait_recv()
    unpack_spatial(core)
    for q in range(2):
        spat[q * half : (q + 1) * half] = bias_ref[...].reshape(1, chans) + conv_part(yc, q)

    y_a.wait_recv()
    z_a = wsend(6, low_part(ypart, h), at_z)
    wsend(9, low_part(ypart, h), at_core)
    y_b.wait_recv()
    z_b = wsend(7, low_part(ypart, 2 + h), at_z)
    wsend(10, low_part(ypart, 2 + h), at_core)
    gate_step(0)
    y_rest.wait_recv()
    wsend(9, rest_part(ypart), at_core)
    forward(0, cstash, chalo)
    z_a.wait_recv()
    wsend(9, low_part(ypart, 1 - h), at_core)
    gate_step(1)
    diagonal = flip(core, 2)
    head_rows = depth * head // (2 * chans)

    def later(slot, part):
        return pltpu.make_async_remote_copy(
            src_ref=part, dst_ref=part, send_sem=w_send.at[0], recv_sem=w_recv.at[slot],
            device_id=at_y, device_id_type=MESH,
        )

    y_tail, y_last = later(4, tail_part(c)), later(5, wp.at[c, 5])

    def pass_head(which):
        @pl.when(mine == which)
        def _():
            y_head.wait_recv()
            wsend(12, head_part(ypart), at_core)
            y_tail.start()
            y_last.start()

    pass_head(1)
    z_b.wait_recv()
    wsend(10, low_part(ypart, 3 - h), at_core)
    for q in range(2):
        cot_near[q].wait_recv()
        far_start(0, chalo, q)
    unpack_spatial(ypart, 0, 4)
    received(block_rows(4 * depth - 2 * low), w_recv.at[9])
    received(block_rows(2 * low), w_recv.at[10])
    unpack_spatial(diagonal, 0, 4)
    pass_head(0)
    for q in range(2):
        part = pl.ds(q * half, half)
        spat[part] = spat[part] + conv_part(1 - yc, q, (0, 1))
    wsend(11, wp.at[c, 5], at_core)
    unpack_spatial(ypart, 4, 1)
    received(block_rows(head_rows), w_recv.at[12])
    unpack_spatial(diagonal, 4, 1)

    hid_near = []
    for q in range(2):
        acc = spat[q * half : (q + 1) * half] + conv_part(1 - yc, q, (2,))
        hidden = (acc * jax.nn.sigmoid(acc)).astype(BF16)
        hb[q * half : (q + 1) * half] = hidden
        hpack[q * quarter : (q + 1) * quarter] = pack(hidden)
        hid_near += [near_send(1, hpack, hhalo, 2 * q + e) for e in range(2)]
        if q == 1:
            stash_start(1, hpack, hstash)
        spat[q * half : (q + 1) * half] = acc
    received(block_rows(2 * chunk), halo_recv.at[2])

    early = (n_tm - n_early) * parity
    late = n_early * (1 - parity)

    def place(products, first, count):
        for i in range(count):
            for owner in range(n_clip):
                gtl[owner % 2, owner // 2, first + i] = products[
                    owner * depth : (owner + 1) * depth, i * lanes : (i + 1) * lanes
                ]

    def core_send(slot, side, first, count):
        part = pl.ds(first, count)
        return send(
            gtl.at[1 - mine, side, part], rx.at[side, part],
            g_send.at[0], g_recv.at[slot], at_core,
        )

    def y_send(slot, first, count):
        for i in range(count):
            ysend[first + i] = (gtl[mine, 1 - yc, first + i] + rx[1 - yc, first + i]).astype(BF16)
        part = pl.ds(first, count)
        return send(ysend.at[part], ry.at[part], g_send.at[1], g_recv.at[slot], at_y)

    share = n_tm // 4
    first_owner = n_tm // 2 - 2
    owns = jnp.logical_and(tm >= first_owner, tm < first_owner + 4)

    def scatter_copy(unit):
        place_in = lax.rem(unit, share)
        return pltpu.make_async_remote_copy(
            src_ref=pb.at[unit], dst_ref=rs.at[tm, place_in],
            send_sem=a_send.at[0], recv_sem=a_recv.at[0],
            device_id=(first_owner + unit // share, c), device_id_type=MESH,
        )

    def gather_copy(owner, to):
        part = ag.at[pl.ds(owner * share, share)]
        return pltpu.make_async_remote_copy(
            src_ref=part, dst_ref=part,
            send_sem=a_send.at[1], recv_sem=a_recv.at[1],
            device_id=(to, c), device_id_type=MESH,
        )

    def scatter(first, count):
        for i in range(count):
            to = first + i
            part = gtl[mine, yc, to] + rx[yc, to] + ry[to].astype(F32)
            psum[to] = part
            pb[to] = part.astype(BF16)

            @pl.when(tm != first_owner + to // share)
            def _():
                scatter_copy(to).start()

    def pass_hidden(q):
        hid_near[q].wait_recv()
        far_start(1, hhalo, q)

    @pl.when(parity == 0)
    def _():
        cote[:, 0:chans] = unpack(chalo, 1)

    @pl.when(parity == 1)
    def _():
        cote[:, chans - skip : 2 * chans - skip] = unpack(chalo, 0)

    place(outer_dot(hb[...], cote[...]), early, n_early)
    core_e = [core_send(e, side, early, n_early) for e, side in enumerate((1 - yc, yc))]
    core_e[0].wait_recv()
    y_e = y_send(4, early, n_early)

    far_recv(0)
    cotl[:, 0:chans] = unpack(chalo, parity)
    place(outer_dot(hb[...], cotl[...]), late, n_late)
    core_l = [core_send(2 + e, side, late, n_late) for e, side in enumerate((1 - yc, yc))]

    y_tail.wait_recv()
    wsend(11, tail_part(ypart), at_core)
    y_last.wait_recv()
    wsend(11, wp.at[ypart, 5], at_core)
    core_l[0].wait_recv()
    y_l = y_send(5, late, n_late)
    pass_hidden(0)

    received(block_rows(3 * depth - head_rows), w_recv.at[11])
    for owner in range(n_clip):
        unpack_pair(owner, 4, (1,))
        unpack_pair(owner, 5)
    grad_h = transpose_dot(unpack(chalo, 1), wg[9])
    grad_h = grad_h + transpose_dot(cot[...].astype(BF16), wg[10])
    grad_h = grad_h + transpose_dot(unpack(chalo, 0), wg[11])
    acc = spat[...]
    sig = jax.nn.sigmoid(acc)
    grad_s = grad_h * (sig * (1.0 + acc * (1.0 - sig)))
    for b in range(3):
        gpad[b, width : width + rows] = shifted(grad_s, b - 1).astype(BF16)

    for r in range(2, rounds):
        gate_step(r)
    core_e[1].wait_recv()
    y_e.wait_recv()
    scatter(early, n_early)

    def grad_conv(q):
        acc = cot[q * half : (q + 1) * half]
        for a in range(3):
            start = (2 - a) * width + q * half
            for b in range(3):
                acc = acc + transpose_dot(gpad[b, start : start + half], wg[3 * a + b])
        gv_v[q * half : (q + 1) * half] = acc

    core_l[1].wait_recv()
    y_l.wait_recv()
    scatter(late, n_late)
    grad_conv(0)
    pass_hidden(1)
    grad_conv(1)
    forward(1, hstash, hhalo)
    out_v[...] = video[...] + nn_dot(hb[...], wg[10])

    @pl.when(owns)
    def _():
        mine_at = tm - first_owner
        rs[tm] = jnp.zeros(rs.shape[1:], BF16)
        received(rs.at[pl.ds(0, n_tm - 1)], a_recv.at[0])
        for e in range(share):
            total = psum[mine_at * share + e]
            for sender in range(n_tm):
                total = total + rs[sender, e].astype(F32)
            ag[mine_at * share + e] = total.astype(BF16)
        for to in (0, 1, n_tm - 2, n_tm - 1, *range(2, n_tm - 2)):
            @pl.when(tm != to)
            def _():
                gather_copy(mine_at, to).start()

    received(block_rows(2 * chunk), halo_recv.at[5])
    out_v[...] = out_v[...] + nn_dot(unpack(hhalo, 1 - parity), wg[11 - 2 * parity])
    far_recv(1)
    out_v[...] = out_v[...] + nn_dot(unpack(hhalo, parity), wg[9 + 2 * parity])

    @pl.when(owns)
    def _():
        received(ag.at[pl.ds(0, 3 * share)], a_recv.at[1])

    @pl.when(jnp.logical_not(owns))
    def _():
        received(ag, a_recv.at[1])

    whole = jnp.concatenate([ag[to] for to in range(n_tm)], axis=1).astype(F32) * scale
    for k in range(3):
        gt_v[k] = whole[:, k * chans : (k + 1) * chans]

    sent(wp.at[pl.ds(0, 3)], w_send.at[0])
    sent(block_rows(half), halo_send.at[0])
    sent(block_rows(half), halo_send.at[1])
    sent(gtl.at[0], g_send.at[0])
    sent(ysend, g_send.at[1])

    @pl.when(sends_far)
    def _():
        sent(chalo, halo_send.at[2])

    @pl.when(gets_far)
    def _():
        sent(block_rows(half), halo_send.at[3])

    @pl.when(owns)
    def _():
        sent(pb.at[pl.ds(0, n_tm - share)], a_send.at[0])
        sent(rs.at[pl.ds(0, n_tm - 1)], a_send.at[1])

    @pl.when(jnp.logical_not(owns))
    def _():
        sent(pb, a_send.at[0])


def hand_over(*refs):
    n = len(refs) // 2
    ins, outs, sem = refs[:n], refs[n : 2 * n], refs[2 * n]
    writes = []
    for e in range(n):
        writes.append(pltpu.make_async_copy(ins[e], outs[e], sem.at[e]))
    for write in writes:
        write.start()
    for write in writes:
        write.wait()


def fused(n_tm, n_clip, video, spatial_w, spatial_b, temporal_w, cotangent):
    clips, frames, height, width, chans = video.shape
    rows = height * width
    depth = spatial_w.shape[1]
    lanes = -(-3 * chans // (128 * n_tm)) * 128
    scale = 1.0 / math.sqrt(rows * n_tm * n_clip)
    any_spec = pl.BlockSpec(memory_space=pltpu.HBM)
    vm_spec = pl.BlockSpec(memory_space=pltpu.VMEM)
    vm = pltpu.VMEM
    dma = pltpu.SemaphoreType.DMA
    results = pl.pallas_call(
        functools.partial(block_kernel, (n_tm, n_clip, height, width, chans, scale)),
        out_shape=(
            vm((rows, chans), F32),
            vm((rows, chans), F32),
            vm((3, depth, chans), F32),
        ),
        in_specs=[any_spec, any_spec, any_spec, any_spec, any_spec],
        out_specs=(vm_spec, vm_spec, vm_spec),
        scratch_shapes=[
            vm((rows, chans), F32),
            vm((rows, chans), F32),
            vm((9, depth, chans), BF16),
            vm((3, depth, chans), F32),
            vm((chans,), F32),
            vm((n_clip, 6, depth, 2 * chans), BF16),
            vm((12, chans, chans), BF16),
            vm((2, rows + 2 * width, 3 * chans // 2), BF16),
            vm((rows // 2, 2 * chans), BF16),
            vm((2, rows // 2, 2 * chans), BF16),
            vm((rows, 2 * chans), BF16),
            vm((rows, n_tm * lanes - 2 * chans), BF16),
            vm((rows, chans), BF16),
            vm((rows // 2, 2 * chans), BF16),
            vm((rows // 2, 2 * chans), BF16),
            vm((2, rows // 2, 2 * chans), BF16),
            vm((rows // 2, 2 * chans), BF16),
            vm((rows, chans), F32),
            vm((3, rows + 2 * width, chans), BF16),
            vm((2, 2, n_tm, depth, lanes), F32),
            vm((2, n_tm, depth, lanes), F32),
            vm((n_tm, depth, lanes), BF16),
            vm((n_tm, depth, lanes), BF16),
            vm((n_tm, depth, lanes), F32),
            vm((n_tm, depth, lanes), BF16),
            vm((n_tm, n_tm // 4, depth, lanes), BF16),
            vm((n_tm, depth, lanes), BF16),
            dma((6,)),
            dma((1,)),
            dma((13,)),
            dma((4,)),
            dma((10,)),
            dma((2,)),
            dma((6,)),
            dma((2,)),
            dma((2,)),
            pltpu.SemaphoreType.REGULAR((n_tm // 2 - 1,)),
        ],
        compiler_params=pltpu.CompilerParams(
            collective_id=0, has_side_effects=True, vmem_limit_bytes=65_000_000
        ),
        name="block",
    )(
        video.reshape(rows, chans), spatial_w, spatial_b, temporal_w,
        cotangent.reshape(rows, chans),
    )
    shapes = tuple(jax.ShapeDtypeStruct(array.shape, F32) for array in results)

    out, gv, gt = pl.pallas_call(
        hand_over,
        out_shape=shapes,
        in_specs=[vm_spec] * 3,
        out_specs=(any_spec,) * 3,
        scratch_shapes=[dma((3,))],
        compiler_params=pltpu.CompilerParams(vmem_limit_bytes=2**20),
        name="hand_over",
    )(*results)
    return out.reshape(video.shape), gv.reshape(video.shape), gt


def padded_2(cells, sides, width):
    for axis, dim in sides:
        count = lax.axis_size(axis)
        ends = count - 1
        head = lax.slice_in_dim(cells, 0, width, axis=dim)
        tail = lax.slice_in_dim(cells, cells.shape[dim] - width, cells.shape[dim], axis=dim)
        cells = jnp.concatenate(
            [
                lax.ppermute(tail, axis, [(i, (i + 1) % count) for i in range(ends)]),
                cells,
                lax.ppermute(head, axis, [((i + 1) % count, i) for i in range(ends)]),
            ],
            axis=dim,
        )
    return cells


def native(video, spatial_w, spatial_b, temporal_w, cotangent):
    clips, frames, height, width, chans = video.shape
    row_count = clips * frames * height * width
    pads = ((0, 0), (0, 0), (1, 1), (1, 1), (0, 0))
    padded = jnp.pad(video.astype(BF16), pads)
    temporal_b = temporal_w.astype(BF16)
    spatial_all = lax.all_gather(spatial_w, "clip", axis=1, tiled=True)
    temporal_all = lax.all_gather(temporal_b, "clip", axis=1, tiled=True)
    spatial = jnp.zeros((row_count, chans), F32)
    for y in range(3):
        for x in range(3):
            window = padded[:, :, y : y + height, x : x + width, :].reshape(row_count, chans)
            spatial = spatial + nn_dot(window, spatial_all[3 * y + x])
    spatial = spatial + spatial_b
    sigmoid_s = jax.nn.sigmoid(spatial)
    hidden = (spatial * sigmoid_s).astype(BF16).reshape(video.shape)
    hidden_pad = padded_2(hidden, (("tm", 1),), 1)
    cot_b = cotangent.astype(BF16)
    cot_flat = cot_b.reshape(row_count, chans)
    cot_pad = padded_2(cot_b, (("tm", 1),), 1)
    temporal = jnp.zeros((row_count, chans), F32)
    grad_hidden = jnp.zeros((row_count, chans), F32)
    grads = []
    for k in range(3):
        shifted_hid = hidden_pad[:, k : k + frames].reshape(row_count, chans)
        temporal = temporal + nn_dot(shifted_hid, temporal_all[k])
        shifted_cot = cot_pad[:, 2 - k : 2 - k + frames].reshape(row_count, chans)
        grad_hidden = grad_hidden + transpose_dot(shifted_cot, temporal_all[k])
        grads.append(outer_dot(shifted_hid, cot_flat))
    total_rows = row_count * lax.axis_size("tm") * lax.axis_size("clip")
    summed = lax.psum(jnp.stack(grads), "tm")
    owned = lax.psum_scatter(summed, "clip", scatter_dimension=1, tiled=True)
    grad_spatial = (grad_hidden * sigmoid_s * (1.0 + spatial * (1.0 - sigmoid_s))).astype(BF16)
    grad_frames = jnp.pad(grad_spatial.reshape(video.shape), pads)
    grad_acc = cotangent.reshape(row_count, chans)
    for y in range(3):
        for x in range(3):
            window = grad_frames[:, :, 2 - y : 2 - y + height, 2 - x : 2 - x + width, :]
            window = window.reshape(row_count, chans)
            grad_acc = grad_acc + transpose_dot(window, spatial_all[3 * y + x])
    return (
        video + temporal.reshape(video.shape),
        grad_acc.reshape(video.shape),
        owned * (1.0 / math.sqrt(total_rows)),
    )


def solution(mesh):
    n_tm, n_clip = mesh.shape["tm"], mesh.shape["clip"]

    def on_device(video, spatial_w, spatial_b, temporal_w, cotangent):
        args = (video, spatial_w, spatial_b, temporal_w, cotangent)
        one_frame = video.shape[0] == 1 and video.shape[1] == 1
        depth, chans = spatial_w.shape[1:]
        lanes = -(-3 * chans // (128 * n_tm)) * 128
        whole_rows = depth * (-(-chans // 128) * 128) % (2 * chans) == 0
        fits = depth % 16 == 0 and depth > 16 * TAIL and 2 * chans % lanes == 0
        if one_frame and fits and n_clip == 4 and n_tm % 4 == 0 and n_tm * lanes <= 4 * chans and whole_rows:
            return fused(n_tm, n_clip, *args)
        return native(*args)

    return jax.shard_map(
        on_device,
        mesh=mesh,
        in_specs=(
            P("clip", "tm", None, None, None),
            P(None, "clip", None),
            P(),
            P(None, "clip", None),
            P("clip", "tm", None, None, None),
        ),
        out_specs=(
            P("clip", "tm", None, None, None),
            P("clip", "tm", None, None, None),
            P(None, "clip", None),
        ),
        check_vma=False,
    )
```

```python
import functools
import math

import jax
import jax.numpy as jnp
from jax import lax
from jax.experimental import pallas as pl
from jax.experimental.pallas import tpu as pltpu
from jax.sharding import PartitionSpec as P

F32 = jnp.float32
BF16 = jnp.bfloat16
MESH = pl.DeviceIdType.MESH


def nn_dot(left, right):
    return lax.dot_general(left, right, (((1,), (0,)), ((), ())), preferred_element_type=F32)


def outer_dot(left, right):
    return lax.dot_general(left, right, (((0,), (0,)), ((), ())), preferred_element_type=F32)


def transpose_dot(left, right):
    return lax.dot_general(left, right, (((1,), (1,)), ((), ())), preferred_element_type=F32)


TAIL = 2


def own_cot_of(ref):
    return ref[...].astype(BF16)


def block_kernel(
    dims,
    video_h, sw_h, bias_h, tw_h, cot_h,
    out_v, gv_v, gt_v,
    video, cot, sw, tw, bias_ref, wp, wg, xcat, cb, chalo, cote, cotl, hb, cstash, hpack, hhalo, hstash, spat, gpad,
    gtl, rx, ysend, ry, psum, pb, rs, ag,
    load_sem, w_send, w_recv, halo_send, halo_recv, g_send, g_recv, a_send, a_recv, gate,
):
    n_tm, n_clip, height, width, chans, scale = dims
    rows = height * width
    depth = sw_h.shape[1]
    half = rows // 2
    quarter = rows // 4
    side_chans = chans // 2
    chunks = 4
    chunk = half // chunks
    low = depth - 16 * TAIL
    head = -(-chans // 128) * 128
    lanes = psum.shape[2]
    n_early = 2 * chans // lanes
    n_late = n_tm - n_early
    skip = n_late * lanes - chans
    tm = lax.axis_index("tm")
    c = lax.axis_index("clip")

    def flip(value, bit):
        return value + bit - 2 * bit * (lax.rem(value // bit, 2))

    core, ypart = flip(c, 1), flip(c, 2)
    xpart, zpart = flip(tm, 1), flip(tm, 2)
    parity = lax.rem(tm, 2)
    h = lax.rem(tm // 2, 2)
    yc = c // 2
    mine = lax.rem(c, 2)
    has_up, has_down = tm + 2 < n_tm, tm >= 2

    def signal(sem, device):
        pl.semaphore_signal(sem, inc=1, device_id=device, device_id_type=MESH)

    def tm_signals(sem):
        signal(sem, (xpart, c))

        @pl.when(has_up)
        def _():
            signal(sem, (tm + 2, c))

        @pl.when(has_down)
        def _():
            signal(sem, (tm - 2, c))

    def tm_waits(sem, extra):
        n_z, z = n_tm // 2, tm // 2
        ups, downs = (2 * n_z - 2 - z) // n_z, (z + n_z - 1) // n_z
        pl.semaphore_wait(sem, 1 + extra + ups + downs)

    rounds = n_tm // 2 - 1

    def gate_step(r):
        if r < rounds:
            tm_waits(gate.at[r], 0)
        if r + 1 < rounds:
            tm_signals(gate.at[r + 1])

    barrier = pltpu.get_barrier_semaphore()
    signal(barrier, (tm, ypart))
    signal(barrier, (tm, core))
    tm_signals(barrier)

    loads = [
        pltpu.make_async_copy(sw_h.at[pl.ds(0, 4)], sw.at[pl.ds(0, 4)], load_sem.at[0]),
        pltpu.make_async_copy(sw_h.at[pl.ds(4, 4)], sw.at[pl.ds(4, 4)], load_sem.at[0]),
        pltpu.make_async_copy(sw_h.at[pl.ds(8, 1)], sw.at[pl.ds(8, 1)], load_sem.at[5]),
        pltpu.make_async_copy(tw_h, tw, load_sem.at[1]),
        pltpu.make_async_copy(cot_h, cot, load_sem.at[2]),
        pltpu.make_async_copy(video_h, video, load_sem.at[3]),
        pltpu.make_async_copy(bias_h, bias_ref, load_sem.at[4]),
    ]
    for load in loads:
        load.start()

    def pack(value):
        return jnp.concatenate([value[:quarter], value[quarter:]], axis=1)

    def unpack(ref, slot):
        parts = []
        for q in range(2):
            both = ref[slot, q * quarter : (q + 1) * quarter]
            parts += [both[:, :chans], both[:, chans:]]
        return jnp.concatenate(parts, axis=0)

    pltpu.make_async_copy(sw_h.at[pl.ds(0, 8)], sw.at[pl.ds(0, 8)], load_sem.at[0]).wait()
    for pair in range(4):
        wp[c, pair] = jnp.concatenate([sw[2 * pair], sw[2 * pair + 1]], axis=1)
    tm_waits(barrier, 2)

    def send(src, dst, ssem, rsem, device):
        copy = pltpu.make_async_remote_copy(
            src_ref=src, dst_ref=dst, send_sem=ssem, recv_sem=rsem,
            device_id=device, device_id_type=MESH,
        )
        copy.start()
        return copy

    def settle(ref, ssem, rsem):
        return pltpu.make_async_remote_copy(
            src_ref=ref, dst_ref=ref, send_sem=ssem, recv_sem=rsem,
            device_id=(tm, core), device_id_type=MESH,
        )

    def sent(ref, sem):
        settle(ref, sem, sem).wait_send()

    def received(ref, sem):
        settle(ref, sem, sem).wait_recv()

    def block_rows(count):
        return chalo.at[0, pl.ds(0, count)]

    def wsend(slot, part, device):
        return send(part, part, w_send.at[0], w_recv.at[slot], device)

    def low_part(owner, pair):
        return wp.at[owner, pair, pl.ds(0, low)]

    def rest_part(owner):
        return wp.at[owner, pl.ds(0, 4), pl.ds(low, depth - low)]

    def head_part(owner):
        return wp.at[owner, 4, :, pl.ds(0, head)]

    def tail_part(owner):
        return wp.at[owner, 4, :, pl.ds(head, 2 * chans - head)]

    at_y, at_core, at_x, at_z = (tm, ypart), (tm, core), (xpart, c), (zpart, c)
    y_a = wsend(0, low_part(c, h), at_y)
    y_b = wsend(1, low_part(c, 2 + h), at_y)
    y_rest = wsend(2, rest_part(c), at_y)
    for load in loads[2:4]:
        load.wait()
    first = tw[0].astype(BF16)
    wp[c, 4] = jnp.concatenate([sw[8], first], axis=1)
    wp[c, 5] = jnp.concatenate([tw[1].astype(BF16), tw[2].astype(BF16)], axis=1)
    y_head = wsend(3, head_part(c), at_y)
    own = wsend(8, wp.at[c, pl.ds(0, 5)], at_core)
    tm_signals(gate.at[0])

    loads[4].wait()
    own_cot = cot[...].astype(BF16)
    for q in range(2):
        cb[q * quarter : (q + 1) * quarter] = pack(own_cot[q * half : (q + 1) * half])

    def near_send(which, own_ref, halo, q):
        part = pl.ds(q * chunk, chunk)
        return send(
            own_ref.at[part, :], halo.at[parity, part, :],
            halo_send.at[which], halo_recv.at[3 * which + min(q, 2)], (xpart, c),
        )

    def far_copy(which, halo, q):
        target = lax.rem(tm + n_tm + 2 - 4 * parity, n_tm)
        part = pl.ds(q * chunk, chunk)
        return pltpu.make_async_remote_copy(
            src_ref=halo.at[1 - parity, part, :],
            dst_ref=halo.at[parity, part, :],
            send_sem=halo_send.at[2],
            recv_sem=halo_recv.at[6 + which],
            device_id=(target, c),
            device_id_type=MESH,
        )

    sends_far = jnp.logical_or(
        jnp.logical_and(parity == 0, has_up), jnp.logical_and(parity == 1, has_down)
    )
    gets_far = jnp.logical_or(
        jnp.logical_and(parity == 0, has_down), jnp.logical_and(parity == 1, has_up)
    )

    def far_start(which, halo, q):
        @pl.when(sends_far)
        def _():
            far_copy(which, halo, q).start()

    def far_recv(which):
        @pl.when(gets_far)
        def _():
            received(block_rows(half), halo_recv.at[6 + which])

    def stash_start(which, own_ref, held):
        @pl.when(gets_far)
        def _():
            for q in range(2, chunks):
                part = pl.ds(q * chunk, chunk)
                pltpu.make_async_remote_copy(
                    src_ref=own_ref.at[part, :], dst_ref=held.at[part, :],
                    send_sem=halo_send.at[3], recv_sem=halo_recv.at[8 + which],
                    device_id=(lax.rem(tm + n_tm + 4 * parity - 2, n_tm), c), device_id_type=MESH,
                ).start()

    def forward(which, held, halo):
        @pl.when(sends_far)
        def _():
            received(block_rows(2 * chunk), halo_recv.at[8 + which])
            for q in range(2, chunks):
                part = pl.ds(q * chunk, chunk)
                pltpu.make_async_remote_copy(
                    src_ref=held.at[part, :], dst_ref=halo.at[1 - parity, part, :],
                    send_sem=halo_send.at[2], recv_sem=halo_recv.at[6 + which],
                    device_id=at_x, device_id_type=MESH,
                ).start()

    cot_near = [near_send(0, cb, chalo, q) for q in range(chunks)]
    stash_start(0, cb, cstash)

    for edge, slot in ((0, 0), (n_tm - 1, 1)):
        @pl.when(tm == edge)
        def _():
            chalo[slot] = jnp.zeros((half, 2 * chans), BF16)
            hhalo[slot] = jnp.zeros((half, 2 * chans), BF16)

    column = lax.rem(lax.broadcasted_iota(jnp.int32, (rows, chans), 0), width)

    def shifted(value, step):
        if step == 0:
            return value
        rolled = pltpu.roll(value, step % rows, 0)
        return jnp.where(column == (0 if step == 1 else width - 1), 0.0, rolled)

    for s in range(2):
        xcat[s, 0:width] = jnp.zeros((width, 3 * side_chans), BF16)
        xcat[s, width + rows :] = jnp.zeros((width, 3 * side_chans), BF16)
    for b in range(3):
        gpad[b, 0:width] = jnp.zeros((width, chans), BF16)
        gpad[b, width + rows :] = jnp.zeros((width, chans), BF16)
    loads[5].wait()
    loads[6].wait()
    frame = video[...]
    views = [shifted(frame, 1 - b).astype(BF16) for b in range(3)]
    for s in range(2):
        xcat[s, width : width + rows] = jnp.concatenate(
            [view[:, s * side_chans : (s + 1) * side_chans] for view in views], axis=1
        )

    def unpack_pair(owner, pair, taps=(0, 1)):
        both = wp[owner, pair] if 1 in taps else wp[owner, pair, :, 0:head]
        band = pl.ds(pl.multiple_of(owner * depth, 16), depth)
        for e in taps:
            wg[2 * pair + e, band] = both[:, e * chans : (e + 1) * chans]

    def unpack_spatial(owner, first=0, count=5):
        for pair in range(first, first + count):
            unpack_pair(owner, pair, (0, 1) if pair < 4 else (0,))

    def conv_part(s, q, taps=(0, 1, 2)):
        total = None
        for a in taps:
            band = pl.ds(pl.multiple_of(s * side_chans, 16), side_chans)
            weights = jnp.concatenate([wg[3 * a + b, band] for b in range(3)], axis=0)
            term = nn_dot(
                xcat[s, a * width + q * half : a * width + (q + 1) * half], weights
            )
            total = term if total is None else total + term
        return total

    unpack_spatial(c)

    @pl.when(parity == 0)
    def _():
        cote[:, chans : 2 * chans] = own_cot_of(cot)
        cotl[:, chans:] = jnp.zeros((rows, skip), BF16)

    @pl.when(parity == 1)
    def _():
        middle = own_cot_of(cot)
        cote[:, 0 : chans - skip] = middle[:, skip:]
        cote[:, 2 * chans - skip :] = jnp.zeros((rows, skip), BF16)
        cotl[:, chans:] = middle[:, :skip]

    own.wait_recv()
    unpack_spatial(core)
    for q in range(2):
        spat[q * half : (q + 1) * half] = bias_ref[...].reshape(1, chans) + conv_part(yc, q)

    y_a.wait_recv()
    z_a = wsend(6, low_part(ypart, h), at_z)
    wsend(9, low_part(ypart, h), at_core)
    y_b.wait_recv()
    z_b = wsend(7, low_part(ypart, 2 + h), at_z)
    wsend(10, low_part(ypart, 2 + h), at_core)
    gate_step(0)
    y_rest.wait_recv()
    wsend(9, rest_part(ypart), at_core)
    forward(0, cstash, chalo)
    z_a.wait_recv()
    wsend(9, low_part(ypart, 1 - h), at_core)
    gate_step(1)
    diagonal = flip(core, 2)
    head_rows = depth * head // (2 * chans)

    def later(slot, part):
        return pltpu.make_async_remote_copy(
            src_ref=part, dst_ref=part, send_sem=w_send.at[0], recv_sem=w_recv.at[slot],
            device_id=at_y, device_id_type=MESH,
        )

    y_tail, y_last = later(4, tail_part(c)), later(5, wp.at[c, 5])

    def pass_head(which):
        @pl.when(mine == which)
        def _():
            y_head.wait_recv()
            wsend(12, head_part(ypart), at_core)
            y_tail.start()
            y_last.start()

    pass_head(1)
    z_b.wait_recv()
    wsend(10, low_part(ypart, 3 - h), at_core)
    for q in range(2):
        cot_near[q].wait_recv()
        far_start(0, chalo, q)
    unpack_spatial(ypart, 0, 4)
    received(block_rows(4 * depth - 2 * low), w_recv.at[9])
    received(block_rows(2 * low), w_recv.at[10])
    unpack_spatial(diagonal, 0, 4)
    pass_head(0)
    for q in range(2):
        part = pl.ds(q * half, half)
        spat[part] = spat[part] + conv_part(1 - yc, q, (0, 1))
    wsend(11, wp.at[c, 5], at_core)
    unpack_spatial(ypart, 4, 1)
    received(block_rows(2 * chunk), halo_recv.at[2])

    @pl.when(parity == 0)
    def _():
        cote[:, 0:chans] = unpack(chalo, 1)

    @pl.when(parity == 1)
    def _():
        cote[:, chans - skip : 2 * chans - skip] = unpack(chalo, 0)

    received(block_rows(head_rows), w_recv.at[12])
    unpack_spatial(diagonal, 4, 1)

    hid_near = []
    for q in range(2):
        acc = spat[q * half : (q + 1) * half] + conv_part(1 - yc, q, (2,))
        hidden = (acc * jax.nn.sigmoid(acc)).astype(BF16)
        hb[q * half : (q + 1) * half] = hidden
        hpack[q * quarter : (q + 1) * quarter] = pack(hidden)
        hid_near += [near_send(1, hpack, hhalo, 2 * q + e) for e in range(2)]
        if q == 1:
            stash_start(1, hpack, hstash)
        spat[q * half : (q + 1) * half] = acc

    early = (n_tm - n_early) * parity
    late = n_early * (1 - parity)

    def place(products, first, count):
        for i in range(count):
            for owner in range(n_clip):
                gtl[owner % 2, owner // 2, first + i] = products[
                    owner * depth : (owner + 1) * depth, i * lanes : (i + 1) * lanes
                ]

    def core_send(slot, side, first, count):
        part = pl.ds(first, count)
        return send(
            gtl.at[1 - mine, side, part], rx.at[side, part],
            g_send.at[0], g_recv.at[slot], at_core,
        )

    def y_send(slot, first, count):
        for i in range(count):
            ysend[first + i] = (gtl[mine, 1 - yc, first + i] + rx[1 - yc, first + i]).astype(BF16)
        part = pl.ds(first, count)
        return send(ysend.at[part], ry.at[part], g_send.at[1], g_recv.at[slot], at_y)

    share = n_tm // 4
    first_owner = n_tm // 2 - 2
    owns = jnp.logical_and(tm >= first_owner, tm < first_owner + 4)

    def scatter_copy(unit):
        place_in = lax.rem(unit, share)
        return pltpu.make_async_remote_copy(
            src_ref=pb.at[unit], dst_ref=rs.at[tm, place_in],
            send_sem=a_send.at[0], recv_sem=a_recv.at[0],
            device_id=(first_owner + unit // share, c), device_id_type=MESH,
        )

    def gather_copy(owner, to):
        part = ag.at[pl.ds(owner * share, share)]
        return pltpu.make_async_remote_copy(
            src_ref=part, dst_ref=part,
            send_sem=a_send.at[1], recv_sem=a_recv.at[1],
            device_id=(to, c), device_id_type=MESH,
        )

    def scatter(first, count):
        for i in range(count):
            to = first + i
            part = gtl[mine, yc, to] + rx[yc, to] + ry[to].astype(F32)
            psum[to] = part
            pb[to] = part.astype(BF16)

            @pl.when(tm != first_owner + to // share)
            def _():
                scatter_copy(to).start()

    def pass_hidden(q):
        hid_near[q].wait_recv()
        far_start(1, hhalo, q)

    place(outer_dot(hb[...], cote[...]), early, n_early)
    core_e = [core_send(e, side, early, n_early) for e, side in enumerate((1 - yc, yc))]
    core_e[0].wait_recv()
    y_e = y_send(4, early, n_early)

    far_recv(0)
    cotl[:, 0:chans] = unpack(chalo, parity)
    place(outer_dot(hb[...], cotl[...]), late, n_late)
    core_l = [core_send(2 + e, side, late, n_late) for e, side in enumerate((1 - yc, yc))]

    y_tail.wait_recv()
    wsend(11, tail_part(ypart), at_core)
    y_last.wait_recv()
    wsend(11, wp.at[ypart, 5], at_core)
    core_l[0].wait_recv()
    y_l = y_send(5, late, n_late)
    pass_hidden(0)

    received(block_rows(3 * depth - head_rows), w_recv.at[11])
    for owner in range(n_clip):
        unpack_pair(owner, 4, (1,))
        unpack_pair(owner, 5)
    grad_h = transpose_dot(unpack(chalo, 1), wg[9])
    grad_h = grad_h + transpose_dot(cot[...].astype(BF16), wg[10])
    grad_h = grad_h + transpose_dot(unpack(chalo, 0), wg[11])
    acc = spat[...]
    sig = jax.nn.sigmoid(acc)
    grad_s = grad_h * (sig * (1.0 + acc * (1.0 - sig)))
    for b in range(3):
        gpad[b, width : width + rows] = shifted(grad_s, b - 1).astype(BF16)

    for r in range(2, rounds):
        gate_step(r)
    core_e[1].wait_recv()
    y_e.wait_recv()
    scatter(early, n_early)

    def grad_conv(q):
        acc = cot[q * half : (q + 1) * half]
        for a in range(3):
            start = (2 - a) * width + q * half
            for b in range(3):
                acc = acc + transpose_dot(gpad[b, start : start + half], wg[3 * a + b])
        gv_v[q * half : (q + 1) * half] = acc

    core_l[1].wait_recv()
    y_l.wait_recv()
    scatter(late, n_late)
    grad_conv(0)
    pass_hidden(1)
    grad_conv(1)
    forward(1, hstash, hhalo)
    out_v[...] = video[...] + nn_dot(hb[...], wg[10])

    @pl.when(owns)
    def _():
        mine_at = tm - first_owner
        rs[tm] = jnp.zeros(rs.shape[1:], BF16)
        received(rs.at[pl.ds(0, n_tm - 1)], a_recv.at[0])
        for e in range(share):
            total = psum[mine_at * share + e]
            for sender in range(n_tm):
                total = total + rs[sender, e].astype(F32)
            ag[mine_at * share + e] = total.astype(BF16)
        for to in (0, 1, n_tm - 2, n_tm - 1, *range(2, n_tm - 2)):
            @pl.when(tm != to)
            def _():
                gather_copy(mine_at, to).start()

    received(block_rows(2 * chunk), halo_recv.at[5])
    out_v[...] = out_v[...] + nn_dot(unpack(hhalo, 1 - parity), wg[11 - 2 * parity])
    far_recv(1)
    out_v[...] = out_v[...] + nn_dot(unpack(hhalo, parity), wg[9 + 2 * parity])

    @pl.when(owns)
    def _():
        received(ag.at[pl.ds(0, 3 * share)], a_recv.at[1])

    @pl.when(jnp.logical_not(owns))
    def _():
        received(ag, a_recv.at[1])

    whole = jnp.concatenate([ag[to] for to in range(n_tm)], axis=1).astype(F32) * scale
    for k in range(3):
        gt_v[k] = whole[:, k * chans : (k + 1) * chans]

    sent(wp.at[pl.ds(0, 3)], w_send.at[0])
    sent(block_rows(half), halo_send.at[0])
    sent(block_rows(half), halo_send.at[1])
    sent(gtl.at[0], g_send.at[0])
    sent(ysend, g_send.at[1])

    @pl.when(sends_far)
    def _():
        sent(chalo, halo_send.at[2])

    @pl.when(gets_far)
    def _():
        sent(block_rows(half), halo_send.at[3])

    @pl.when(owns)
    def _():
        sent(pb.at[pl.ds(0, n_tm - share)], a_send.at[0])
        sent(rs.at[pl.ds(0, n_tm - 1)], a_send.at[1])

    @pl.when(jnp.logical_not(owns))
    def _():
        sent(pb, a_send.at[0])


def hand_over(*refs):
    n = len(refs) // 2
    ins, outs, sem = refs[:n], refs[n : 2 * n], refs[2 * n]
    writes = []
    for e in range(n):
        writes.append(pltpu.make_async_copy(ins[e], outs[e], sem.at[e]))
    for write in writes:
        write.start()
    for write in writes:
        write.wait()


def fused(n_tm, n_clip, video, spatial_w, spatial_b, temporal_w, cotangent):
    clips, frames, height, width, chans = video.shape
    rows = height * width
    depth = spatial_w.shape[1]
    lanes = -(-3 * chans // (128 * n_tm)) * 128
    scale = 1.0 / math.sqrt(rows * n_tm * n_clip)
    any_spec = pl.BlockSpec(memory_space=pltpu.HBM)
    vm_spec = pl.BlockSpec(memory_space=pltpu.VMEM)
    vm = pltpu.VMEM
    dma = pltpu.SemaphoreType.DMA
    results = pl.pallas_call(
        functools.partial(block_kernel, (n_tm, n_clip, height, width, chans, scale)),
        out_shape=(
            vm((rows, chans), F32),
            vm((rows, chans), F32),
            vm((3, depth, chans), F32),
        ),
        in_specs=[any_spec, any_spec, any_spec, any_spec, any_spec],
        out_specs=(vm_spec, vm_spec, vm_spec),
        scratch_shapes=[
            vm((rows, chans), F32),
            vm((rows, chans), F32),
            vm((9, depth, chans), BF16),
            vm((3, depth, chans), F32),
            vm((chans,), F32),
            vm((n_clip, 6, depth, 2 * chans), BF16),
            vm((12, chans, chans), BF16),
            vm((2, rows + 2 * width, 3 * chans // 2), BF16),
            vm((rows // 2, 2 * chans), BF16),
            vm((2, rows // 2, 2 * chans), BF16),
            vm((rows, 2 * chans), BF16),
            vm((rows, n_tm * lanes - 2 * chans), BF16),
            vm((rows, chans), BF16),
            vm((rows // 2, 2 * chans), BF16),
            vm((rows // 2, 2 * chans), BF16),
            vm((2, rows // 2, 2 * chans), BF16),
            vm((rows // 2, 2 * chans), BF16),
            vm((rows, chans), F32),
            vm((3, rows + 2 * width, chans), BF16),
            vm((2, 2, n_tm, depth, lanes), F32),
            vm((2, n_tm, depth, lanes), F32),
            vm((n_tm, depth, lanes), BF16),
            vm((n_tm, depth, lanes), BF16),
            vm((n_tm, depth, lanes), F32),
            vm((n_tm, depth, lanes), BF16),
            vm((n_tm, n_tm // 4, depth, lanes), BF16),
            vm((n_tm, depth, lanes), BF16),
            dma((6,)),
            dma((1,)),
            dma((13,)),
            dma((4,)),
            dma((10,)),
            dma((2,)),
            dma((6,)),
            dma((2,)),
            dma((2,)),
            pltpu.SemaphoreType.REGULAR((n_tm // 2 - 1,)),
        ],
        compiler_params=pltpu.CompilerParams(
            collective_id=0, has_side_effects=True, vmem_limit_bytes=65_000_000
        ),
        name="block",
    )(
        video.reshape(rows, chans), spatial_w, spatial_b, temporal_w,
        cotangent.reshape(rows, chans),
    )
    shapes = tuple(jax.ShapeDtypeStruct(array.shape, F32) for array in results)

    out, gv, gt = pl.pallas_call(
        hand_over,
        out_shape=shapes,
        in_specs=[vm_spec] * 3,
        out_specs=(any_spec,) * 3,
        scratch_shapes=[dma((3,))],
        compiler_params=pltpu.CompilerParams(vmem_limit_bytes=2**20),
        name="hand_over",
    )(*results)
    return out.reshape(video.shape), gv.reshape(video.shape), gt


def padded_2(cells, sides, width):
    for axis, dim in sides:
        count = lax.axis_size(axis)
        ends = count - 1
        head = lax.slice_in_dim(cells, 0, width, axis=dim)
        tail = lax.slice_in_dim(cells, cells.shape[dim] - width, cells.shape[dim], axis=dim)
        cells = jnp.concatenate(
            [
                lax.ppermute(tail, axis, [(i, (i + 1) % count) for i in range(ends)]),
                cells,
                lax.ppermute(head, axis, [((i + 1) % count, i) for i in range(ends)]),
            ],
            axis=dim,
        )
    return cells


def native(video, spatial_w, spatial_b, temporal_w, cotangent):
    clips, frames, height, width, chans = video.shape
    row_count = clips * frames * height * width
    pads = ((0, 0), (0, 0), (1, 1), (1, 1), (0, 0))
    padded = jnp.pad(video.astype(BF16), pads)
    temporal_b = temporal_w.astype(BF16)
    spatial_all = lax.all_gather(spatial_w, "clip", axis=1, tiled=True)
    temporal_all = lax.all_gather(temporal_b, "clip", axis=1, tiled=True)
    spatial = jnp.zeros((row_count, chans), F32)
    for y in range(3):
        for x in range(3):
            window = padded[:, :, y : y + height, x : x + width, :].reshape(row_count, chans)
            spatial = spatial + nn_dot(window, spatial_all[3 * y + x])
    spatial = spatial + spatial_b
    sigmoid_s = jax.nn.sigmoid(spatial)
    hidden = (spatial * sigmoid_s).astype(BF16).reshape(video.shape)
    hidden_pad = padded_2(hidden, (("tm", 1),), 1)
    cot_b = cotangent.astype(BF16)
    cot_flat = cot_b.reshape(row_count, chans)
    cot_pad = padded_2(cot_b, (("tm", 1),), 1)
    temporal = jnp.zeros((row_count, chans), F32)
    grad_hidden = jnp.zeros((row_count, chans), F32)
    grads = []
    for k in range(3):
        shifted_hid = hidden_pad[:, k : k + frames].reshape(row_count, chans)
        temporal = temporal + nn_dot(shifted_hid, temporal_all[k])
        shifted_cot = cot_pad[:, 2 - k : 2 - k + frames].reshape(row_count, chans)
        grad_hidden = grad_hidden + transpose_dot(shifted_cot, temporal_all[k])
        grads.append(outer_dot(shifted_hid, cot_flat))
    total_rows = row_count * lax.axis_size("tm") * lax.axis_size("clip")
    summed = lax.psum(jnp.stack(grads), "tm")
    owned = lax.psum_scatter(summed, "clip", scatter_dimension=1, tiled=True)
    grad_spatial = (grad_hidden * sigmoid_s * (1.0 + spatial * (1.0 - sigmoid_s))).astype(BF16)
    grad_frames = jnp.pad(grad_spatial.reshape(video.shape), pads)
    grad_acc = cotangent.reshape(row_count, chans)
    for y in range(3):
        for x in range(3):
            window = grad_frames[:, :, 2 - y : 2 - y + height, 2 - x : 2 - x + width, :]
            window = window.reshape(row_count, chans)
            grad_acc = grad_acc + transpose_dot(window, spatial_all[3 * y + x])
    return (
        video + temporal.reshape(video.shape),
        grad_acc.reshape(video.shape),
        owned * (1.0 / math.sqrt(total_rows)),
    )


def solution(mesh):
    n_tm, n_clip = mesh.shape["tm"], mesh.shape["clip"]

    def on_device(video, spatial_w, spatial_b, temporal_w, cotangent):
        args = (video, spatial_w, spatial_b, temporal_w, cotangent)
        one_frame = video.shape[0] == 1 and video.shape[1] == 1
        depth, chans = spatial_w.shape[1:]
        lanes = -(-3 * chans // (128 * n_tm)) * 128
        whole_rows = depth * (-(-chans // 128) * 128) % (2 * chans) == 0
        fits = depth % 16 == 0 and depth > 16 * TAIL and 2 * chans % lanes == 0
        if one_frame and fits and n_clip == 4 and n_tm % 4 == 0 and n_tm * lanes <= 4 * chans and whole_rows:
            return fused(n_tm, n_clip, *args)
        return native(*args)

    return jax.shard_map(
        on_device,
        mesh=mesh,
        in_specs=(
            P("clip", "tm", None, None, None),
            P(None, "clip", None),
            P(),
            P(None, "clip", None),
            P("clip", "tm", None, None, None),
        ),
        out_specs=(
            P("clip", "tm", None, None, None),
            P("clip", "tm", None, None, None),
            P(None, "clip", None),
        ),
        check_vma=False,
    )
```

```python
import functools
import math

import jax
import jax.numpy as jnp
from jax import lax
from jax.experimental import pallas as pl
from jax.experimental.pallas import tpu as pltpu
from jax.sharding import PartitionSpec as P

F32 = jnp.float32
BF16 = jnp.bfloat16
MESH = pl.DeviceIdType.MESH


def nn_dot(left, right):
    return lax.dot_general(left, right, (((1,), (0,)), ((), ())), preferred_element_type=F32)


def outer_dot(left, right):
    return lax.dot_general(left, right, (((0,), (0,)), ((), ())), preferred_element_type=F32)


def transpose_dot(left, right):
    return lax.dot_general(left, right, (((1,), (1,)), ((), ())), preferred_element_type=F32)


TAIL = 2


def own_cot_of(ref):
    return ref[...].astype(BF16)


def block_kernel(
    dims,
    video_h, sw_h, bias_h, tw_h, cot_h,
    out_v, gv_v, gt_v,
    video, cot, sw, tw, bias_ref, wp, wg, xcat, cb, chalo, cote, cotl, hb, cstash, hpack, hhalo, hstash, spat, gpad,
    gtl, rx, ysend, ry, psum, pb, rs, ag,
    load_sem, w_send, w_recv, halo_send, halo_recv, g_send, g_recv, a_send, a_recv, gate,
):
    n_tm, n_clip, height, width, chans, scale = dims
    rows = height * width
    depth = sw_h.shape[1]
    half = rows // 2
    quarter = rows // 4
    side_chans = chans // 2
    chunks = 4
    chunk = half // chunks
    low = depth - 16 * TAIL
    head = -(-chans // 128) * 128
    lanes = psum.shape[2]
    n_early = 2 * chans // lanes
    n_late = n_tm - n_early
    skip = n_late * lanes - chans
    tm = lax.axis_index("tm")
    c = lax.axis_index("clip")

    def flip(value, bit):
        return value + bit - 2 * bit * (lax.rem(value // bit, 2))

    core, ypart = flip(c, 1), flip(c, 2)
    xpart, zpart = flip(tm, 1), flip(tm, 2)
    parity = lax.rem(tm, 2)
    h = lax.rem(tm // 2, 2)
    yc = c // 2
    mine = lax.rem(c, 2)
    has_up, has_down = tm + 2 < n_tm, tm >= 2

    def signal(sem, device):
        pl.semaphore_signal(sem, inc=1, device_id=device, device_id_type=MESH)

    def tm_signals(sem):
        signal(sem, (xpart, c))

        @pl.when(has_up)
        def _():
            signal(sem, (tm + 2, c))

        @pl.when(has_down)
        def _():
            signal(sem, (tm - 2, c))

    def tm_waits(sem, extra):
        n_z, z = n_tm // 2, tm // 2
        ups, downs = (2 * n_z - 2 - z) // n_z, (z + n_z - 1) // n_z
        pl.semaphore_wait(sem, 1 + extra + ups + downs)

    rounds = n_tm // 2 - 1

    def gate_step(r):
        if r < rounds:
            tm_waits(gate.at[r], 0)
        if r + 1 < rounds:
            tm_signals(gate.at[r + 1])

    loads = [
        pltpu.make_async_copy(sw_h.at[pl.ds(0, 4)], sw.at[pl.ds(0, 4)], load_sem.at[0]),
        pltpu.make_async_copy(sw_h.at[pl.ds(4, 4)], sw.at[pl.ds(4, 4)], load_sem.at[0]),
        pltpu.make_async_copy(sw_h.at[pl.ds(8, 1)], sw.at[pl.ds(8, 1)], load_sem.at[5]),
        pltpu.make_async_copy(tw_h, tw, load_sem.at[1]),
        pltpu.make_async_copy(cot_h, cot, load_sem.at[2]),
        pltpu.make_async_copy(video_h, video, load_sem.at[3]),
        pltpu.make_async_copy(bias_h, bias_ref, load_sem.at[4]),
    ]
    for load in loads:
        load.start()

    barrier = pltpu.get_barrier_semaphore()
    signal(barrier, (tm, ypart))
    signal(barrier, (tm, core))
    tm_signals(barrier)

    def pack(value):
        return jnp.concatenate([value[:quarter], value[quarter:]], axis=1)

    def unpack(ref, slot):
        parts = []
        for q in range(2):
            both = ref[slot, q * quarter : (q + 1) * quarter]
            parts += [both[:, :chans], both[:, chans:]]
        return jnp.concatenate(parts, axis=0)

    pltpu.make_async_copy(sw_h.at[pl.ds(0, 8)], sw.at[pl.ds(0, 8)], load_sem.at[0]).wait()
    for pair in range(4):
        wp[c, pair] = jnp.concatenate([sw[2 * pair], sw[2 * pair + 1]], axis=1)
    tm_waits(barrier, 2)

    def send(src, dst, ssem, rsem, device):
        copy = pltpu.make_async_remote_copy(
            src_ref=src, dst_ref=dst, send_sem=ssem, recv_sem=rsem,
            device_id=device, device_id_type=MESH,
        )
        copy.start()
        return copy

    def settle(ref, ssem, rsem):
        return pltpu.make_async_remote_copy(
            src_ref=ref, dst_ref=ref, send_sem=ssem, recv_sem=rsem,
            device_id=(tm, core), device_id_type=MESH,
        )

    def sent(ref, sem):
        settle(ref, sem, sem).wait_send()

    def received(ref, sem):
        settle(ref, sem, sem).wait_recv()

    def block_rows(count):
        return chalo.at[0, pl.ds(0, count)]

    def wsend(slot, part, device):
        return send(part, part, w_send.at[0], w_recv.at[slot], device)

    def low_part(owner, pair):
        return wp.at[owner, pair, pl.ds(0, low)]

    def rest_part(owner):
        return wp.at[owner, pl.ds(0, 4), pl.ds(low, depth - low)]

    def head_part(owner):
        return wp.at[owner, 4, :, pl.ds(0, head)]

    def tail_part(owner):
        return wp.at[owner, 4, :, pl.ds(head, 2 * chans - head)]

    at_y, at_core, at_x, at_z = (tm, ypart), (tm, core), (xpart, c), (zpart, c)
    y_a = wsend(0, low_part(c, h), at_y)
    y_b = wsend(1, low_part(c, 2 + h), at_y)
    y_rest = wsend(2, rest_part(c), at_y)
    for load in loads[2:4]:
        load.wait()
    first = tw[0].astype(BF16)
    wp[c, 4] = jnp.concatenate([sw[8], first], axis=1)
    wp[c, 5] = jnp.concatenate([tw[1].astype(BF16), tw[2].astype(BF16)], axis=1)
    y_head = wsend(3, head_part(c), at_y)
    own = wsend(8, wp.at[c, pl.ds(0, 5)], at_core)
    tm_signals(gate.at[0])

    loads[4].wait()
    own_cot = cot[...].astype(BF16)
    for q in range(2):
        cb[q * quarter : (q + 1) * quarter] = pack(own_cot[q * half : (q + 1) * half])

    def near_send(which, own_ref, halo, q):
        part = pl.ds(q * chunk, chunk)
        return send(
            own_ref.at[part, :], halo.at[parity, part, :],
            halo_send.at[which], halo_recv.at[3 * which + min(q, 2)], (xpart, c),
        )

    def far_copy(which, halo, q):
        target = lax.rem(tm + n_tm + 2 - 4 * parity, n_tm)
        part = pl.ds(q * chunk, chunk)
        return pltpu.make_async_remote_copy(
            src_ref=halo.at[1 - parity, part, :],
            dst_ref=halo.at[parity, part, :],
            send_sem=halo_send.at[2],
            recv_sem=halo_recv.at[6 + which],
            device_id=(target, c),
            device_id_type=MESH,
        )

    sends_far = jnp.logical_or(
        jnp.logical_and(parity == 0, has_up), jnp.logical_and(parity == 1, has_down)
    )
    gets_far = jnp.logical_or(
        jnp.logical_and(parity == 0, has_down), jnp.logical_and(parity == 1, has_up)
    )

    def far_start(which, halo, q):
        @pl.when(sends_far)
        def _():
            far_copy(which, halo, q).start()

    def far_recv(which):
        @pl.when(gets_far)
        def _():
            received(block_rows(half), halo_recv.at[6 + which])

    def stash_start(which, own_ref, held):
        @pl.when(gets_far)
        def _():
            for q in range(2, chunks):
                part = pl.ds(q * chunk, chunk)
                pltpu.make_async_remote_copy(
                    src_ref=own_ref.at[part, :], dst_ref=held.at[part, :],
                    send_sem=halo_send.at[3], recv_sem=halo_recv.at[8 + which],
                    device_id=(lax.rem(tm + n_tm + 4 * parity - 2, n_tm), c), device_id_type=MESH,
                ).start()

    def forward(which, held, halo):
        @pl.when(sends_far)
        def _():
            received(block_rows(2 * chunk), halo_recv.at[8 + which])
            for q in range(2, chunks):
                part = pl.ds(q * chunk, chunk)
                pltpu.make_async_remote_copy(
                    src_ref=held.at[part, :], dst_ref=halo.at[1 - parity, part, :],
                    send_sem=halo_send.at[2], recv_sem=halo_recv.at[6 + which],
                    device_id=at_x, device_id_type=MESH,
                ).start()

    cot_near = [near_send(0, cb, chalo, q) for q in range(chunks)]
    stash_start(0, cb, cstash)

    for edge, slot in ((0, 0), (n_tm - 1, 1)):
        @pl.when(tm == edge)
        def _():
            chalo[slot] = jnp.zeros((half, 2 * chans), BF16)
            hhalo[slot] = jnp.zeros((half, 2 * chans), BF16)

    column = lax.rem(lax.broadcasted_iota(jnp.int32, (rows, chans), 0), width)

    def shifted(value, step):
        if step == 0:
            return value
        rolled = pltpu.roll(value, step % rows, 0)
        return jnp.where(column == (0 if step == 1 else width - 1), 0.0, rolled)

    for s in range(2):
        xcat[s, 0:width] = jnp.zeros((width, 3 * side_chans), BF16)
        xcat[s, width + rows :] = jnp.zeros((width, 3 * side_chans), BF16)
    for b in range(3):
        gpad[b, 0:width] = jnp.zeros((width, chans), BF16)
        gpad[b, width + rows :] = jnp.zeros((width, chans), BF16)
    loads[5].wait()
    loads[6].wait()
    frame = video[...]
    views = [shifted(frame, 1 - b).astype(BF16) for b in range(3)]
    for s in range(2):
        xcat[s, width : width + rows] = jnp.concatenate(
            [view[:, s * side_chans : (s + 1) * side_chans] for view in views], axis=1
        )

    def unpack_pair(owner, pair, taps=(0, 1)):
        both = wp[owner, pair] if 1 in taps else wp[owner, pair, :, 0:head]
        band = pl.ds(pl.multiple_of(owner * depth, 16), depth)
        for e in taps:
            wg[2 * pair + e, band] = both[:, e * chans : (e + 1) * chans]

    def unpack_spatial(owner, first=0, count=5):
        for pair in range(first, first + count):
            unpack_pair(owner, pair, (0, 1) if pair < 4 else (0,))

    def conv_part(s, q, taps=(0, 1, 2)):
        total = None
        for a in taps:
            band = pl.ds(pl.multiple_of(s * side_chans, 16), side_chans)
            weights = jnp.concatenate([wg[3 * a + b, band] for b in range(3)], axis=0)
            term = nn_dot(
                xcat[s, a * width + q * half : a * width + (q + 1) * half], weights
            )
            total = term if total is None else total + term
        return total

    unpack_spatial(c)

    @pl.when(parity == 0)
    def _():
        cote[:, chans : 2 * chans] = own_cot_of(cot)
        cotl[:, chans:] = jnp.zeros((rows, skip), BF16)

    @pl.when(parity == 1)
    def _():
        middle = own_cot_of(cot)
        cote[:, 0 : chans - skip] = middle[:, skip:]
        cote[:, 2 * chans - skip :] = jnp.zeros((rows, skip), BF16)
        cotl[:, chans:] = middle[:, :skip]

    own.wait_recv()
    unpack_spatial(core)
    for q in range(2):
        spat[q * half : (q + 1) * half] = bias_ref[...].reshape(1, chans) + conv_part(yc, q)

    y_a.wait_recv()
    z_a = wsend(6, low_part(ypart, h), at_z)
    wsend(9, low_part(ypart, h), at_core)
    y_b.wait_recv()
    z_b = wsend(7, low_part(ypart, 2 + h), at_z)
    wsend(10, low_part(ypart, 2 + h), at_core)
    gate_step(0)
    y_rest.wait_recv()
    wsend(9, rest_part(ypart), at_core)
    forward(0, cstash, chalo)
    z_a.wait_recv()
    wsend(9, low_part(ypart, 1 - h), at_core)
    gate_step(1)
    diagonal = flip(core, 2)
    head_rows = depth * head // (2 * chans)

    def later(slot, part):
        return pltpu.make_async_remote_copy(
            src_ref=part, dst_ref=part, send_sem=w_send.at[0], recv_sem=w_recv.at[slot],
            device_id=at_y, device_id_type=MESH,
        )

    y_tail, y_last = later(4, tail_part(c)), later(5, wp.at[c, 5])

    def pass_head(which):
        @pl.when(mine == which)
        def _():
            y_head.wait_recv()
            wsend(12, head_part(ypart), at_core)
            y_tail.start()
            y_last.start()

    pass_head(1)
    z_b.wait_recv()
    wsend(10, low_part(ypart, 3 - h), at_core)
    for q in range(2):
        cot_near[q].wait_recv()
        far_start(0, chalo, q)
    unpack_spatial(ypart, 0, 4)
    received(block_rows(4 * depth - 2 * low), w_recv.at[9])
    received(block_rows(2 * low), w_recv.at[10])
    unpack_spatial(diagonal, 0, 4)
    pass_head(0)
    for q in range(2):
        part = pl.ds(q * half, half)
        spat[part] = spat[part] + conv_part(1 - yc, q, (0, 1))
    wsend(11, wp.at[c, 5], at_core)
    unpack_spatial(ypart, 4, 1)
    received(block_rows(head_rows), w_recv.at[12])
    unpack_spatial(diagonal, 4, 1)

    hid_near = []
    for q in range(2):
        acc = spat[q * half : (q + 1) * half] + conv_part(1 - yc, q, (2,))
        hidden = (acc * jax.nn.sigmoid(acc)).astype(BF16)
        hb[q * half : (q + 1) * half] = hidden
        hpack[q * quarter : (q + 1) * quarter] = pack(hidden)
        hid_near += [near_send(1, hpack, hhalo, 2 * q + e) for e in range(2)]
        if q == 1:
            stash_start(1, hpack, hstash)
        spat[q * half : (q + 1) * half] = acc
    received(block_rows(2 * chunk), halo_recv.at[2])

    early = (n_tm - n_early) * parity
    late = n_early * (1 - parity)

    def place(products, first, count):
        for i in range(count):
            for owner in range(n_clip):
                gtl[owner % 2, owner // 2, first + i] = products[
                    owner * depth : (owner + 1) * depth, i * lanes : (i + 1) * lanes
                ]

    def core_send(slot, side, first, count):
        part = pl.ds(first, count)
        return send(
            gtl.at[1 - mine, side, part], rx.at[side, part],
            g_send.at[0], g_recv.at[slot], at_core,
        )

    def y_send(slot, first, count):
        for i in range(count):
            ysend[first + i] = (gtl[mine, 1 - yc, first + i] + rx[1 - yc, first + i]).astype(BF16)
        part = pl.ds(first, count)
        return send(ysend.at[part], ry.at[part], g_send.at[1], g_recv.at[slot], at_y)

    share = n_tm // 4
    first_owner = n_tm // 2 - 2
    owns = jnp.logical_and(tm >= first_owner, tm < first_owner + 4)

    def scatter_copy(unit):
        place_in = lax.rem(unit, share)
        return pltpu.make_async_remote_copy(
            src_ref=pb.at[unit], dst_ref=rs.at[tm, place_in],
            send_sem=a_send.at[0], recv_sem=a_recv.at[0],
            device_id=(first_owner + unit // share, c), device_id_type=MESH,
        )

    def gather_copy(owner, to):
        part = ag.at[pl.ds(owner * share, share)]
        return pltpu.make_async_remote_copy(
            src_ref=part, dst_ref=part,
            send_sem=a_send.at[1], recv_sem=a_recv.at[1],
            device_id=(to, c), device_id_type=MESH,
        )

    def scatter(first, count):
        for i in range(count):
            to = first + i
            part = gtl[mine, yc, to] + rx[yc, to] + ry[to].astype(F32)
            psum[to] = part
            pb[to] = part.astype(BF16)

            @pl.when(tm != first_owner + to // share)
            def _():
                scatter_copy(to).start()

    def pass_hidden(q):
        hid_near[q].wait_recv()
        far_start(1, hhalo, q)

    @pl.when(parity == 0)
    def _():
        cote[:, 0:chans] = unpack(chalo, 1)

    @pl.when(parity == 1)
    def _():
        cote[:, chans - skip : 2 * chans - skip] = unpack(chalo, 0)

    place(outer_dot(hb[...], cote[...]), early, n_early)
    core_e = [core_send(e, side, early, n_early) for e, side in enumerate((1 - yc, yc))]
    core_e[0].wait_recv()
    y_e = y_send(4, early, n_early)

    far_recv(0)
    cotl[:, 0:chans] = unpack(chalo, parity)
    place(outer_dot(hb[...], cotl[...]), late, n_late)
    core_l = [core_send(2 + e, side, late, n_late) for e, side in enumerate((1 - yc, yc))]

    y_tail.wait_recv()
    wsend(11, tail_part(ypart), at_core)
    y_last.wait_recv()
    wsend(11, wp.at[ypart, 5], at_core)
    core_l[0].wait_recv()
    y_l = y_send(5, late, n_late)
    pass_hidden(0)

    received(block_rows(3 * depth - head_rows), w_recv.at[11])
    for owner in range(n_clip):
        unpack_pair(owner, 4, (1,))
        unpack_pair(owner, 5)
    grad_h = transpose_dot(unpack(chalo, 1), wg[9])
    grad_h = grad_h + transpose_dot(cot[...].astype(BF16), wg[10])
    grad_h = grad_h + transpose_dot(unpack(chalo, 0), wg[11])
    acc = spat[...]
    sig = jax.nn.sigmoid(acc)
    grad_s = grad_h * (sig * (1.0 + acc * (1.0 - sig)))
    for b in range(3):
        gpad[b, width : width + rows] = shifted(grad_s, b - 1).astype(BF16)

    for r in range(2, rounds):
        gate_step(r)
    core_e[1].wait_recv()
    y_e.wait_recv()
    scatter(early, n_early)

    def grad_conv(q):
        acc = cot[q * half : (q + 1) * half]
        for a in range(3):
            start = (2 - a) * width + q * half
            for b in range(3):
                acc = acc + transpose_dot(gpad[b, start : start + half], wg[3 * a + b])
        gv_v[q * half : (q + 1) * half] = acc

    core_l[1].wait_recv()
    y_l.wait_recv()
    scatter(late, n_late)
    grad_conv(0)
    pass_hidden(1)
    grad_conv(1)
    forward(1, hstash, hhalo)
    out_v[...] = video[...] + nn_dot(hb[...], wg[10])

    @pl.when(owns)
    def _():
        mine_at = tm - first_owner
        rs[tm] = jnp.zeros(rs.shape[1:], BF16)
        received(rs.at[pl.ds(0, n_tm - 1)], a_recv.at[0])
        for e in range(share):
            total = psum[mine_at * share + e]
            for sender in range(n_tm):
                total = total + rs[sender, e].astype(F32)
            ag[mine_at * share + e] = total.astype(BF16)
        for to in (0, 1, n_tm - 2, n_tm - 1, *range(2, n_tm - 2)):
            @pl.when(tm != to)
            def _():
                gather_copy(mine_at, to).start()

    received(block_rows(2 * chunk), halo_recv.at[5])
    out_v[...] = out_v[...] + nn_dot(unpack(hhalo, 1 - parity), wg[11 - 2 * parity])
    far_recv(1)
    out_v[...] = out_v[...] + nn_dot(unpack(hhalo, parity), wg[9 + 2 * parity])

    @pl.when(owns)
    def _():
        received(ag.at[pl.ds(0, 3 * share)], a_recv.at[1])

    @pl.when(jnp.logical_not(owns))
    def _():
        received(ag, a_recv.at[1])

    whole = jnp.concatenate([ag[to] for to in range(n_tm)], axis=1).astype(F32) * scale
    for k in range(3):
        gt_v[k] = whole[:, k * chans : (k + 1) * chans]

    sent(wp.at[pl.ds(0, 3)], w_send.at[0])
    sent(block_rows(half), halo_send.at[0])
    sent(block_rows(half), halo_send.at[1])
    sent(gtl.at[0], g_send.at[0])
    sent(ysend, g_send.at[1])

    @pl.when(sends_far)
    def _():
        sent(chalo, halo_send.at[2])

    @pl.when(gets_far)
    def _():
        sent(block_rows(half), halo_send.at[3])

    @pl.when(owns)
    def _():
        sent(pb.at[pl.ds(0, n_tm - share)], a_send.at[0])
        sent(rs.at[pl.ds(0, n_tm - 1)], a_send.at[1])

    @pl.when(jnp.logical_not(owns))
    def _():
        sent(pb, a_send.at[0])


def hand_over(*refs):
    n = len(refs) // 2
    ins, outs, sem = refs[:n], refs[n : 2 * n], refs[2 * n]
    writes = []
    for e in range(n):
        writes.append(pltpu.make_async_copy(ins[e], outs[e], sem.at[e]))
    for write in writes:
        write.start()
    for write in writes:
        write.wait()


def fused(n_tm, n_clip, video, spatial_w, spatial_b, temporal_w, cotangent):
    clips, frames, height, width, chans = video.shape
    rows = height * width
    depth = spatial_w.shape[1]
    lanes = -(-3 * chans // (128 * n_tm)) * 128
    scale = 1.0 / math.sqrt(rows * n_tm * n_clip)
    any_spec = pl.BlockSpec(memory_space=pltpu.HBM)
    vm_spec = pl.BlockSpec(memory_space=pltpu.VMEM)
    vm = pltpu.VMEM
    dma = pltpu.SemaphoreType.DMA
    results = pl.pallas_call(
        functools.partial(block_kernel, (n_tm, n_clip, height, width, chans, scale)),
        out_shape=(
            vm((rows, chans), F32),
            vm((rows, chans), F32),
            vm((3, depth, chans), F32),
        ),
        in_specs=[any_spec, any_spec, any_spec, any_spec, any_spec],
        out_specs=(vm_spec, vm_spec, vm_spec),
        scratch_shapes=[
            vm((rows, chans), F32),
            vm((rows, chans), F32),
            vm((9, depth, chans), BF16),
            vm((3, depth, chans), F32),
            vm((chans,), F32),
            vm((n_clip, 6, depth, 2 * chans), BF16),
            vm((12, chans, chans), BF16),
            vm((2, rows + 2 * width, 3 * chans // 2), BF16),
            vm((rows // 2, 2 * chans), BF16),
            vm((2, rows // 2, 2 * chans), BF16),
            vm((rows, 2 * chans), BF16),
            vm((rows, n_tm * lanes - 2 * chans), BF16),
            vm((rows, chans), BF16),
            vm((rows // 2, 2 * chans), BF16),
            vm((rows // 2, 2 * chans), BF16),
            vm((2, rows // 2, 2 * chans), BF16),
            vm((rows // 2, 2 * chans), BF16),
            vm((rows, chans), F32),
            vm((3, rows + 2 * width, chans), BF16),
            vm((2, 2, n_tm, depth, lanes), F32),
            vm((2, n_tm, depth, lanes), F32),
            vm((n_tm, depth, lanes), BF16),
            vm((n_tm, depth, lanes), BF16),
            vm((n_tm, depth, lanes), F32),
            vm((n_tm, depth, lanes), BF16),
            vm((n_tm, n_tm // 4, depth, lanes), BF16),
            vm((n_tm, depth, lanes), BF16),
            dma((6,)),
            dma((1,)),
            dma((13,)),
            dma((4,)),
            dma((10,)),
            dma((2,)),
            dma((6,)),
            dma((2,)),
            dma((2,)),
            pltpu.SemaphoreType.REGULAR((n_tm // 2 - 1,)),
        ],
        compiler_params=pltpu.CompilerParams(
            collective_id=0, has_side_effects=True, vmem_limit_bytes=65_000_000
        ),
        name="block",
    )(
        video.reshape(rows, chans), spatial_w, spatial_b, temporal_w,
        cotangent.reshape(rows, chans),
    )
    shapes = tuple(jax.ShapeDtypeStruct(array.shape, F32) for array in results)

    out, gv, gt = pl.pallas_call(
        hand_over,
        out_shape=shapes,
        in_specs=[vm_spec] * 3,
        out_specs=(any_spec,) * 3,
        scratch_shapes=[dma((3,))],
        compiler_params=pltpu.CompilerParams(vmem_limit_bytes=2**20),
        name="hand_over",
    )(*results)
    return out.reshape(video.shape), gv.reshape(video.shape), gt


def padded_2(cells, sides, width):
    for axis, dim in sides:
        count = lax.axis_size(axis)
        ends = count - 1
        head = lax.slice_in_dim(cells, 0, width, axis=dim)
        tail = lax.slice_in_dim(cells, cells.shape[dim] - width, cells.shape[dim], axis=dim)
        cells = jnp.concatenate(
            [
                lax.ppermute(tail, axis, [(i, (i + 1) % count) for i in range(ends)]),
                cells,
                lax.ppermute(head, axis, [((i + 1) % count, i) for i in range(ends)]),
            ],
            axis=dim,
        )
    return cells


def native(video, spatial_w, spatial_b, temporal_w, cotangent):
    clips, frames, height, width, chans = video.shape
    row_count = clips * frames * height * width
    pads = ((0, 0), (0, 0), (1, 1), (1, 1), (0, 0))
    padded = jnp.pad(video.astype(BF16), pads)
    temporal_b = temporal_w.astype(BF16)
    spatial_all = lax.all_gather(spatial_w, "clip", axis=1, tiled=True)
    temporal_all = lax.all_gather(temporal_b, "clip", axis=1, tiled=True)
    spatial = jnp.zeros((row_count, chans), F32)
    for y in range(3):
        for x in range(3):
            window = padded[:, :, y : y + height, x : x + width, :].reshape(row_count, chans)
            spatial = spatial + nn_dot(window, spatial_all[3 * y + x])
    spatial = spatial + spatial_b
    sigmoid_s = jax.nn.sigmoid(spatial)
    hidden = (spatial * sigmoid_s).astype(BF16).reshape(video.shape)
    hidden_pad = padded_2(hidden, (("tm", 1),), 1)
    cot_b = cotangent.astype(BF16)
    cot_flat = cot_b.reshape(row_count, chans)
    cot_pad = padded_2(cot_b, (("tm", 1),), 1)
    temporal = jnp.zeros((row_count, chans), F32)
    grad_hidden = jnp.zeros((row_count, chans), F32)
    grads = []
    for k in range(3):
        shifted_hid = hidden_pad[:, k : k + frames].reshape(row_count, chans)
        temporal = temporal + nn_dot(shifted_hid, temporal_all[k])
        shifted_cot = cot_pad[:, 2 - k : 2 - k + frames].reshape(row_count, chans)
        grad_hidden = grad_hidden + transpose_dot(shifted_cot, temporal_all[k])
        grads.append(outer_dot(shifted_hid, cot_flat))
    total_rows = row_count * lax.axis_size("tm") * lax.axis_size("clip")
    summed = lax.psum(jnp.stack(grads), "tm")
    owned = lax.psum_scatter(summed, "clip", scatter_dimension=1, tiled=True)
    grad_spatial = (grad_hidden * sigmoid_s * (1.0 + spatial * (1.0 - sigmoid_s))).astype(BF16)
    grad_frames = jnp.pad(grad_spatial.reshape(video.shape), pads)
    grad_acc = cotangent.reshape(row_count, chans)
    for y in range(3):
        for x in range(3):
            window = grad_frames[:, :, 2 - y : 2 - y + height, 2 - x : 2 - x + width, :]
            window = window.reshape(row_count, chans)
            grad_acc = grad_acc + transpose_dot(window, spatial_all[3 * y + x])
    return (
        video + temporal.reshape(video.shape),
        grad_acc.reshape(video.shape),
        owned * (1.0 / math.sqrt(total_rows)),
    )


def solution(mesh):
    n_tm, n_clip = mesh.shape["tm"], mesh.shape["clip"]

    def on_device(video, spatial_w, spatial_b, temporal_w, cotangent):
        args = (video, spatial_w, spatial_b, temporal_w, cotangent)
        one_frame = video.shape[0] == 1 and video.shape[1] == 1
        depth, chans = spatial_w.shape[1:]
        lanes = -(-3 * chans // (128 * n_tm)) * 128
        whole_rows = depth * (-(-chans // 128) * 128) % (2 * chans) == 0
        fits = depth % 16 == 0 and depth > 16 * TAIL and 2 * chans % lanes == 0
        if one_frame and fits and n_clip == 4 and n_tm % 4 == 0 and n_tm * lanes <= 4 * chans and whole_rows:
            return fused(n_tm, n_clip, *args)
        return native(*args)

    return jax.shard_map(
        on_device,
        mesh=mesh,
        in_specs=(
            P("clip", "tm", None, None, None),
            P(None, "clip", None),
            P(),
            P(None, "clip", None),
            P("clip", "tm", None, None, None),
        ),
        out_specs=(
            P("clip", "tm", None, None, None),
            P("clip", "tm", None, None, None),
            P(None, "clip", None),
        ),
        check_vma=False,
    )
```
